32 devices in a mesh: dp: 16 (over z, x, core), blk: 2 (over y).
Axes of the slice: x: 2, y: 2, z: 4, core: 2. Of those that a mesh axis runs over, the one named last changes fastest.
Arguments:
- hidden_in: bfloat16 [32, 1024, 768], P('dp', 'blk'), may hold values from -6 to 6
- cell_lengths: int32 [32], P('dp'), may hold values from 1 to 1024, as said below
- cotangent: bfloat16 [32, 1024, 768], P('dp', 'blk'), may hold values from -6 to 6
- ln_gains: float32 [2, 2, 768], replicated, may hold values from 0.5 to 1.5
- ln_biases: float32 [2, 2, 768], replicated, may hold values from -1.75 to 1.75
- w_qkv: bfloat16 [2, 768, 2304], replicated, may hold values from -0.21875 to 0.21875
- b_query: float32 [2, 768], replicated, may hold values from -3 to 3
- b_value: float32 [2, 768], replicated, may hold values from -1.75 to 1.75
- w_out: bfloat16 [2, 768, 768], replicated, may hold values from -1.75 to 1.75
- b_out: float32 [2, 768], replicated, may hold values from -1.75 to 1.75
- w_up: bfloat16 [2, 768, 3072], replicated, may hold values from -0.21875 to 0.21875
- b_up: float32 [2, 3072], replicated, may hold values from -3 to 3
- w_down: bfloat16 [2, 3072, 768], replicated, may hold values from -0.109375 to 0.109375
- b_down: float32 [2, 768], replicated, may hold values from -1.75 to 1.75
Outputs:
- hidden_out: bfloat16 [32, 1024, 768], P('dp', 'blk')
- grad_in: float32 [32, 1024, 768], P('dp', 'blk')
- grad_ln_gains: float32 [2, 2, 768], P(None, None, ('dp', 'blk'))
- grad_ln_biases: float32 [2, 2, 768], P(None, None, ('dp', 'blk'))
- grad_w_qkv: float32 [2, 768, 2304], P(None, None, ('dp', 'blk'))
- grad_b_query: float32 [2, 768], P(None, ('dp', 'blk'))
- grad_b_value: float32 [2, 768], P(None, ('dp', 'blk'))
- grad_w_out: float32 [2, 768, 768], P(None, None, ('dp', 'blk'))
- grad_b_out: float32 [2, 768], P(None, ('dp', 'blk'))
- grad_w_up: float32 [2, 768, 3072], P(None, None, ('dp', 'blk'))
- grad_b_up: float32 [2, 3072], P(None, ('dp', 'blk'))
- grad_w_down: float32 [2, 3072, 768], P(None, None, ('dp', 'blk'))
- grad_b_down: float32 [2, 768], P(None, ('dp', 'blk'))
The draws below stay inside these ranges and needn't reach their ends.
Inputs may be any that keep to these rules, and one draw needn't show every extreme that they name: `cell_lengths`: among the 2 cells of each index of dp one has more than 512 genes, and some cell has 1024.
All inputs are finite; a program needn't handle non-finite values.
Results may differ from the reference program's by a relative error of at most 0.01.
Values may be sent and summed in bfloat16 or wider, within the bound.
No kernel may reach another device: no remote copies, remote signals or barrier semaphores. Data moves between devices by JAX's collectives and lax.ppermute only.
A program may use at most 384 MiB of HBM per device.

```python
import math
import jax
import jax.numpy as jnp
from jax import lax

D = 768
HEADS = 12
HEAD_DIM = 64
FF = 3072
LAYERS = 2
SLOTS = 1024
CELLS_DEV = 2
SHARD = 512
CELLS = 32


def draw_cell_lengths(key, part):
    subkeys = jax.random.split(key, 4)
    baseline = jax.random.randint(subkeys[0], (CELLS,), 1, SLOTS + 1)
    group_count = CELLS // CELLS_DEV
    chosen_slot = jax.random.randint(subkeys[1], (group_count,), 0, CELLS_DEV)
    longest = jax.random.randint(subkeys[2], (group_count,), SLOTS - SHARD + 1, SLOTS + 1)
    position = jnp.arange(CELLS)
    owner_group = position // CELLS_DEV
    chosen = position % CELLS_DEV == chosen_slot[owner_group]
    lengths = jnp.where(chosen, longest[owner_group], baseline)
    fullest = jax.random.randint(subkeys[3], (), 0, CELLS)
    return jnp.where(position == fullest, SLOTS, lengths).astype(jnp.int32)


def with_spikes(values, key, source, target, shards_of, factor):
    def block_of(dim):
        return (jnp.arange(values.shape[dim]) // (values.shape[dim] // shards_of)).reshape((-1,) + (1,) * (values.ndim - 1 - dim))

    first = jax.random.permutation(key, shards_of)[block_of(target)]
    far = (block_of(target) + shards_of // 2) % shards_of
    return jnp.where((block_of(source) == first) | (block_of(source) == far), factor * values, values)


def level_of(rng, shape, cuts, smallest, top_value):
    level, own = 1.0, jax.random.fold_in(rng, 6)
    for dim, parts in cuts:
        draws = jnp.exp(jax.random.uniform(jax.random.fold_in(own, dim), (parts,), jnp.float32, smallest / len(cuts), top_value / len(cuts)))
        level = level * jnp.repeat(draws, shape[dim] // parts).reshape([-1 if axis == dim else 1 for axis in range(len(shape))])
    return level


def gaussian(key, dims, width, reach, shards=(), dtype=jnp.bfloat16):
    entries = width * jax.random.normal(key, dims, jnp.float32)
    if shards:
        entries = entries * level_of(key, dims, shards, -0.22, 0.18)
    return jnp.clip(entries, -reach, reach).astype(dtype)


def noise_with(rng, extent, deviation, limit, shards, heavy, kind=jnp.bfloat16):
    values = deviation * jax.random.normal(rng, extent, jnp.float32)
    if shards:
        values = values * level_of(rng, extent, shards, -0.22, 0.18)
    return jnp.clip(with_spikes(values, jax.random.fold_in(rng, 3), *heavy), -limit, limit).astype(kind)


def setup_inputs(seed: int = 0) -> dict:
    splits = jax.random.split(jax.random.key(seed), 15)
    hidden_in = gaussian(splits[0], (CELLS, SLOTS, D), 1.0, 6.0, ((0, 16), (1, 2)))
    cell_lengths = draw_cell_lengths(jax.random.fold_in(splits[14], 71), 0)
    cotangent = noise_with(splits[2], (CELLS, SLOTS, D), 1.0, 6.0, ((0, 16), (1, 2)), (0, 2, 16, 2.0))
    ln_gains = jnp.clip(1.0 + 0.1 * jax.random.normal(splits[3], (LAYERS, 2, D), jnp.float32), 0.5, 1.5)
    ln_biases = gaussian(splits[4], (LAYERS, 2, D), 0.3, 1.75, (), jnp.float32)
    w_qkv = gaussian(splits[5], (LAYERS, D, 3 * D), D ** -0.5, 0.21875)
    b_query = gaussian(splits[6], (LAYERS, D), 0.5, 3.0, (), jnp.float32)
    b_value = gaussian(splits[7], (LAYERS, D), 0.3, 1.75, (), jnp.float32)
    w_out = gaussian(splits[8], (LAYERS, D, D), (D // 64) ** -0.5, 1.75)
    b_out = gaussian(splits[9], (LAYERS, D), 0.3, 1.75, (), jnp.float32)
    w_up = gaussian(splits[10], (LAYERS, D, FF), D ** -0.5, 0.21875)
    b_up = gaussian(splits[11], (LAYERS, FF), 0.5, 3.0, (), jnp.float32)
    w_down = gaussian(splits[12], (LAYERS, FF, D), FF ** -0.5, 0.109375)
    b_down = gaussian(splits[13], (LAYERS, D), 0.3, 1.75, (), jnp.float32)
    return {"hidden_in": hidden_in, "cell_lengths": cell_lengths, "cotangent": cotangent, "ln_gains": ln_gains, "ln_biases": ln_biases, "w_qkv": w_qkv, "b_query": b_query, "b_value": b_value, "w_out": w_out, "b_out": b_out, "w_up": w_up, "b_up": b_up, "w_down": w_down, "b_down": b_down}


EPSILON = 1e-05
HIGH = lax.Precision.HIGHEST

@jax.custom_vjp
def low(v):
    return lax.optimization_barrier(v.astype(jnp.bfloat16)).astype(jnp.float32)

@jax.custom_vjp
def low_back(v):
    return v

def low_keep(v):
    return (low(v), None)

def low_pass(kept, grad):
    return (grad,)

def back_keep(v):
    return (v, None)

def back_low(kept, grad):
    return (low(grad),)
low.defvjp(low_keep, low_pass)
low_back.defvjp(back_keep, back_low)

def layer_norm(values, gain_vec, shift_vec):
    row_mean = lax.optimization_barrier(jnp.mean(values, -1, keepdims=True))
    centered = values - row_mean
    variance = lax.optimization_barrier(jnp.mean(centered * centered, -1, keepdims=True))
    return centered * lax.rsqrt(variance + EPSILON) * gain_vec + shift_vec

def attend_cell(cell_items):
    queries, key_rows, values, length = cell_items
    raw_scores = jnp.einsum('qhd,khd->hqk', queries, key_rows, precision=HIGH) * (1.0 / math.sqrt(HEAD_DIM))
    scores = low_back(raw_scores)
    valid_keys = jnp.arange(SLOTS) < length
    scores = jnp.where(valid_keys[None, None, :], scores, -jnp.inf)
    row_max = lax.optimization_barrier(jnp.max(scores, -1, keepdims=True))
    exponent = jnp.exp(scores - row_max)
    attention = low(exponent / lax.optimization_barrier(jnp.sum(exponent, -1, keepdims=True)))
    return jnp.einsum('hqk,khd->qhd', attention, values, precision=HIGH)

def encoder_block(carried, params, cell_lengths):
    gains, shifts, wqkv, bquery, bvalue, wout, bout, wup, bup, wdown, bdown = params
    flat = carried.reshape(-1, D)
    normed = low(layer_norm(flat, gains[0], shifts[0]))
    bias_all = jnp.concatenate([bquery, jnp.zeros_like(bquery), bvalue])
    projected = low(low_back(jnp.dot(normed, wqkv, precision=HIGH) + bias_all))
    split_heads = projected.reshape(CELLS, SLOTS, 3, HEADS, HEAD_DIM)
    mixed_heads = lax.map(jax.checkpoint(attend_cell), (split_heads[:, :, 0], split_heads[:, :, 1], split_heads[:, :, 2], cell_lengths))
    mixed_heads = low(low_back(mixed_heads.reshape(-1, D)))
    residual = flat + low_back(jnp.dot(mixed_heads, wout, precision=HIGH) + bout)
    normed2 = low(layer_norm(residual, gains[1], shifts[1]))
    upper_pre = low_back(jnp.dot(normed2, wup, precision=HIGH) + bup)
    active = low(jax.nn.gelu(upper_pre, approximate=False))
    branch_out = low_back(jnp.dot(active, wdown, precision=HIGH) + bdown)
    return (residual + branch_out).reshape(carried.shape)

def reference(hidden_in, cell_lengths, cotangent, ln_gains, ln_biases, w_qkv, b_query, b_value, w_out, b_out, w_up, b_up, w_down, b_down):
    weights = tuple((array.astype(jnp.float32) for array in (ln_gains, ln_biases, w_qkv, b_query, b_value, w_out, b_out, w_up, b_up, w_down, b_down)))

    def forward(carried, *params):
        for depth_index in range(LAYERS):
            carried = encoder_block(carried, tuple((param[depth_index] for param in params)), cell_lengths)
        return carried
    result, pullback = jax.vjp(forward, hidden_in.astype(jnp.float32), *weights)
    grads = pullback(cotangent.astype(jnp.float32))
    return (result.astype(jnp.bfloat16), grads[0], grads[1], grads[2], grads[3], grads[4], grads[5], grads[6], grads[7], grads[8], grads[9], grads[10], grads[11])
```

```python
import functools
import math

import jax
import jax.numpy as jnp
from jax import lax
from jax.experimental import pallas as pl
from jax.experimental.pallas import tpu as pltpu
from jax.sharding import PartitionSpec as P

HEAD_DIM = 64
LAYERS = 2
EPSILON = 1e-05
NEG = -1e30
BF = jnp.bfloat16
F32 = jnp.float32
QSCALE = math.log2(math.e) / math.sqrt(HEAD_DIM)


def dot_nn(a, b):
    return lax.dot_general(a, b, (((1,), (0,)), ((), ())), preferred_element_type=F32)


def dot_nt(a, b):
    return lax.dot_general(a, b, (((1,), (1,)), ((), ())), preferred_element_type=F32)


def dot_tn(a, b):
    return lax.dot_general(a, b, (((0,), (0,)), ((), ())), preferred_element_type=F32)


def mask_block(meta_ref, kaug, qone, tokens):
    rows = lax.broadcasted_iota(jnp.int32, (tokens, 128), 0)
    lanes = lax.broadcasted_iota(jnp.int32, (tokens, 128), 1)
    half = tokens // 2
    position = jnp.where(rows < half, rows + meta_ref[1], rows - meta_ref[1])
    masked = jnp.logical_and(lanes == 0, position >= meta_ref[0])
    kaug[...] = jnp.where(masked, NEG, 0.0).astype(BF)
    qone[...] = jnp.where(lanes == 0, 1.0, 0.0).astype(BF)


def attn_fwd_kernel(
    chunk, ahead, meta_ref, q_ref, k_ref, v_ref, o_ref, low_ref, lse_ref, kaug, qone
):
    tokens = q_ref.shape[0]

    @pl.when(pl.program_id(0) == 0)
    def _():
        mask_block(meta_ref, kaug, qone, tokens)

    first = lax.broadcasted_iota(jnp.int32, (tokens, 128), 1) < HEAD_DIM
    q, k, v = q_ref[...], k_ref[...], v_ref[...]
    zero = jnp.zeros_like(k)
    sel = [first, jnp.logical_not(first)]
    keys = [jnp.concatenate([jnp.where(sel[h], k, zero), kaug[...]], 1) for h in range(2)]
    vals = [jnp.where(sel[h], v, zero).T for h in range(2)]
    qa = jnp.concatenate([q, qone[...]], 1)
    units = [(c, h) for c in range(tokens // chunk) for h in range(2)]
    ready = {}

    def scores(unit):
        c, h = unit
        ready[unit] = dot_nt(keys[h], qa[c * chunk : (c + 1) * chunk])

    for unit in units[:ahead]:
        scores(unit)
    kept = {}
    for n, unit in enumerate(units):
        if n + ahead < len(units):
            scores(units[n + ahead])
        c, h = unit
        cols = slice(c * chunk, (c + 1) * chunk)
        st = ready.pop(unit)
        top = jnp.max(st, axis=0, keepdims=True)
        p = jnp.exp2(st - top)
        p = p.astype(BF)
        total = jnp.sum(p.astype(F32), axis=0, keepdims=True)
        kept[h] = (dot_nn(vals[h], p), top, total)
        if h == 1:
            head = lax.broadcasted_iota(jnp.int32, (128, chunk), 0) < HEAD_DIM
            inv = jnp.where(head, 1.0 / kept[0][2], 1.0 / kept[1][2])
            out = ((kept[0][0] + kept[1][0]) * inv).T
            high = out.astype(BF)
            o_ref[cols, :] = high
            low_ref[cols, :] = (out - high.astype(F32)).astype(BF)
            for g in range(2):
                lse_ref[0, g : g + 1, cols] = kept[g][1] + jnp.log2(kept[g][2])


def attn_fwd(proj, meta):
    tokens, width = proj.shape[0], proj.shape[1] // 3
    pairs = width // 128
    spec = lambda off: pl.BlockSpec((tokens, 128), lambda i, m: (0, off + i))
    return pl.pallas_call(
        functools.partial(attn_fwd_kernel, tokens // 2, 2),
        grid_spec=pltpu.PrefetchScalarGridSpec(
            num_scalar_prefetch=1,
            grid=(pairs,),
            in_specs=[spec(0), spec(pairs), spec(2 * pairs)],
            out_specs=[spec(0), spec(0), pl.BlockSpec((1, 8, tokens), lambda i, m: (i, 0, 0))],
            scratch_shapes=[pltpu.VMEM((tokens, 128), BF), pltpu.VMEM((tokens, 128), BF)],
        ),
        out_shape=[
            jax.ShapeDtypeStruct((tokens, width), BF),
            jax.ShapeDtypeStruct((tokens, width), BF),
            jax.ShapeDtypeStruct((pairs, 8, tokens), F32),
        ],
        compiler_params=pltpu.CompilerParams(
            vmem_limit_bytes=56 << 20, dimension_semantics=("arbitrary",)
        ),
        cost_estimate=pl.CostEstimate(
            flops=4 * tokens * tokens * width * 3,
            bytes_accessed=tokens * width * 8,
            transcendentals=pairs * 2 * tokens * tokens,
        ),
        name="attn_fwd",
    )(meta, proj, proj, proj)


def attn_bwd_kernel(
    meta_ref, q_ref, k_ref, v_ref, o_ref, low_ref, do_ref, lse_ref, dq_ref, dk_ref, dv_ref, kaug, qone
):
    tokens = q_ref.shape[0]

    @pl.when(pl.program_id(0) == 0)
    def _():
        mask_block(meta_ref, kaug, qone, tokens)

    first = lax.broadcasted_iota(jnp.int32, (tokens, 128), 1) < HEAD_DIM
    q, k, v, do = q_ref[...], k_ref[...], v_ref[...], do_ref[...]
    zero = jnp.zeros_like(k)
    sel = [first, jnp.logical_not(first)]
    qa = jnp.concatenate([q, qone[...]], 1)
    prod = ((o_ref[...].astype(F32) + low_ref[...].astype(F32)) * do.astype(F32)).T
    dq = dk = dv = None
    for h in range(2):
        kh = jnp.where(sel[h], k, zero)
        delta = jnp.sum(prod[h * HEAD_DIM : (h + 1) * HEAD_DIM], 0, keepdims=True)
        st = dot_nt(jnp.concatenate([kh, kaug[...]], 1), qa)
        dpt = dot_nt(jnp.where(sel[h], v, zero), do)
        p = jnp.exp2(st - lse_ref[0, h : h + 1, :])
        ds = (p * (dpt - delta)).astype(BF)
        dvh = dot_nn(p.astype(BF), jnp.where(sel[h], do, zero))
        dkh = dot_nn(ds, jnp.where(sel[h], q, zero))
        dqh = dot_nn(kh.T, ds)
        dq, dk, dv = (dqh, dkh, dvh) if h == 0 else (dq + dqh, dk + dkh, dv + dvh)
    dq_ref[...] = (dq * (1.0 / math.sqrt(HEAD_DIM))).T.astype(BF)
    dk_ref[...] = (dk * math.log(2.0)).astype(BF)
    dv_ref[...] = dv.astype(BF)


def attn_bwd(proj, mixed, low, g_mixed, lse, meta):
    tokens, width = mixed.shape
    pairs = width // 128
    spec = lambda off: pl.BlockSpec((tokens, 128), lambda i, m: (0, off + i))
    return pl.pallas_call(
        attn_bwd_kernel,
        grid_spec=pltpu.PrefetchScalarGridSpec(
            num_scalar_prefetch=1,
            grid=(pairs,),
            in_specs=[spec(0), spec(pairs), spec(2 * pairs), spec(0), spec(0), spec(0)]
            + [pl.BlockSpec((1, 8, tokens), lambda i, m: (i, 0, 0))],
            out_specs=[spec(0)] * 3,
            scratch_shapes=[pltpu.VMEM((tokens, 128), BF), pltpu.VMEM((tokens, 128), BF)],
        ),
        out_shape=[jax.ShapeDtypeStruct((tokens, width), BF)] * 3,
        compiler_params=pltpu.CompilerParams(
            vmem_limit_bytes=56 << 20, dimension_semantics=("arbitrary",)
        ),
        cost_estimate=pl.CostEstimate(
            flops=10 * tokens * tokens * width * 2,
            bytes_accessed=tokens * width * 16,
            transcendentals=pairs * 2 * tokens * tokens,
        ),
        name="attn_bwd",
    )(meta, proj, proj, proj, mixed, low, g_mixed, lse)


VMEM = pltpu.CompilerParams(vmem_limit_bytes=58 << 20, dimension_semantics=("arbitrary",))


def whole(arr):
    return pl.BlockSpec(arr.shape, lambda *_: (0,) * arr.ndim, pipeline_mode=pl.Buffered(1))


def tile(rows, width, first=0):
    return pl.BlockSpec((rows, width), lambda i, *_: (first + i, 0))


def sds(rows, width, dtype):
    return jax.ShapeDtypeStruct((rows, width), dtype)


def cost(flops, nbytes, trans=0):
    return pl.CostEstimate(flops=int(flops), bytes_accessed=int(nbytes), transcendentals=int(trans))


def normalize(x):
    mean = jnp.mean(x, -1, keepdims=True)
    centered = x - mean
    variance = jnp.mean(centered * centered, -1, keepdims=True)
    rstd = lax.rsqrt(variance + EPSILON)
    return centered * rstd, rstd


def project(n1, wqkv_ref, bias_ref, proj_ref, width):
    for j, factor in enumerate((QSCALE, 1.0, 1.0)):
        cols = slice(j * width, (j + 1) * width)
        part = dot_nn(n1, wqkv_ref[:, cols]) + bias_ref[:, cols]
        proj_ref[:, cols] = (part * factor).astype(BF)


def enter_kernel(x_ref, gain_ref, shift_ref, wqkv_ref, bias_ref, *refs):
    n1_ref, proj_ref = refs[-2:]
    width = x_ref.shape[1]
    xhat, _ = normalize(x_ref[...].astype(F32))
    n1 = (xhat * gain_ref[...] + shift_ref[...]).astype(BF)
    n1_ref[...] = n1
    project(n1, wqkv_ref, bias_ref, proj_ref, width)


def enter(x, gain, shift, wqkv, bias, into, tokens, first):
    rows, width = x.shape
    block = 256
    at = first // block
    ops = [x, gain, shift, wqkv, bias]
    specs = [tile(block, width)] + [whole(a) for a in ops[1:]]
    alias = {}
    if into is not None:
        ops += list(into)
        specs += [pl.BlockSpec(memory_space=pl.ANY)] * 2
        alias = {5: 0, 6: 1}
    return pl.pallas_call(
        enter_kernel,
        grid=(rows // block,),
        in_specs=specs,
        out_specs=[tile(block, width, at), tile(block, 3 * width, at)],
        out_shape=[sds(tokens, width, BF), sds(tokens, 3 * width, BF)],
        input_output_aliases=alias,
        compiler_params=VMEM,
        cost_estimate=cost(6 * rows * width * width, rows * width * 10 + 6 * width * width),
        name="enter",
    )(*ops)


def post_kernel(last, parts, *refs):
    it = iter(refs)
    mixed_ref, x_ref = next(it), next(it)
    wout_ref, bout_ref, gain_ref, shift_ref = next(it), next(it), next(it), next(it)
    wup_ref, bup_ref, wdown_ref, bdown_ref = next(it), next(it), next(it), next(it)
    if not last:
        gain1_ref, shift1_ref, wqkv_ref, bias_ref = next(it), next(it), next(it), next(it)
    resid_ref, n2_ref, active_ref, slope_ref = next(it), next(it), next(it), next(it)
    width = x_ref.shape[1]
    resid = x_ref[...].astype(F32) + dot_nn(mixed_ref[...], wout_ref[...]) + bout_ref[...]
    resid_ref[...] = resid
    xhat, _ = normalize(resid)
    n2 = (xhat * gain_ref[...] + shift_ref[...]).astype(BF)
    n2_ref[...] = n2
    hidden = wup_ref.shape[1] // parts
    total = resid + bdown_ref[...]
    for j in range(parts):
        cols = slice(j * hidden, (j + 1) * hidden)
        upper = dot_nn(n2, wup_ref[:, cols]) + bup_ref[:, cols]
        cdf = 0.5 + 0.5 * lax.erf(upper * math.sqrt(0.5))
        dens = jnp.exp2(upper * upper * (-0.5 * math.log2(math.e))) * (1.0 / math.sqrt(2.0 * math.pi))
        active = (upper * cdf).astype(BF)
        active_ref[:, cols] = active
        slope_ref[:, cols] = (cdf + upper * dens).astype(BF)
        total = total + dot_nn(active, wdown_ref[cols, :])
    if last:
        next(it)[...] = total.astype(BF)
    else:
        x_out, n1_ref, proj_ref = next(it), next(it), next(it)
        x_out[...] = total
        xhat, _ = normalize(total)
        n1 = (xhat * gain1_ref[...] + shift1_ref[...]).astype(BF)
        n1_ref[...] = n1
        project(n1, wqkv_ref, bias_ref, proj_ref, width)


def post(mixed, x, weights, following):
    tokens, width = x.shape
    block = 256
    ff = weights[4].shape[1]
    last = following is None
    ops = [mixed, x] + list(weights) + ([] if last else list(following))
    outs = [(width, F32), (width, BF), (ff, BF), (ff, BF)]
    outs += [(width, BF)] if last else [(width, F32), (width, BF), (3 * width, BF)]
    flops = 2 * tokens * width * (width + 2 * ff + (0 if last else 3 * width))
    return pl.pallas_call(
        functools.partial(post_kernel, last, 4),
        grid=(tokens // block,),
        in_specs=[tile(block, width)] * 2 + [whole(a) for a in ops[2:]],
        out_specs=[tile(block, w) for w, _ in outs],
        out_shape=[sds(tokens, w, t) for w, t in outs],
        compiler_params=VMEM,
        cost_estimate=cost(flops, tokens * ff * 10, 2 * tokens * ff),
        name="post",
    )(*ops)


def norm_back(g_normed, xhat, rstd, gain):
    scaled = g_normed * gain
    mean1 = jnp.mean(scaled, -1, keepdims=True)
    mean2 = jnp.mean(scaled * xhat, -1, keepdims=True)
    return rstd * (scaled - mean1 - xhat * mean2)


def add_row(ref, row, start, value, fresh):
    cols = slice(start, start + value.shape[1])

    @pl.when(fresh)
    def _():
        ref[row : row + 1, cols] = value

    @pl.when(jnp.logical_not(fresh))
    def _():
        ref[row : row + 1, cols] += value


def colsum(x):
    return jnp.sum(x, 0, keepdims=True)


def ff_back_kernel(parts, gx_ref, slope_ref, resid_ref, wdown_ref, wup_ref, wout_ref, gain_ref, *outs):
    gy_ref, gu_ref, gres_ref, ga_ref, gmix_ref, vec_ref = outs
    fresh = pl.program_id(0) == 0
    width = gx_ref.shape[1]
    gx = gx_ref[...].astype(F32)
    gy = gx.astype(BF)
    gy_ref[...] = gy
    hidden = wup_ref.shape[1] // parts
    g_n2 = None
    for j in range(parts):
        cols = slice(j * hidden, (j + 1) * hidden)
        g_act = dot_nt(gy, wdown_ref[cols, :])
        gu = (g_act * slope_ref[:, cols].astype(F32)).astype(BF)
        gu_ref[:, cols] = gu
        add_row(vec_ref, 0, j * hidden, colsum(gu.astype(F32)), fresh)
        part = dot_nt(gu, wup_ref[:, cols])
        g_n2 = part if g_n2 is None else g_n2 + part
    xhat, rstd = normalize(resid_ref[...])
    g_resid = gx + norm_back(g_n2, xhat, rstd, gain_ref[...])
    gres_ref[...] = g_resid
    ga = g_resid.astype(BF)
    ga_ref[...] = ga
    gmix_ref[...] = dot_nt(ga, wout_ref[...]).astype(BF)
    add_row(vec_ref, 1, 0, colsum(g_n2 * xhat), fresh)
    add_row(vec_ref, 1, width, colsum(g_n2), fresh)
    add_row(vec_ref, 1, 2 * width, colsum(gy.astype(F32)), fresh)
    add_row(vec_ref, 1, 3 * width, colsum(ga.astype(F32)), fresh)


def ff_back(gx, slope, resid, wdown, wup, wout, gain):
    tokens, width = resid.shape
    ff = slope.shape[1]
    block = 256
    outs = [(width, BF), (ff, BF), (width, F32), (width, BF), (width, BF)]
    assert ff == 4 * width
    return pl.pallas_call(
        functools.partial(ff_back_kernel, 4),
        grid=(tokens // block,),
        in_specs=[tile(block, width), tile(block, ff), tile(block, width)]
        + [whole(a) for a in (wdown, wup, wout, gain)],
        out_specs=[tile(block, w) for w, _ in outs] + [pl.BlockSpec((8, ff), lambda i: (0, 0))],
        out_shape=[sds(tokens, w, t) for w, t in outs] + [sds(8, ff, F32)],
        compiler_params=VMEM,
        cost_estimate=cost(2 * tokens * width * (2 * ff + width), tokens * ff * 8),
        name="ff_back",
    )(gx, slope, resid, wdown, wup, wout, gain)


def qkv_back_kernel(dq_ref, dk_ref, dv_ref, wqkv_ref, x_ref, gres_ref, gain_ref, *refs):
    gx_ref, vec_ref = refs[-2:]
    fresh = pl.program_id(0) == 0
    width = x_ref.shape[1]
    grads = [dq_ref[...], dk_ref[...], dv_ref[...]]
    g_norm = dot_nt(jnp.concatenate(grads, 1), wqkv_ref[...])
    xhat, rstd = normalize(x_ref[...].astype(F32))
    gx = gres_ref[...] + norm_back(g_norm, xhat, rstd, gain_ref[...])
    gx_ref[...] = gx.astype(gx_ref.dtype)
    add_row(vec_ref, 0, 0, colsum(g_norm * xhat), fresh)
    add_row(vec_ref, 0, width, colsum(g_norm), fresh)
    add_row(vec_ref, 0, 2 * width, colsum(grads[0].astype(F32)), fresh)
    add_row(vec_ref, 0, 3 * width, colsum(grads[2].astype(F32)), fresh)


def qkv_back(grads, wqkv, x, x_first, g_resid, gain, first, rows, dtype):
    width = x.shape[1]
    block = 256
    at = first // block
    return pl.pallas_call(
        qkv_back_kernel,
        grid=(rows // block,),
        in_specs=[tile(block, width, at)] * 3
        + [whole(wqkv), tile(block, width, x_first // block), tile(block, width, at), whole(gain)],
        out_specs=[tile(block, width), pl.BlockSpec((8, 4 * width), lambda i: (0, 0))],
        out_shape=[sds(rows, width, dtype), sds(8, 4 * width, F32)],
        compiler_params=VMEM,
        cost_estimate=cost(6 * rows * width * width, rows * width * 20),
        name="qkv_back",
    )(*grads, wqkv, x, g_resid, gain)


def plain_grad(lefts, right):
    return jnp.concatenate([dot_tn(left, right) for left in lefts], 0).astype(BF)


def swap_halves(x):
    return lax.ppermute(x, "blk", [(0, 1), (1, 0)])


class Halving:
    def __init__(self, mesh):
        self.dp = mesh.shape["dp"]
        self.blk = mesh.shape["blk"]
        self.bits = self.dp.bit_length() - 1
        assert self.blk == 2 and 1 << self.bits == self.dp

    def stages(self, blk_first):
        dp_bits = list(range(self.bits))
        rest = ["blk", 1] if blk_first else [1, "blk"]
        return [0] + rest + dp_bits[2:]

    def split(self, rows):
        owners = self.dp * self.blk
        return rows.reshape((2,) * (self.bits + 1) + (rows.shape[0] // owners, rows.shape[1]))

    def run(self, rows, blk_first, wide=False):
        arr = self.split(rows)
        names = list(reversed(range(self.bits))) + ["blk"]
        order = self.stages(blk_first)
        for n, stage in enumerate(order):
            dim = names.index(stage)
            names.pop(dim)
            if stage == "blk":
                mine = lax.axis_index("blk")
                send = lambda x: lax.ppermute(x, "blk", [(0, 1), (1, 0)])
            else:
                mine = (lax.axis_index("dp") >> stage) & 1
                perm = [(i, i ^ (1 << stage)) for i in range(self.dp)]
                send = lambda x: lax.ppermute(x, "dp", perm)
            keep = lax.dynamic_index_in_dim(arr, mine, dim, keepdims=False)
            other = lax.dynamic_index_in_dim(arr, 1 - mine, dim, keepdims=False)
            arr = keep.astype(F32) + send(other).astype(F32)
            if not wide and n + 1 < len(order):
                arr = arr.astype(BF)
        return arr


def shards(
    mesh,
    hidden_in,
    cell_lengths,
    cotangent,
    ln_gains,
    ln_biases,
    w_qkv,
    b_query,
    b_value,
    w_out,
    b_out,
    w_up,
    b_up,
    w_down,
    b_down,
):
    cells, half, width = hidden_in.shape
    tokens = cells * half
    halving = Halving(mesh)
    assert cells == halving.blk
    owners = halving.dp * halving.blk
    side = lax.axis_index("blk")
    meta = jnp.stack([lax.dynamic_index_in_dim(cell_lengths, side, 0, False), side * half])
    meta = meta.astype(jnp.int32)

    def split_cell(both):
        own = lax.dynamic_index_in_dim(both, side, 0, False)
        other = lax.dynamic_index_in_dim(both, 1 - side, 0, False)
        return own, swap_halves(other)

    def return_cell(own, back):
        return jnp.where(side == 0, jnp.stack([own, back]), jnp.stack([back, own]))

    row = lambda v: v[None, :]
    biases = [
        row(jnp.concatenate([b_query[d], jnp.zeros_like(b_query[d]), b_value[d]]))
        for d in range(LAYERS)
    ]
    first = [(row(ln_gains[d, 0]), row(ln_biases[d, 0]), w_qkv[d], biases[d]) for d in range(LAYERS)]
    own, other = split_cell(hidden_in)
    entered = enter(own, *first[0], None, tokens, 0)
    n1, proj = enter(other, *first[0], entered, tokens, half)
    carried = jnp.concatenate([own, other], 0)
    saved = []
    for d in range(LAYERS):
        mixed, low, lse = attn_fwd(proj, meta)
        weights = (
            w_out[d],
            row(b_out[d]),
            row(ln_gains[d, 1]),
            row(ln_biases[d, 1]),
            w_up[d],
            row(b_up[d]),
            w_down[d],
            row(b_down[d]),
        )
        last = d + 1 == LAYERS
        outs = post(mixed, carried, weights, None if last else first[d + 1])
        saved.append((carried, n1, proj, mixed, low, lse) + tuple(outs[:4]))
        if not last:
            carried, n1, proj = outs[4:]
    out16 = outs[4]
    hidden_out = return_cell(out16[:half], swap_halves(out16[half:]))

    gx = jnp.concatenate(split_cell(cotangent), 0)
    sums = {}
    vectors = {}
    for d in reversed(range(LAYERS)):
        layer_in, n1, proj, mixed, low, lse, resid, n2, active, slope = saved[d]
        gy, gu, g_resid, ga, g_mixed, vec2 = ff_back(
            gx, slope, resid, w_down[d], w_up[d], w_out[d], row(ln_gains[d, 1])
        )
        sums["down", d] = halving.run(plain_grad([gy], active), False)
        sums["up", d] = halving.run(plain_grad([gu], n2), True)
        sums["out", d] = halving.run(plain_grad([ga], mixed), False)
        grads = attn_bwd(proj, mixed, low, g_mixed, lse, meta)
        sums["qkv", d] = halving.run(plain_grad(grads, n1), d == 0)
        gain1 = row(ln_gains[d, 0])
        if d > 0:
            gx, vec1 = qkv_back(grads, w_qkv[d], layer_in, 0, g_resid, gain1, 0, tokens, F32)
        else:
            theirs, vec_a = qkv_back(
                grads, w_qkv[d], layer_in, half, g_resid, gain1, half, half, BF
            )
            back = swap_halves(theirs)
            mine, vec_b = qkv_back(grads, w_qkv[d], layer_in, 0, g_resid, gain1, 0, half, F32)
            vec1 = vec_a + vec_b
        at = lambda v, r, n: v[r, n * width : (n + 1) * width]
        vectors[d] = [
            at(vec1, 0, 0),
            at(vec2, 1, 0),
            at(vec1, 0, 1),
            at(vec2, 1, 1),
            at(vec1, 0, 2),
            at(vec1, 0, 3),
            at(vec2, 1, 3),
            at(vec2, 1, 2),
            vec2[0],
        ]
    grad_in = return_cell(mine, back.astype(F32))

    flat = [v.reshape(owners, -1) for d in range(LAYERS) for v in vectors[d]]
    widths = [f.shape[1] for f in flat]
    flat = halving.run(jnp.concatenate(flat, 1), False, wide=True)[0]
    pieces = jnp.split(flat, [sum(widths[: i + 1]) for i in range(len(widths) - 1)])
    per = [pieces[:9], pieces[9:]]
    pick = lambda i: jnp.stack([per[0][i], per[1][i]])
    gains = jnp.stack([jnp.stack([per[d][0], per[d][1]]) for d in range(LAYERS)])
    shifts = jnp.stack([jnp.stack([per[d][2], per[d][3]]) for d in range(LAYERS)])
    mat = lambda name: jnp.stack([sums[name, d].T for d in range(LAYERS)])
    return (
        hidden_out,
        grad_in,
        gains,
        shifts,
        mat("qkv"),
        pick(4),
        pick(5),
        mat("out"),
        pick(6),
        mat("up"),
        pick(8),
        mat("down"),
        pick(7),
    )


def solution(mesh):
    both = ("dp", "blk")
    row = P("dp", "blk", None)
    last3 = P(None, None, both)
    last2 = P(None, both)
    return jax.shard_map(
        functools.partial(shards, mesh),
        mesh=mesh,
        in_specs=(row, P("dp"), row) + (P(),) * 11,
        out_specs=(
            row,
            row,
            last3,
            last3,
            last3,
            last2,
            last2,
            last3,
            last2,
            last3,
            last2,
            last3,
            last2,
        ),
        check_vma=False,
    )
```

```python
import functools
import math

import jax
import jax.numpy as jnp
from jax import lax
from jax.experimental import pallas as pl
from jax.experimental.pallas import tpu as pltpu
from jax.sharding import PartitionSpec as P

HEAD_DIM = 64
LAYERS = 2
EPSILON = 1e-05
NEG = -1e30
BF = jnp.bfloat16
F32 = jnp.float32
QSCALE = math.log2(math.e) / math.sqrt(HEAD_DIM)


def dot_nn(a, b):
    return lax.dot_general(a, b, (((1,), (0,)), ((), ())), preferred_element_type=F32)


def dot_nt(a, b):
    return lax.dot_general(a, b, (((1,), (1,)), ((), ())), preferred_element_type=F32)


def dot_tn(a, b):
    return lax.dot_general(a, b, (((0,), (0,)), ((), ())), preferred_element_type=F32)


def mask_block(meta_ref, kaug, qone, tokens):
    side = lax.axis_index("blk")
    rows = lax.broadcasted_iota(jnp.int32, (tokens, 128), 0)
    lanes = lax.broadcasted_iota(jnp.int32, (tokens, 128), 1)
    half = tokens // 2
    position = jnp.where(rows < half, rows + side * half, rows - side * half)
    masked = jnp.logical_and(lanes == 0, position >= meta_ref[side])
    kaug[...] = jnp.where(masked, NEG, 0.0).astype(BF)
    qone[...] = jnp.where(lanes == 0, 1.0, 0.0).astype(BF)


def attn_fwd_kernel(
    chunk, ahead, meta_ref, q_ref, k_ref, v_ref, o_ref, low_ref, lse_ref, kaug, qone
):
    tokens = q_ref.shape[0]

    @pl.when(pl.program_id(0) == 0)
    def _():
        mask_block(meta_ref, kaug, qone, tokens)

    first = lax.broadcasted_iota(jnp.int32, (tokens, 128), 1) < HEAD_DIM
    q, k, v = q_ref[...], k_ref[...], v_ref[...]
    zero = jnp.zeros_like(k)
    sel = [first, jnp.logical_not(first)]
    keys = [jnp.concatenate([jnp.where(sel[h], k, zero), kaug[...]], 1) for h in range(2)]
    vals = [jnp.where(sel[h], v, zero).T for h in range(2)]
    qa = jnp.concatenate([q, qone[...]], 1)
    units = [(c, h) for c in range(tokens // chunk) for h in range(2)]
    ready = {}

    def scores(unit):
        c, h = unit
        ready[unit] = dot_nt(keys[h], qa[c * chunk : (c + 1) * chunk])

    for unit in units[:ahead]:
        scores(unit)
    kept = {}
    for n, unit in enumerate(units):
        if n + ahead < len(units):
            scores(units[n + ahead])
        c, h = unit
        cols = slice(c * chunk, (c + 1) * chunk)
        st = ready.pop(unit)
        top = jnp.max(st, axis=0, keepdims=True)
        p = jnp.exp2(st - top)
        p = p.astype(BF)
        total = jnp.sum(p.astype(F32), axis=0, keepdims=True)
        kept[h] = (dot_nn(vals[h], p), top, total)
        if h == 1:
            head = lax.broadcasted_iota(jnp.int32, (128, chunk), 0) < HEAD_DIM
            inv = jnp.where(head, 1.0 / kept[0][2], 1.0 / kept[1][2])
            out = ((kept[0][0] + kept[1][0]) * inv).T
            high = out.astype(BF)
            o_ref[cols, :] = high
            low_ref[cols, :] = (out - high.astype(F32)).astype(BF)
            for g in range(2):
                lse_ref[0, g : g + 1, cols] = kept[g][1] + jnp.log2(kept[g][2])


def attn_fwd(proj, meta):
    tokens, width = proj.shape[0], proj.shape[1] // 3
    pairs = width // 128
    spec = lambda off: pl.BlockSpec((tokens, 128), lambda i, m: (0, off + i))
    return pl.pallas_call(
        functools.partial(attn_fwd_kernel, tokens // 2, 2),
        grid_spec=pltpu.PrefetchScalarGridSpec(
            num_scalar_prefetch=1,
            grid=(pairs,),
            in_specs=[spec(0), spec(pairs), spec(2 * pairs)],
            out_specs=[spec(0), spec(0), pl.BlockSpec((1, 8, tokens), lambda i, m: (i, 0, 0))],
            scratch_shapes=[pltpu.VMEM((tokens, 128), BF), pltpu.VMEM((tokens, 128), BF)],
        ),
        out_shape=[
            jax.ShapeDtypeStruct((tokens, width), BF),
            jax.ShapeDtypeStruct((tokens, width), BF),
            jax.ShapeDtypeStruct((pairs, 8, tokens), F32),
        ],
        compiler_params=pltpu.CompilerParams(
            vmem_limit_bytes=56 << 20, dimension_semantics=("arbitrary",)
        ),
        cost_estimate=pl.CostEstimate(
            flops=4 * tokens * tokens * width * 3,
            bytes_accessed=tokens * width * 8,
            transcendentals=pairs * 2 * tokens * tokens,
        ),
        name="attn_fwd",
    )(meta, proj, proj, proj)


def attn_bwd_kernel(
    meta_ref, q_ref, k_ref, v_ref, o_ref, low_ref, do_ref, lse_ref, out_ref, kaug, qone
):
    tokens = q_ref.shape[0]

    @pl.when(pl.program_id(0) == 0)
    def _():
        mask_block(meta_ref, kaug, qone, tokens)

    first = lax.broadcasted_iota(jnp.int32, (tokens, 128), 1) < HEAD_DIM
    q, k, v, do = q_ref[...], k_ref[...], v_ref[...], do_ref[...]
    zero = jnp.zeros_like(k)
    sel = [first, jnp.logical_not(first)]
    qa = jnp.concatenate([q, qone[...]], 1)
    prod = ((o_ref[...].astype(F32) + low_ref[...].astype(F32)) * do.astype(F32)).T
    dq = dk = dv = None
    for h in range(2):
        kh = jnp.where(sel[h], k, zero)
        delta = jnp.sum(prod[h * HEAD_DIM : (h + 1) * HEAD_DIM], 0, keepdims=True)
        st = dot_nt(jnp.concatenate([kh, kaug[...]], 1), qa)
        dpt = dot_nt(jnp.where(sel[h], v, zero), do)
        p = jnp.exp2(st - lse_ref[0, h : h + 1, :])
        ds = (p * (dpt - delta)).astype(BF)
        dvh = dot_nn(p.astype(BF), jnp.where(sel[h], do, zero))
        dkh = dot_nn(ds, jnp.where(sel[h], q, zero))
        dqh = dot_nn(kh.T, ds)
        dq, dk, dv = (dqh, dkh, dvh) if h == 0 else (dq + dqh, dk + dkh, dv + dvh)
    out_ref[0] = (dq * (1.0 / math.sqrt(HEAD_DIM))).T.astype(BF)
    out_ref[1] = (dk * math.log(2.0)).astype(BF)
    out_ref[2] = dv.astype(BF)


def attn_bwd(proj, mixed, low, g_mixed, lse, meta, pairs, into=None, deps=()):
    tokens, width = mixed.shape
    count = width // 128
    start, stop = pairs
    spec = lambda off: pl.BlockSpec((tokens, 128), lambda i, m: (0, off + start + i))
    ops = [meta, proj, proj, proj, mixed, low, g_mixed, lse]
    specs = [spec(0), spec(count), spec(2 * count), spec(0), spec(0), spec(0)]
    specs += [pl.BlockSpec((1, 8, tokens), lambda i, m: (start + i, 0, 0))]
    extra = ([] if into is None else [into]) + list(deps)
    return pl.pallas_call(
        ordered(attn_bwd_kernel, len(ops), extra),
        grid_spec=pltpu.PrefetchScalarGridSpec(
            num_scalar_prefetch=1,
            grid=(stop - start,),
            in_specs=specs + anywhere(extra),
            out_specs=pl.BlockSpec((3, tokens, 128), lambda i, m: (0, 0, start + i)),
            scratch_shapes=[pltpu.VMEM((tokens, 128), BF), pltpu.VMEM((tokens, 128), BF)],
        ),
        out_shape=jax.ShapeDtypeStruct((3, tokens, width), BF),
        input_output_aliases={} if into is None else {len(ops): 0},
        compiler_params=pltpu.CompilerParams(
            vmem_limit_bytes=56 << 20, dimension_semantics=("arbitrary",)
        ),
        cost_estimate=pl.CostEstimate(
            flops=20 * tokens * tokens * 128 * (stop - start),
            bytes_accessed=tokens * 128 * (stop - start) * 18,
            transcendentals=2 * (stop - start) * tokens * tokens,
        ),
        name="attn_bwd",
    )(*ops, *extra)


VMEM = pltpu.CompilerParams(vmem_limit_bytes=58 << 20, dimension_semantics=("arbitrary",))


def ordered(kernel, n_in, deps):
    if not deps:
        return kernel
    return lambda *refs: kernel(*refs[:n_in], *refs[n_in + len(deps) :])


def anywhere(arrays):
    return [pl.BlockSpec(memory_space=pl.ANY)] * len(arrays)


def layer(arr, d, n=0):
    lead = arr.ndim - 2
    index = (d, n)[:lead] + (0, 0)
    return pl.BlockSpec(
        (None,) * lead + arr.shape[lead:], lambda *_: index, pipeline_mode=pl.Buffered(1)
    )


def tile(rows, width, first=0):
    return pl.BlockSpec((rows, width), lambda i, *_: (first + i, 0))


def sds(rows, width, dtype):
    return jax.ShapeDtypeStruct((rows, width), dtype)


def cost(flops, nbytes, trans=0):
    return pl.CostEstimate(flops=int(flops), bytes_accessed=int(nbytes), transcendentals=int(trans))


def normalize(x):
    mean = jnp.mean(x, -1, keepdims=True)
    centered = x - mean
    variance = jnp.mean(centered * centered, -1, keepdims=True)
    rstd = lax.rsqrt(variance + EPSILON)
    return centered * rstd, rstd


def project(n1, wqkv_ref, bias_ref, proj_ref, width):
    for j, factor in enumerate((QSCALE, 1.0, 1.0)):
        cols = slice(j * width, (j + 1) * width)
        part = dot_nn(n1, wqkv_ref[:, cols]) + bias_ref[:, cols]
        proj_ref[:, cols] = (part * factor).astype(BF)


def attn_in(params, d):
    arrays = [params["gains"], params["shifts"], params["wqkv"], params["bias"]]
    return arrays, [layer(arrays[0], d, 0), layer(arrays[1], d, 0), layer(arrays[2], d), layer(arrays[3], d)]


def ff_in(params, d):
    names = ("wout", "bout", "gains", "shifts", "wup", "bup", "wdown", "bdown")
    arrays = [params[n] for n in names]
    return arrays, [layer(a, d, 1) for a in arrays]


def enter_kernel(x_ref, gain_ref, shift_ref, wqkv_ref, bias_ref, *refs):
    n1_ref, proj_ref = refs[-2:]
    width = x_ref.shape[1]
    xhat, _ = normalize(x_ref[...].astype(F32))
    n1 = (xhat * gain_ref[...] + shift_ref[...]).astype(BF)
    n1_ref[...] = n1
    project(n1, wqkv_ref, bias_ref, proj_ref, width)


def enter(x, params, d, into, tokens, first):
    rows, width = x.shape
    block = 256
    at = first // block
    arrays, specs = attn_in(params, d)
    ops = [x] + arrays
    specs = [tile(block, width)] + specs
    alias = {}
    if into is not None:
        ops += list(into)
        specs += [pl.BlockSpec(memory_space=pl.ANY)] * 2
        alias = {5: 0, 6: 1}
    return pl.pallas_call(
        enter_kernel,
        grid=(rows // block,),
        in_specs=specs,
        out_specs=[tile(block, width, at), tile(block, 3 * width, at)],
        out_shape=[sds(tokens, width, BF), sds(tokens, 3 * width, BF)],
        input_output_aliases=alias,
        compiler_params=VMEM,
        cost_estimate=cost(6 * rows * width * width, rows * width * 10 + 6 * width * width),
        name="enter",
    )(*ops)


def halves(tokens, block, width):
    turn = tokens // block // 2
    own = pl.BlockSpec((block, width), lambda i, *_: (jnp.minimum(i, turn - 1), 0))
    other = pl.BlockSpec((block, width), lambda i, *_: (jnp.maximum(i - turn, 0), 0))
    return [own, other]


def joined(refs):
    if len(refs) == 1:
        return refs[0][...].astype(F32)
    early = pl.program_id(0) < pl.num_programs(0) // 2
    return jnp.where(early, refs[0][...].astype(F32), refs[1][...].astype(F32))


def post_kernel(last, parts, n_x, *refs):
    it = iter(refs)
    mixed_ref = next(it)
    x_refs = [next(it) for _ in range(n_x)]
    wout_ref, bout_ref, gain_ref, shift_ref = next(it), next(it), next(it), next(it)
    wup_ref, bup_ref, wdown_ref, bdown_ref = next(it), next(it), next(it), next(it)
    if not last:
        gain1_ref, shift1_ref, wqkv_ref, bias_ref = next(it), next(it), next(it), next(it)
    resid_ref, n2_ref, active_ref, slope_ref = next(it), next(it), next(it), next(it)
    width = mixed_ref.shape[1]
    resid = joined(x_refs) + dot_nn(mixed_ref[...], wout_ref[...]) + bout_ref[...]
    resid_ref[...] = resid
    xhat, _ = normalize(resid)
    n2 = (xhat * gain_ref[...] + shift_ref[...]).astype(BF)
    n2_ref[...] = n2
    hidden = wup_ref.shape[1] // parts
    total = resid + bdown_ref[...]
    for j in range(parts):
        cols = slice(j * hidden, (j + 1) * hidden)
        upper = dot_nn(n2, wup_ref[:, cols]) + bup_ref[:, cols]
        cdf = 0.5 + 0.5 * lax.erf(upper * math.sqrt(0.5))
        dens = jnp.exp2(upper * upper * (-0.5 * math.log2(math.e))) * (1.0 / math.sqrt(2.0 * math.pi))
        active = (upper * cdf).astype(BF)
        active_ref[:, cols] = active
        slope_ref[:, cols] = (cdf + upper * dens).astype(BF)
        total = total + dot_nn(active, wdown_ref[cols, :])
    if last:
        next(it)[...] = total.astype(BF)
    else:
        x_out, n1_ref, proj_ref = next(it), next(it), next(it)
        x_out[...] = total
        xhat, _ = normalize(total)
        n1 = (xhat * gain1_ref[...] + shift1_ref[...]).astype(BF)
        n1_ref[...] = n1
        project(n1, wqkv_ref, bias_ref, proj_ref, width)


def post(mixed, xs, params, d, last):
    tokens, width = mixed.shape
    block = 256
    ff = params["wup"].shape[2]
    arrays, specs = ff_in(params, d)
    if not last:
        more, more_specs = attn_in(params, d + 1)
        arrays, specs = arrays + more, specs + more_specs
    ops = [mixed] + list(xs) + arrays
    x_specs = [tile(block, width)] if len(xs) == 1 else halves(tokens, block, width)
    outs = [(width, F32), (width, BF), (ff, BF), (ff, BF)]
    outs += [(width, BF)] if last else [(width, F32), (width, BF), (3 * width, BF)]
    flops = 2 * tokens * width * (width + 2 * ff + (0 if last else 3 * width))
    return pl.pallas_call(
        functools.partial(post_kernel, last, 4, len(xs)),
        grid=(tokens // block,),
        in_specs=[tile(block, width)] + x_specs + specs,
        out_specs=[tile(block, w) for w, _ in outs],
        out_shape=[sds(tokens, w, t) for w, t in outs],
        compiler_params=VMEM,
        cost_estimate=cost(flops, tokens * ff * 10, 2 * tokens * ff),
        name="post",
    )(*ops)


def norm_back(g_normed, xhat, rstd, gain):
    scaled = g_normed * gain
    mean1 = jnp.mean(scaled, -1, keepdims=True)
    mean2 = jnp.mean(scaled * xhat, -1, keepdims=True)
    return rstd * (scaled - mean1 - xhat * mean2)


def add_row(ref, row, start, value, fresh):
    cols = slice(start, start + value.shape[1])

    @pl.when(fresh)
    def _():
        ref[row : row + 1, cols] = value

    @pl.when(jnp.logical_not(fresh))
    def _():
        ref[row : row + 1, cols] += value


def colsum(x):
    return jnp.sum(x, 0, keepdims=True)


def ff_back_kernel(parts, n_x, *refs):
    gx_refs = refs[:n_x]
    slope_ref, resid_ref, wdown_ref, wup_ref, wout_ref, gain_ref = refs[n_x : n_x + 6]
    gy_ref, gu_ref, gres_ref, ga_ref, gmix_ref, vec_ref = refs[n_x + 6 :]
    fresh = pl.program_id(0) == 0
    width = resid_ref.shape[1]
    gx = joined(gx_refs)
    gy = gx.astype(BF)
    gy_ref[...] = gy
    hidden = wup_ref.shape[1] // parts
    g_n2 = None
    for j in range(parts):
        cols = slice(j * hidden, (j + 1) * hidden)
        g_act = dot_nt(gy, wdown_ref[cols, :])
        gu = (g_act * slope_ref[:, cols].astype(F32)).astype(BF)
        gu_ref[:, cols] = gu
        part = dot_nt(gu, wup_ref[:, cols])
        g_n2 = part if g_n2 is None else g_n2 + part
    xhat, rstd = normalize(resid_ref[...])
    g_resid = gx + norm_back(g_n2, xhat, rstd, gain_ref[...])
    gres_ref[...] = g_resid
    ga = g_resid.astype(BF)
    ga_ref[...] = ga
    gmix_ref[...] = dot_nt(ga, wout_ref[...]).astype(BF)
    add_row(vec_ref, 0, 0, colsum(g_n2 * xhat), fresh)
    add_row(vec_ref, 0, width, colsum(g_n2), fresh)


def ff_back(gxs, slope, resid, params, d, deps=()):
    tokens, width = resid.shape
    ff = slope.shape[1]
    block = 512
    outs = [(width, BF), (ff, BF), (width, F32), (width, BF), (width, BF)]
    assert ff == 4 * width
    x_specs = [tile(block, width)] if len(gxs) == 1 else halves(tokens, block, width)
    arrays = [params[n] for n in ("wdown", "wup", "wout", "gains")]
    return pl.pallas_call(
        ordered(functools.partial(ff_back_kernel, 4, len(gxs)), len(gxs) + 6, deps),
        grid=(tokens // block,),
        in_specs=x_specs
        + [tile(block, ff), tile(block, width)]
        + [layer(a, d, 1) for a in arrays]
        + anywhere(deps),
        out_specs=[tile(block, w) for w, _ in outs] + [pl.BlockSpec((8, 2 * width), lambda i: (0, 0))],
        out_shape=[sds(tokens, w, t) for w, t in outs] + [sds(8, 2 * width, F32)],
        compiler_params=VMEM,
        cost_estimate=cost(2 * tokens * width * (2 * ff + width), tokens * ff * 8),
        name="ff_back",
    )(*gxs, slope, resid, *arrays, *deps)


def qkv_back_kernel(grads_ref, wqkv_ref, x_ref, gres_ref, gain_ref, *refs):
    gx_ref, vec_ref = refs[-2:]
    fresh = pl.program_id(0) == 0
    width = x_ref.shape[1]
    grads = [grads_ref[n] for n in range(3)]
    g_norm = dot_nt(jnp.concatenate(grads, 1), wqkv_ref[...])
    xhat, rstd = normalize(x_ref[...].astype(F32))
    gx = gres_ref[...] + norm_back(g_norm, xhat, rstd, gain_ref[...])
    gx_ref[...] = gx.astype(gx_ref.dtype)
    add_row(vec_ref, 0, 0, colsum(g_norm * xhat), fresh)
    add_row(vec_ref, 0, width, colsum(g_norm), fresh)


def qkv_back(grads, x, g_resid, params, d, first, rows, dtype, deps=()):
    width = x.shape[1]
    block = 256
    at = first // block
    return pl.pallas_call(
        ordered(qkv_back_kernel, 5, deps),
        grid=(rows // block,),
        in_specs=[
            pl.BlockSpec((3, block, width), lambda i: (0, at + i, 0)),
            layer(params["wqkv"], d),
            tile(block, width),
            tile(block, width, at),
            layer(params["gains"], d, 0),
            *anywhere(deps),
        ],
        out_specs=[tile(block, width), pl.BlockSpec((8, 2 * width), lambda i: (0, 0))],
        out_shape=[sds(rows, width, dtype), sds(8, 2 * width, F32)],
        compiler_params=VMEM,
        cost_estimate=cost(6 * rows * width * width, rows * width * 20),
        name="qkv_back",
    )(grads, params["wqkv"], x, g_resid, params["gains"], *deps)


def plain_grad(lefts, right):
    return jnp.concatenate([dot_tn(left, right) for left in lefts], 0).astype(BF)


def deal(left_ref, right_ref, rows, start, refs, at):
    total = left_ref.shape[1]

    def store(mine):
        result = dot_tn(left_ref[...], right_ref[...])
        place = (lambda o: o) if mine is None else chunk_of
        owner = start // rows
        base = 0 if refs[0].shape[0] == place(31) + 1 else place(owner)
        while owner * rows < start + total:
            low = max(owner * rows, start)
            high = min((owner + 1) * rows, start + total)
            ref = refs[0] if mine is None or (owner >> 1) & 1 == mine else refs[1]
            to = at + low - owner * rows
            ref[place(owner) - base, to : to + high - low, :] = result[
                low - start : high - start
            ].astype(BF)
            owner += 1

    if len(refs) == 1:
        store(None)
        return
    core = lax.axis_index("dp") & 1
    for mine in range(2):
        pl.when(core == mine)(functools.partial(store, mine))


def chunk_of(owner):
    return (owner >> 2) * 2 + (owner & 1)


def grad_kernel(rows, by_left, n_out, left_ref, right_ref, *refs):
    sum_ref = refs[-1]
    deal(left_ref, right_ref, rows, 0, refs[-1 - n_out : -1], 0)

    @pl.when(jnp.logical_or(by_left, pl.program_id(0) == 0))
    def _():
        sum_ref[...] = jnp.broadcast_to(colsum(left_ref[...].astype(F32)), sum_ref.shape)


def grad_call(left, right, into, total, rows, offset, by_left, n_out=2, deps=()):
    tokens, wide = left.shape
    block = 768
    places = 32 // n_out
    deep = right.shape[1]
    if by_left:
        steps = wide // block
        lspec = pl.BlockSpec((tokens, block), lambda i: (0, i))
        rspec = pl.BlockSpec((tokens, block), lambda i: (0, 0))
        out = pl.BlockSpec((places // steps, rows, block), lambda i: (i, offset // rows, 0))
        sums = pl.BlockSpec((8, block), lambda i: (0, i))
    else:
        steps = deep // block
        lspec = pl.BlockSpec((tokens, block), lambda i: (0, 0))
        rspec = pl.BlockSpec((tokens, block), lambda i: (0, i))
        out = pl.BlockSpec((places, rows, block), lambda i: (0, offset // rows + i, 0))
        sums = pl.BlockSpec((8, block), lambda i: (0, 0))
    extra = list(into or ()) + list(deps)
    shape = jax.ShapeDtypeStruct((places, total, block), BF)
    return pl.pallas_call(
        functools.partial(grad_kernel, rows, by_left, n_out),
        grid=(steps,),
        in_specs=[lspec, rspec] + anywhere(extra),
        out_specs=[out] * n_out + [sums],
        out_shape=[shape] * n_out + [sds(8, wide, F32)],
        input_output_aliases={2 + n: n for n in range(len(into or ()))},
        compiler_params=VMEM,
        cost_estimate=cost(2 * tokens * wide * deep, 2 * (tokens + 16) * (wide + deep)),
        name="grad",
    )(left, right, *extra)


def qkv_grad_kernel(rows, n_out, left_ref, right_ref, *refs):
    sum_ref = refs[-1]
    step = pl.program_id(0)
    for n in range(3):

        @pl.when(step == n)
        def _():
            deal(left_ref, right_ref, rows, n * left_ref.shape[1], refs[-1 - n_out : -1], 0)

    sum_ref[...] = jnp.broadcast_to(colsum(left_ref[...].astype(F32)), sum_ref.shape)


def qkv_grad(grads, n1, into, total, n_out=2, deps=()):
    _, tokens, width = grads.shape
    rows = 3 * width // 32
    places = 32 // n_out
    extra = list(into or ()) + list(deps)
    shape = jax.ShapeDtypeStruct((places, total, width), BF)
    out = pl.BlockSpec((places, rows, width), lambda i: (0, total // rows - 1, 0))
    return pl.pallas_call(
        functools.partial(qkv_grad_kernel, rows, n_out),
        grid=(3,),
        in_specs=[
            pl.BlockSpec((None, tokens, width), lambda i: (i, 0, 0)),
            pl.BlockSpec((tokens, width), lambda i: (0, 0)),
        ]
        + anywhere(extra),
        out_specs=[out] * n_out + [pl.BlockSpec((8, width), lambda i: (0, i))],
        out_shape=[shape] * n_out + [sds(8, 3 * width, F32)],
        input_output_aliases={2 + n: n for n in range(len(into or ()))},
        compiler_params=VMEM,
        cost_estimate=cost(6 * tokens * width * width, 16 * tokens * width),
        name="qkv_grad",
    )(grads, n1, *extra)


ROWS = 512


def ff_all_kernel(n_x, n_out, firsts, d, *refs):
    it = iter(refs)
    gx_refs = [next(it) for _ in range(n_x)]
    slope_ref, resid_ref, gain_ref, active_ref = next(it), next(it), next(it), next(it)
    sources = [next(it) for _ in range(5)]
    refs = list(it)
    gres_ref, gmix_ref, vec_ref = refs[-16 - n_out : -13 - n_out]
    bufs = refs[-13 - n_out : -13]
    wdown, wup, wout, n2, mixed, gy_all, gu_all, ga_all, down, up, out, arrive, leave = refs[-13:]
    step = pl.program_id(0)
    tokens, width = gy_all.shape
    parts = wup.shape[1] // width
    blocks = tokens // ROWS
    thin = width // 32
    core = lax.axis_index("dp") & 1

    def load(n):
        j = n // 2
        rows = pl.ds(j * width, width)
        if j < parts and n % 2 == 0:
            pair = sources[0].at[d, rows], wdown.at[rows]
        elif j < parts:
            pair = sources[1].at[d, :, rows], wup.at[:, rows]
        else:
            late = n - 2 * parts
            pair = (sources[2].at[d], sources[3], sources[4])[late], (wout, n2, mixed)[late]
        return pltpu.make_async_copy(*pair, arrive.at[n])

    def arrived(n):
        pl.when(step == 0)(lambda: load(n).wait())

    @pl.when(step == 0)
    def _():
        for n in range(2 * parts + 3):
            load(n).start()

    def stores(kind, j):
        slot = j % 2
        if kind == "up":
            held, row, count, tall, place = up, firsts + 4 * thin, 8, 4 * thin, 8 * j
        else:
            held = down if kind == "down" else out
            row, count, tall, place = firsts + (j if kind == "down" else 8) * thin, 32, thin, 0
        sem = {"down": 0, "up": 4, "out": 8}[kind] + 2 * slot
        rows = pl.ds(row, tall)
        if n_out == 1:
            dst = bufs[0].at[pl.ds(place, count), rows]
            return [pltpu.make_async_copy(held.at[slot], dst, leave.at[sem])]
        part = count // 2
        found = []
        for n, buf in enumerate(bufs):
            src = held.at[slot, pl.ds((core if n == 0 else 1 - core) * part, part)]
            dst = buf.at[pl.ds(place // 2, part), rows]
            found.append(pltpu.make_async_copy(src, dst, leave.at[sem + n]))
        return found

    def put(held, slot, result):
        count, tall = held.shape[1], held.shape[2]
        for owner in range(count):
            at = owner if n_out == 1 else ((owner >> 1) & 1) * (count // 2) + chunk_of(owner)
            held[slot, at] = result[owner * tall : (owner + 1) * tall].astype(BF)

    @pl.when(step < blocks)
    def _():
        rows = pl.ds(pl.multiple_of(step * ROWS, ROWS), ROWS)
        fresh = step == 0
        gx = joined_rows(gx_refs, step)
        gy = gx.astype(BF)
        gy_all[rows, :] = gy
        g_n2 = None
        for j in range(parts):
            cols = slice(j * width, (j + 1) * width)
            arrived(2 * j)
            g_act = dot_nt(gy, wdown[cols, :])
            gu = (g_act * slope_ref[:, cols].astype(F32)).astype(BF)
            gu_all[rows, cols] = gu
            arrived(2 * j + 1)
            part = dot_nt(gu, wup[:, cols])
            g_n2 = part if g_n2 is None else g_n2 + part
        xhat, rstd = normalize(resid_ref[...])
        g_resid = gx + norm_back(g_n2, xhat, rstd, gain_ref[...])
        gres_ref[...] = g_resid
        ga = g_resid.astype(BF)
        ga_all[rows, :] = ga
        arrived(2 * parts)
        gmix_ref[...] = dot_nt(ga, wout[...]).astype(BF)
        add_row(vec_ref, 0, 0, colsum(g_n2 * xhat), fresh)
        add_row(vec_ref, 0, width, colsum(g_n2), fresh)
        add_row(vec_ref, 0, 2 * width, colsum(gy.astype(F32)), fresh)
        add_row(vec_ref, 0, 3 * width, colsum(ga.astype(F32)), fresh)

    arrived(2 * parts + 1)
    arrived(2 * parts + 2)
    for j in range(parts):

        @pl.when(step == blocks + j)
        def _():
            if j >= 2:
                for copy in stores("down", j - 2):
                    copy.wait()
            put(down, j % 2, dot_tn(gy_all[...], active_ref[...]))
            for copy in stores("down", j):
                copy.start()

        @pl.when(step == blocks + parts + j)
        def _():
            if j >= 2:
                for copy in stores("up", j - 2):
                    copy.wait()
            cols = slice(j * width, (j + 1) * width)
            left = gu_all[:, cols]
            put(up, j % 2, dot_tn(left, n2[...]))
            vec_ref[1:2, cols] = colsum(left.astype(F32))
            for copy in stores("up", j):
                copy.start()

    @pl.when(step == blocks + 2 * parts)
    def _():
        put(out, 0, dot_tn(ga_all[...], mixed[...]))
        for copy in stores("out", 0):
            copy.start()
        for kind, first, count in (("down", parts - 2, 2), ("up", parts - 2, 2), ("out", 0, 1)):
            for j in range(first, first + count):
                for copy in stores(kind, j):
                    copy.wait()


def joined_rows(refs, step):
    if len(refs) == 1:
        return refs[0][...].astype(F32)
    return jnp.where(step == 0, refs[0][...].astype(F32), refs[1][...].astype(F32))


def ff_all(gxs, slope, resid, active, n2, mixed, params, d, into, total, n_out):
    tokens, width = resid.shape
    ff = slope.shape[1]
    parts, blocks = ff // width, tokens // ROWS
    thin = width // 32
    early = lambda i: jnp.minimum(i, blocks - 1)
    row = lambda w: pl.BlockSpec((ROWS, w), lambda i: (early(i), 0))
    if len(gxs) == 1:
        x_specs = [row(width)]
    else:
        x_specs = [pl.BlockSpec((ROWS, width), lambda i: (0, 0), pipeline_mode=pl.Buffered(1))] * 2
    weights = [params[n] for n in ("wdown", "wup", "wout")]
    ops = [*gxs, slope, resid, params["gains"], active, *weights, n2, mixed]
    specs = x_specs + [
        row(ff),
        row(width),
        layer(params["gains"], d, 1),
        pl.BlockSpec((tokens, width), lambda i: (0, jnp.clip(i - blocks, 0, parts - 1))),
    ]
    extra = list(into or ())
    specs += anywhere(ops[len(specs) :]) + anywhere(extra)
    shape = jax.ShapeDtypeStruct((32 // n_out, total, width), BF)
    vec = pl.BlockSpec((8, ff), lambda i: (0, 0))
    vm = pltpu.VMEM
    scratch = [vm((ff, width), BF), vm((width, ff), BF), vm((width, width), BF)]
    scratch += [vm((tokens, width), BF)] * 3 + [vm((tokens, ff), BF), vm((tokens, width), BF)]
    scratch += [vm((2, 32, thin, width), BF), vm((2, 8, 4 * thin, width), BF), vm((1, 32, thin, width), BF)]
    scratch += [pltpu.SemaphoreType.DMA((2 * parts + 3,)), pltpu.SemaphoreType.DMA((12,))]
    flops = 2 * tokens * width * (4 * ff + 2 * width)
    return pl.pallas_call(
        functools.partial(ff_all_kernel, len(gxs), n_out, 0, d),
        grid=(blocks + 2 * parts + 1,),
        in_specs=specs,
        out_specs=[row(width), row(width), vec] + [pl.BlockSpec(memory_space=pl.ANY)] * n_out,
        out_shape=[sds(tokens, width, F32), sds(tokens, width, BF), sds(8, ff, F32)] + [shape] * n_out,
        input_output_aliases={len(ops) + n: 3 + n for n in range(len(extra))},
        scratch_shapes=scratch,
        compiler_params=pltpu.CompilerParams(
            vmem_limit_bytes=63 << 20, dimension_semantics=("arbitrary",)
        ),
        cost_estimate=cost(flops, 50 << 20),
        name="ff_all",
    )(*ops, *extra)


def plus(*parts):
    total = parts[0].astype(F32)
    for part in parts[1:]:
        total = total + part.astype(F32)
    return total


def place_xy():
    return (lax.axis_index("dp") >> 1) & 1, lax.axis_index("blk")


def stage1_kernel(tall, has_vec, keep, recv, *refs):
    kp, sp, kq, sq = refs[-4:]
    x, y = place_xy()
    both = lambda a, b, rows: plus(keep[0, a, b, rows], recv[0, a, b, rows]).astype(BF)
    up, low = slice(0, tall), slice(tall, keep.shape[3])
    stop = keep.shape[3] - tall
    for n in range(2):
        kp[0, n] = both(x, n, up)
        sp[0, n] = both(1 - x, n, up)
        kq[0, n, :stop] = both(n, y, low)
        sq[0, n, :stop] = both(n, 1 - y, low)
    if has_vec:
        vk, vr = refs[:2]
        for n in range(2):
            kq[0, n, stop:] = plus(vk[0, n, y], vr[0, n, y]).astype(BF)
            sq[0, n, stop:] = plus(vk[0, n, 1 - y], vr[0, n, 1 - y]).astype(BF)


def stage2_kernel(kp, rp, kq, rq, kp2, sp2, kq2, sq2):
    x, y = place_xy()
    kp2[0] = plus(kp[0, y], rp[0, y]).astype(BF)
    sp2[0] = plus(kp[0, 1 - y], rp[0, 1 - y]).astype(BF)
    kq2[0] = plus(kq[0, x], rq[0, x]).astype(BF)
    sq2[0] = plus(kq[0, 1 - x], rq[0, 1 - x]).astype(BF)


def stage3_kernel(kp, rp, kq, rq, own, *sends):
    tall = kp.shape[1]
    z = lax.axis_index("dp") >> 2
    for n, ref in enumerate((own,) + sends):
        at = z ^ n
        ref[:tall, :] = plus(kp[at], rp[at]).astype(ref.dtype)
        ref[tall:, :] = plus(kq[at], rq[at]).astype(ref.dtype)


def stage_call(kernel, name, ops, outs, deps):
    nbytes = sum(math.prod(a.shape) * 2 for a in ops) + sum(math.prod(s) * 2 for s in outs)
    spec = lambda shape: pl.BlockSpec((1,) + shape[1:], lambda i: (i,) + (0,) * (len(shape) - 1))
    return pl.pallas_call(
        ordered(kernel, len(ops), deps),
        grid=(ops[0].shape[0],),
        in_specs=[spec(a.shape) for a in ops] + anywhere(deps),
        out_specs=[spec(s) for s in outs],
        out_shape=[jax.ShapeDtypeStruct(s, BF) for s in outs],
        compiler_params=VMEM,
        cost_estimate=cost(nbytes, nbytes),
        name=name,
    )(*ops, *deps)


def xor_permute(x, dp, mask):
    return lax.ppermute(x, "dp", [(i, i ^ mask) for i in range(dp)])


class Group:
    def __init__(self, keep, send, tall, dp):
        self.tall, self.dp = tall, dp
        self.keep, self.recv = keep, xor_permute(send, dp, 1)

    def stage1(self, vec=None, deps=()):
        _, total, width = self.keep.shape
        tall = self.tall
        cut = lambda a: a.reshape(4, 2, 2, a.shape[1], width)
        ops = [cut(self.keep), cut(self.recv)]
        low = total - tall
        if vec is not None:
            ops += [cut(v) for v in vec]
            low += vec[0].shape[1]
        p, q = (4, 2, tall, width), (4, 2, low, width)
        kernel = functools.partial(stage1_kernel, tall, vec is not None)
        self.kp, sp, self.kq, sq = stage_call(kernel, "stage1", ops, [p, p, q, q], deps)
        self.rp, self.rq = xor_permute(sp, self.dp, 2), swap_halves(sq)
        return [self.kp]

    def stage2(self, deps=()):
        p, q = [(4,) + a.shape[2:] for a in (self.kp, self.kq)]
        ops = [self.kp, self.rp, self.kq, self.rq]
        self.kp, sp, self.kq, sq = stage_call(stage2_kernel, "stage2", ops, [p, p, q, q], deps)
        self.rp, self.rq = swap_halves(sp), xor_permute(sq, self.dp, 2)
        return [self.kp]

    def stage3(self, deps=()):
        ops = [self.kp, self.rp, self.kq, self.rq]
        total, width = self.kp.shape[1] + self.kq.shape[1], self.kp.shape[2]
        nbytes = total * width * 24
        pieces = pl.pallas_call(
            ordered(stage3_kernel, 4, deps),
            grid=(1,),
            in_specs=[pl.BlockSpec(a.shape, lambda i: (0, 0, 0)) for a in ops] + anywhere(deps),
            out_specs=[pl.BlockSpec((total, width), lambda i: (0, 0))] * 4,
            out_shape=[sds(total, width, F32)] + [sds(total, width, BF)] * 3,
            compiler_params=VMEM,
            cost_estimate=cost(nbytes, nbytes),
            name="stage3",
        )(*ops, *deps)
        moved = [xor_permute(pieces[n], self.dp, n << 2) for n in range(1, 4)]
        self.pieces = [pieces[0]] + moved
        return [pieces[0]]


def final_kernel(layout, counts, *refs):
    groups = []
    for count in counts:
        groups.append(refs[:count])
        refs = refs[count:]
    outs = dict(zip(layout["outs"], refs))
    width = groups[0][0].shape[1]

    def rows(group, start, count):
        return plus(*(ref[start : start + count, :] for ref in groups[group]))

    for d in range(LAYERS):
        place = layout["rows"][d]
        for name in ("qkv", "out", "up"):
            outs[name][d] = rows(*place[name])
        down = rows(*place["down"])
        thin = outs["down"].shape[1]
        for j in range(down.shape[0] // thin):
            outs["down"][d, :, j * width : (j + 1) * width] = down[j * thin : (j + 1) * thin]
    vec = rows(*layout["vec"])[0:1]
    at = 0
    for d in range(LAYERS):
        for name, n in layout["vectors"]:
            ref = outs[name]
            size = ref.shape[-1]
            value = vec[:, at : at + size]
            if n is None:
                ref[d : d + 1, :] = value
            else:
                ref[d, n : n + 1, :] = value
            at += size


VECTORS = (
    ("gains", 0),
    ("gains", 1),
    ("shifts", 0),
    ("shifts", 1),
    ("bq", None),
    ("bv", None),
    ("bout", None),
    ("bdown", None),
    ("bup", None),
)


def finish(layout, groups, shapes):
    ops = [a for g in groups for a in g]
    names = list(shapes)
    layout = dict(layout, outs=names, vectors=VECTORS)
    total = sum(math.prod(a.shape) for a in ops) * 2
    return dict(
        zip(
            names,
            pl.pallas_call(
                functools.partial(final_kernel, layout, [len(g) for g in groups]),
                out_shape=[jax.ShapeDtypeStruct(shapes[n], F32) for n in names],
                compiler_params=pltpu.CompilerParams(vmem_limit_bytes=58 << 20),
                cost_estimate=cost(total, total),
                name="finish",
            )(*ops),
        )
    )


def swap_halves(x):
    return lax.ppermute(x, "blk", [(0, 1), (1, 0)])


class Halving:
    def __init__(self, mesh):
        self.dp = mesh.shape["dp"]
        self.blk = mesh.shape["blk"]
        self.bits = self.dp.bit_length() - 1
        assert self.blk == 2 and 1 << self.bits == self.dp

    def stages(self, blk_first):
        dp_bits = list(range(self.bits))
        rest = ["blk", 1] if blk_first else [1, "blk"]
        return [0] + rest + dp_bits[2:]

    def split(self, rows):
        owners = self.dp * self.blk
        return rows.reshape((2,) * (self.bits + 1) + (rows.shape[0] // owners, rows.shape[1]))

    def run(self, rows, blk_first, wide=False):
        arr = self.split(rows)
        names = list(reversed(range(self.bits))) + ["blk"]
        order = self.stages(blk_first)
        for n, stage in enumerate(order):
            dim = names.index(stage)
            names.pop(dim)
            if stage == "blk":
                mine = lax.axis_index("blk")
                send = lambda x: lax.ppermute(x, "blk", [(0, 1), (1, 0)])
            else:
                mine = (lax.axis_index("dp") >> stage) & 1
                perm = [(i, i ^ (1 << stage)) for i in range(self.dp)]
                send = lambda x: lax.ppermute(x, "dp", perm)
            keep = lax.dynamic_index_in_dim(arr, mine, dim, keepdims=False)
            other = lax.dynamic_index_in_dim(arr, 1 - mine, dim, keepdims=False)
            arr = keep.astype(F32) + send(other).astype(F32)
            if not wide and n + 1 < len(order):
                arr = arr.astype(BF)
        return arr


class PlainSums:
    def __init__(self, mesh):
        self.halving = Halving(mesh)
        self.held = {}

    def add(self, name, d, lefts, right, blk_first):
        self.held[name, d] = self.halving.run(plain_grad(lefts, right), blk_first)

    def results(self, vec):
        vec = self.halving.run(vec, False, wide=True)[0]
        out = {
            n: jnp.stack([self.held[n, d].T for d in range(LAYERS)])
            for n in ("qkv", "out", "up", "down")
        }
        thin = vec.shape[0] // (12 * LAYERS)
        at = 0
        found = {}
        for d in range(LAYERS):
            for name, n in VECTORS:
                size = 4 * thin if name == "bup" else thin
                found.setdefault((name, d), []).append(vec[at : at + size])
                at += size
        for name in dict(VECTORS):
            rows = [jnp.stack(found[name, d]) for d in range(LAYERS)]
            out[name] = jnp.stack(rows if len(rows[0]) == 2 else [r[0] for r in rows])
        return out


def shards(
    mesh,
    hidden_in,
    cell_lengths,
    cotangent,
    ln_gains,
    ln_biases,
    w_qkv,
    b_query,
    b_value,
    w_out,
    b_out,
    w_up,
    b_up,
    w_down,
    b_down,
):
    cells, half, width = hidden_in.shape
    tokens = cells * half
    dp, blk = mesh.shape["dp"], mesh.shape["blk"]
    owners = dp * blk
    assert cells == blk == 2
    side = lax.axis_index("blk")
    meta = cell_lengths
    grouped = dp == 16 and width == 768 and b_up.shape[1] == 4 * width

    def split_cell(both):
        own = lax.dynamic_index_in_dim(both, side, 0, False)
        other = lax.dynamic_index_in_dim(both, 1 - side, 0, False)
        return own, swap_halves(other)

    def return_cell(own, back):
        return jnp.where(side == 0, jnp.stack([own, back]), jnp.stack([back, own]))

    rows = lambda v: v[..., None, :]
    params = {
        "gains": rows(ln_gains),
        "shifts": rows(ln_biases),
        "wqkv": w_qkv,
        "bias": rows(jnp.concatenate([b_query, jnp.zeros_like(b_query), b_value], 1)),
        "wout": w_out,
        "bout": rows(b_out),
        "wup": w_up,
        "bup": rows(b_up),
        "wdown": w_down,
        "bdown": rows(b_down),
    }
    own, other = split_cell(hidden_in)
    entered = enter(own, params, 0, None, tokens, 0)
    n1, proj = enter(other, params, 0, entered, tokens, half)
    xs = (own, other)
    saved = []
    for d in range(LAYERS):
        mixed, low, lse = attn_fwd(proj, meta)
        last = d + 1 == LAYERS
        outs = post(mixed, xs, params, d, last)
        saved.append((xs, n1, proj, mixed, low, lse) + tuple(outs[:4]))
        if not last:
            x, n1, proj = outs[4:]
            xs = (x,)
    out16 = outs[4]
    returned = swap_halves(out16[half:])
    hidden_out = return_cell(out16[:half], returned)

    gxs = split_cell(cotangent)
    backward = backward_grouped if grouped else backward_plain
    gx, out = backward(mesh, params, saved, gxs, meta, [returned])
    grad_in = return_cell(gx[0], gx[1].astype(F32))
    order = ("gains", "shifts", "qkv", "bq", "bv", "out", "bout", "up", "bup", "down", "bdown")
    return (hidden_out, grad_in) + tuple(out[n] for n in order)


def vector_rows(owners, width, ln1, ln2, sums):
    flat = []
    for d in range(LAYERS):
        for v in (
            ln1[d][:width],
            ln2[d][:width],
            ln1[d][width:],
            ln2[d][width:],
            sums["qkv", d][:width],
            sums["qkv", d][2 * width :],
            sums["out", d],
            sums["down", d],
            sums["up", d],
        ):
            flat.append(v.reshape(owners, -1))
    return jnp.concatenate(flat, 1)


def backward_plain(mesh, params, saved, gxs, meta, early):
    sums = PlainSums(mesh)
    ln1, ln2, cols = {}, {}, {}
    for d in reversed(range(LAYERS)):
        xs, n1, proj, mixed, low, lse, resid, n2, active, slope = saved[d]
        tokens, width = resid.shape
        gy, gu, g_resid, ga, g_mixed, vec2 = ff_back(gxs, slope, resid, params, d)
        sums.add("down", d, [gy], active, False)
        sums.add("up", d, [gu], n2, True)
        sums.add("out", d, [ga], mixed, False)
        grads = attn_bwd(proj, mixed, low, g_mixed, lse, meta, (0, width // 128))
        sums.add("qkv", d, [grads[n] for n in range(3)], n1, True)
        total = lambda a: jnp.sum(a.astype(F32), 0)
        cols.update({("down", d): total(gy), ("up", d): total(gu), ("out", d): total(ga)})
        cols["qkv", d] = jnp.concatenate([total(grads[n]) for n in range(3)])
        ln2[d] = vec2[0]
        if d > 0:
            gx, vec1 = qkv_back(grads, xs[0], g_resid, params, d, 0, tokens, F32)
            gxs = (gx,)
            ln1[d] = vec1[0]
        else:
            half = tokens // 2
            theirs, vec_a = qkv_back(grads, xs[1], g_resid, params, d, half, half, BF)
            mine, vec_b = qkv_back(grads, xs[0], g_resid, params, d, 0, half, F32)
            ln1[d] = vec_a[0] + vec_b[0]
    owners = mesh.shape["dp"] * mesh.shape["blk"]
    out = sums.results(vector_rows(owners, width, ln1, ln2, cols))
    return (mine, swap_halves(theirs)), out


def backward_grouped(mesh, params, saved, gxs, meta, early):
    dp = mesh.shape["dp"]
    ln1, ln2, cols = {}, {}, {}
    tokens, width = saved[0][6].shape
    half, t, pairs = tokens // 2, width // 32, width // 128

    def ff_grads(gxs, d, into, total, n_out):
        mixed, resid, n2, active, slope = saved[d][3], *saved[d][6:]
        g_resid, g_mixed, vec, *bufs = ff_all(
            gxs, slope, resid, active, n2, mixed, params, d, into, total, n_out
        )
        ln2[d] = vec[0, : 2 * width]
        cols["down", d], cols["out", d] = vec[0, 2 * width : 3 * width], vec[0, 3 * width :]
        cols["up", d] = vec[1]
        return g_resid, g_mixed, bufs

    xs, n1, proj, mixed, low, lse, resid, n2, active, slope = saved[1]
    g_resid, g_mixed, bufs = ff_grads(gxs, 1, None, 9 * t, 1)
    layer1 = lax.psum_scatter(bufs[0], ("dp", "blk"), scatter_dimension=0, tiled=True)[0]
    grads = attn_bwd(proj, mixed, low, g_mixed, lse, meta, (0, pairs), None, bufs + early)
    *bufs, sums = qkv_grad(grads, n1, None, 12 * t)
    cols["qkv", 1] = sums[0]
    gx, vec = qkv_back(grads, xs[0], g_resid, params, 1, 0, tokens, F32, bufs)
    ln1[1] = vec[0]
    xs, n1, proj, mixed, low, lse, resid, n2, active, slope = saved[0]
    g_resid, g_mixed, bufs = ff_grads((gx,), 0, bufs, 12 * t, 2)
    ff0 = Group(*bufs, 6 * t, dp)
    grads = attn_bwd(proj, mixed, low, g_mixed, lse, meta, (0, 2), None, [ff0.keep])
    dep = ff0.stage1(deps=[grads])
    grads = attn_bwd(proj, mixed, low, g_mixed, lse, meta, (2, pairs), grads, dep)
    *bufs, sums = qkv_grad(grads, n1, None, 3 * t)
    cols["qkv", 0] = sums[0]
    at0 = Group(*bufs, 48, dp)
    theirs, vec_a = qkv_back(grads, xs[1], g_resid, params, 0, half, half, BF, [at0.keep])
    back = swap_halves(theirs)
    dep = ff0.stage2(deps=[theirs])
    mine, vec_b = qkv_back(grads, xs[0], g_resid, params, 0, 0, half, F32, dep)
    ln1[0] = vec_a[0] + vec_b[0]
    vec = vector_rows(32, width, ln1, ln2, cols)
    vec = jnp.pad(vec, ((0, 0), (0, width - vec.shape[1]))).astype(BF)
    vec = jnp.pad(vec[:, None], ((0, 0), (0, 7), (0, 0))).reshape(8, 2, 2, 8, width)
    core = lax.axis_index("dp") & 1
    deal_core = lambda core: lax.dynamic_index_in_dim(vec, core, 1, False).reshape(16, 8, width)
    kept, sent = deal_core(core), deal_core(1 - core)
    vec = [kept, xor_permute(sent, dp, 1)]
    dep = at0.stage1(vec, deps=[back])
    dep = ff0.stage3(deps=dep)
    dep = at0.stage2(deps=dep)
    at0.stage3(deps=ff0.pieces[1:])
    layout = {
        "rows": [
            {"down": (1, 0, 4 * t), "up": (1, 4 * t, 4 * t), "out": (1, 8 * t, t), "qkv": (2, 0, 3 * t)},
            {"down": (0, 0, 4 * t), "up": (0, 4 * t, 4 * t), "out": (0, 8 * t, t), "qkv": (1, 9 * t, 3 * t)},
        ],
        "vec": (2, 3 * t, 8),
    }
    shapes = {
        "qkv": (LAYERS, 3 * t, width),
        "out": (LAYERS, t, width),
        "up": (LAYERS, 4 * t, width),
        "down": (LAYERS, t, 4 * width),
        "gains": (LAYERS, 2, t),
        "shifts": (LAYERS, 2, t),
        "bq": (LAYERS, t),
        "bv": (LAYERS, t),
        "bout": (LAYERS, t),
        "bdown": (LAYERS, t),
        "bup": (LAYERS, 4 * t),
    }
    out = finish(layout, [[layer1], ff0.pieces, at0.pieces], shapes)
    for name in ("qkv", "out", "up", "down"):
        out[name] = jnp.swapaxes(out[name], 1, 2)
    return (mine, back), out


def solution(mesh):
    both = ("dp", "blk")
    row = P("dp", "blk", None)
    last3 = P(None, None, both)
    last2 = P(None, both)
    return jax.shard_map(
        functools.partial(shards, mesh),
        mesh=mesh,
        in_specs=(row, P("dp"), row) + (P(),) * 11,
        out_specs=(
            row,
            row,
            last3,
            last3,
            last3,
            last2,
            last2,
            last3,
            last2,
            last3,
            last2,
            last3,
            last2,
        ),
        check_vma=False,
    )
```

```python
import functools
import math

import jax
import jax.numpy as jnp
from jax import lax
from jax.experimental import pallas as pl
from jax.experimental.pallas import tpu as pltpu
from jax.sharding import PartitionSpec as P

HEAD_DIM = 64
LAYERS = 2
EPSILON = 1e-05
NEG = -1e30
BF = jnp.bfloat16
F32 = jnp.float32
QSCALE = math.log2(math.e) / math.sqrt(HEAD_DIM)


def dot_nn(a, b):
    return lax.dot_general(a, b, (((1,), (0,)), ((), ())), preferred_element_type=F32)


def dot_nt(a, b):
    return lax.dot_general(a, b, (((1,), (1,)), ((), ())), preferred_element_type=F32)


def dot_tn(a, b):
    return lax.dot_general(a, b, (((0,), (0,)), ((), ())), preferred_element_type=F32)


def mask_block(meta_ref, kaug, qone, tokens):
    side = lax.axis_index("blk")
    rows = lax.broadcasted_iota(jnp.int32, (tokens, 128), 0)
    lanes = lax.broadcasted_iota(jnp.int32, (tokens, 128), 1)
    half = tokens // 2
    position = jnp.where(rows < half, rows + side * half, rows - side * half)
    masked = jnp.logical_and(lanes == 0, position >= meta_ref[side])
    kaug[...] = jnp.where(masked, NEG, 0.0).astype(BF)
    qone[...] = jnp.where(lanes == 0, 1.0, 0.0).astype(BF)


def attn_fwd_kernel(
    chunk, ahead, meta_ref, q_ref, k_ref, v_ref, o_ref, low_ref, lse_ref, kaug, qone
):
    tokens = q_ref.shape[0]

    @pl.when(pl.program_id(0) == 0)
    def _():
        mask_block(meta_ref, kaug, qone, tokens)

    first = lax.broadcasted_iota(jnp.int32, (tokens, 128), 1) < HEAD_DIM
    q, k, v = q_ref[...], k_ref[...], v_ref[...]
    zero = jnp.zeros_like(k)
    sel = [first, jnp.logical_not(first)]
    keys = [jnp.concatenate([jnp.where(sel[h], k, zero), kaug[...]], 1) for h in range(2)]
    vals = [jnp.where(sel[h], v, zero).T for h in range(2)]
    qa = jnp.concatenate([q, qone[...]], 1)
    units = [(c, h) for c in range(tokens // chunk) for h in range(2)]
    ready = {}

    def scores(unit):
        c, h = unit
        ready[unit] = dot_nt(keys[h], qa[c * chunk : (c + 1) * chunk])

    for unit in units[:ahead]:
        scores(unit)
    kept = {}
    for n, unit in enumerate(units):
        if n + ahead < len(units):
            scores(units[n + ahead])
        c, h = unit
        cols = slice(c * chunk, (c + 1) * chunk)
        st = ready.pop(unit)
        top = jnp.max(st, axis=0, keepdims=True)
        p = jnp.exp2(st - top)
        p = p.astype(BF)
        total = jnp.sum(p.astype(F32), axis=0, keepdims=True)
        kept[h] = (dot_nn(vals[h], p), top, total)
        if h == 1:
            head = lax.broadcasted_iota(jnp.int32, (128, chunk), 0) < HEAD_DIM
            inv = jnp.where(head, 1.0 / kept[0][2], 1.0 / kept[1][2])
            out = ((kept[0][0] + kept[1][0]) * inv).T
            high = out.astype(BF)
            o_ref[cols, :] = high
            low_ref[cols, :] = (out - high.astype(F32)).astype(BF)
            for g in range(2):
                lse_ref[0, g : g + 1, cols] = kept[g][1] + jnp.log2(kept[g][2])


def attn_fwd(proj, meta):
    tokens, width = proj.shape[0], proj.shape[1] // 3
    pairs = width // 128
    spec = lambda off: pl.BlockSpec((tokens, 128), lambda i, m: (0, off + i))
    return pl.pallas_call(
        functools.partial(attn_fwd_kernel, tokens // 2, 2),
        grid_spec=pltpu.PrefetchScalarGridSpec(
            num_scalar_prefetch=1,
            grid=(pairs,),
            in_specs=[spec(0), spec(pairs), spec(2 * pairs)],
            out_specs=[spec(0), spec(0), pl.BlockSpec((1, 8, tokens), lambda i, m: (i, 0, 0))],
            scratch_shapes=[pltpu.VMEM((tokens, 128), BF), pltpu.VMEM((tokens, 128), BF)],
        ),
        out_shape=[
            jax.ShapeDtypeStruct((tokens, width), BF),
            jax.ShapeDtypeStruct((tokens, width), BF),
            jax.ShapeDtypeStruct((pairs, 8, tokens), F32),
        ],
        compiler_params=pltpu.CompilerParams(
            vmem_limit_bytes=56 << 20, dimension_semantics=("arbitrary",)
        ),
        cost_estimate=pl.CostEstimate(
            flops=4 * tokens * tokens * width * 3,
            bytes_accessed=tokens * width * 8,
            transcendentals=pairs * 2 * tokens * tokens,
        ),
        name="attn_fwd",
    )(meta, proj, proj, proj)


def attn_bwd_kernel(
    meta_ref, q_ref, k_ref, v_ref, o_ref, low_ref, do_ref, lse_ref, out_ref, kaug, qone
):
    tokens = q_ref.shape[0]

    @pl.when(pl.program_id(0) == 0)
    def _():
        mask_block(meta_ref, kaug, qone, tokens)

    first = lax.broadcasted_iota(jnp.int32, (tokens, 128), 1) < HEAD_DIM
    q, k, v, do = q_ref[...], k_ref[...], v_ref[...], do_ref[...]
    zero = jnp.zeros_like(k)
    sel = [first, jnp.logical_not(first)]
    qa = jnp.concatenate([q, qone[...]], 1)
    prod = ((o_ref[...].astype(F32) + low_ref[...].astype(F32)) * do.astype(F32)).T
    dq = dk = dv = None
    for h in range(2):
        kh = jnp.where(sel[h], k, zero)
        delta = jnp.sum(prod[h * HEAD_DIM : (h + 1) * HEAD_DIM], 0, keepdims=True)
        st = dot_nt(jnp.concatenate([kh, kaug[...]], 1), qa)
        dpt = dot_nt(jnp.where(sel[h], v, zero), do)
        p = jnp.exp2(st - lse_ref[0, h : h + 1, :])
        ds = (p * (dpt - delta)).astype(BF)
        dvh = dot_nn(p.astype(BF), jnp.where(sel[h], do, zero))
        dkh = dot_nn(ds, jnp.where(sel[h], q, zero))
        dqh = dot_nn(kh.T, ds)
        dq, dk, dv = (dqh, dkh, dvh) if h == 0 else (dq + dqh, dk + dkh, dv + dvh)
    out_ref[0] = (dq * (1.0 / math.sqrt(HEAD_DIM))).T.astype(BF)
    out_ref[1] = (dk * math.log(2.0)).astype(BF)
    out_ref[2] = dv.astype(BF)


def attn_bwd(proj, mixed, low, g_mixed, lse, meta, pairs, into=None, deps=()):
    tokens, width = mixed.shape
    count = width // 128
    start, stop = pairs
    spec = lambda off: pl.BlockSpec((tokens, 128), lambda i, m: (0, off + start + i))
    ops = [meta, proj, proj, proj, mixed, low, g_mixed, lse]
    specs = [spec(0), spec(count), spec(2 * count), spec(0), spec(0), spec(0)]
    specs += [pl.BlockSpec((1, 8, tokens), lambda i, m: (start + i, 0, 0))]
    extra = ([] if into is None else [into]) + list(deps)
    return pl.pallas_call(
        ordered(attn_bwd_kernel, len(ops), extra),
        grid_spec=pltpu.PrefetchScalarGridSpec(
            num_scalar_prefetch=1,
            grid=(stop - start,),
            in_specs=specs + anywhere(extra),
            out_specs=pl.BlockSpec((3, tokens, 128), lambda i, m: (0, 0, start + i)),
            scratch_shapes=[pltpu.VMEM((tokens, 128), BF), pltpu.VMEM((tokens, 128), BF)],
        ),
        out_shape=jax.ShapeDtypeStruct((3, tokens, width), BF),
        input_output_aliases={} if into is None else {len(ops): 0},
        compiler_params=pltpu.CompilerParams(
            vmem_limit_bytes=56 << 20, dimension_semantics=("arbitrary",)
        ),
        cost_estimate=cost(1, 1),
        name="attn_bwd",
    )(*ops, *extra)


VMEM = pltpu.CompilerParams(vmem_limit_bytes=58 << 20, dimension_semantics=("arbitrary",))


def ordered(kernel, n_in, deps):
    if not deps:
        return kernel
    return lambda *refs: kernel(*refs[:n_in], *refs[n_in + len(deps) :])


def after(array, deps):
    return lax.optimization_barrier((array, *deps))[0]


def anywhere(arrays):
    return [pl.BlockSpec(memory_space=pl.ANY)] * len(arrays)


def layer(arr, d, n=0):
    lead = arr.ndim - 2
    index = (d, n)[:lead] + (0, 0)
    return pl.BlockSpec(
        (None,) * lead + arr.shape[lead:], lambda *_: index, pipeline_mode=pl.Buffered(1)
    )


def tile(rows, width, first=0):
    return pl.BlockSpec((rows, width), lambda i, *_: (first + i, 0))


def sds(rows, width, dtype):
    return jax.ShapeDtypeStruct((rows, width), dtype)


def cost(flops, nbytes, trans=0):
    return pl.CostEstimate(flops=int(flops), bytes_accessed=int(nbytes), transcendentals=int(trans))


def normalize(x):
    mean = jnp.mean(x, -1, keepdims=True)
    centered = x - mean
    variance = jnp.mean(centered * centered, -1, keepdims=True)
    rstd = lax.rsqrt(variance + EPSILON)
    return centered * rstd, rstd


def project(n1, wqkv_ref, bias_ref, proj_ref, width):
    for j, factor in enumerate((QSCALE, 1.0, 1.0)):
        cols = slice(j * width, (j + 1) * width)
        part = dot_nn(n1, wqkv_ref[:, cols]) + bias_ref[:, cols]
        proj_ref[:, cols] = (part * factor).astype(BF)


def attn_in(params, d):
    arrays = [params["gains"], params["shifts"], params["wqkv"], params["bias"]]
    return arrays, [layer(arrays[0], d, 0), layer(arrays[1], d, 0), layer(arrays[2], d), layer(arrays[3], d)]


def enter_kernel(x_ref, gain_ref, shift_ref, wqkv_ref, bias_ref, *refs):
    n1_ref, proj_ref = refs[-2:]
    width = x_ref.shape[1]
    xhat, _ = normalize(x_ref[...].astype(F32))
    n1 = (xhat * gain_ref[...] + shift_ref[...]).astype(BF)
    n1_ref[...] = n1
    project(n1, wqkv_ref, bias_ref, proj_ref, width)


def enter(x, params, d, into, tokens, first):
    rows, width = x.shape
    block = 256
    at = first // block
    arrays, specs = attn_in(params, d)
    ops = [x] + arrays
    specs = [tile(block, width)] + specs
    alias = {}
    if into is not None:
        ops += list(into)
        specs += [pl.BlockSpec(memory_space=pl.ANY)] * 2
        alias = {5: 0, 6: 1}
    return pl.pallas_call(
        enter_kernel,
        grid=(rows // block,),
        in_specs=specs,
        out_specs=[tile(block, width, at), tile(block, 3 * width, at)],
        out_shape=[sds(tokens, width, BF), sds(tokens, 3 * width, BF)],
        input_output_aliases=alias,
        compiler_params=VMEM,
        cost_estimate=cost(6 * rows * width * width, rows * width * 10 + 6 * width * width),
        name="enter",
    )(*ops)


def halves(tokens, block, width):
    turn = tokens // block // 2
    own = pl.BlockSpec((block, width), lambda i, *_: (jnp.minimum(i, turn - 1), 0))
    other = pl.BlockSpec((block, width), lambda i, *_: (jnp.maximum(i - turn, 0), 0))
    return [own, other]


def joined(refs):
    if len(refs) == 1:
        return refs[0][...].astype(F32)
    early = pl.program_id(0) < pl.num_programs(0) // 2
    return jnp.where(early, refs[0][...].astype(F32), refs[1][...].astype(F32))


def post_kernel(d, last, parts, n_x, *refs):
    it = iter(refs)
    mixed_ref = next(it)
    x_refs = [next(it) for _ in range(n_x)]
    bout_ref, gain_ref, shift_ref, bup_ref, bdown_ref = [next(it) for _ in range(5)]
    if not last:
        gain1_ref, shift1_ref, bias_ref = next(it), next(it), next(it)
    sources = [next(it) for _ in range(3 if last else 4)]
    resid_ref, n2_ref, active_ref, slope_ref = next(it), next(it), next(it), next(it)
    outs = [next(it) for _ in range(2 if last else 3)]
    wout, wup, wdown = next(it), next(it), next(it)
    wqkv = None if last else next(it)
    arrive = next(it)
    step = pl.program_id(0)
    width = mixed_ref.shape[1]
    hidden = wup.shape[1] // parts

    def load(n):
        part = pl.ds((n - 1) // 2 * hidden, hidden)
        if n == 0:
            pair = sources[0].at[d], wout
        elif n > 2 * parts:
            pair = sources[3].at[d + 1], wqkv
        elif n % 2:
            pair = sources[1].at[d, :, part], wup.at[:, part]
        else:
            pair = sources[2].at[d, part], wdown.at[part]
        return pltpu.make_async_copy(*pair, arrive.at[n])

    @pl.when(step == 0)
    def _():
        for n in range(2 * parts + (1 if last else 2)):
            load(n).start()

    def body(wait):
        wait(0)
        resid = joined(x_refs) + dot_nn(mixed_ref[...], wout[...]) + bout_ref[...]
        resid_ref[...] = resid
        xhat, _ = normalize(resid)
        n2 = (xhat * gain_ref[...] + shift_ref[...]).astype(BF)
        n2_ref[...] = n2
        total = resid + bdown_ref[...]
        for j in range(parts):
            cols = slice(j * hidden, (j + 1) * hidden)
            wait(2 * j + 1)
            upper = dot_nn(n2, wup[:, cols]) + bup_ref[:, cols]
            cdf = 0.5 + 0.5 * lax.erf(upper * math.sqrt(0.5))
            dens = jnp.exp2(upper * upper * (-0.5 * math.log2(math.e))) * (1.0 / math.sqrt(2.0 * math.pi))
            active = (upper * cdf).astype(BF)
            active_ref[:, cols] = active
            slope_ref[:, cols] = (cdf + upper * dens).astype(BF)
            wait(2 * j + 2)
            total = total + dot_nn(active, wdown[cols, :])
        if last:
            for n, ref in enumerate(outs):

                @pl.when(step // (pl.num_programs(0) // 2) == n)
                def _():
                    ref[...] = total.astype(BF)
        else:
            x_out, n1_ref, proj_ref = outs
            x_out[...] = total
            xhat, _ = normalize(total)
            n1 = (xhat * gain1_ref[...] + shift1_ref[...]).astype(BF)
            n1_ref[...] = n1
            wait(2 * parts + 1)
            project(n1, wqkv, bias_ref, proj_ref, width)

    pl.when(step == 0)(lambda: body(lambda n: load(n).wait()))
    pl.when(step > 0)(lambda: body(lambda n: None))


def post(mixed, xs, params, d, last):
    tokens, width = mixed.shape
    block = 256
    parts = 4
    ff = params["wup"].shape[2]
    small = [(params[n], d) for n in ("bout", "gains", "shifts", "bup", "bdown")]
    specs = [layer(a, e, 1) for a, e in small]
    weights = ["wout", "wup", "wdown"]
    if not last:
        more = [(params[n], d + 1) for n in ("gains", "shifts", "bias")]
        specs += [layer(a, e, 0) for a, e in more]
        small += more
        weights.append("wqkv")
    arrays = [a for a, _ in small] + [params[n] for n in weights]
    ops = [mixed] + list(xs) + arrays
    x_specs = [tile(block, width)] if len(xs) == 1 else halves(tokens, block, width)
    outs = [(tokens, width, F32), (tokens, width, BF), (tokens, ff, BF), (tokens, ff, BF)]
    out_specs = [tile(block, w) for _, w, _ in outs]
    if last:
        outs += [(tokens // 2, width, BF)] * 2
        out_specs += halves(tokens, block, width)
    else:
        outs += [(tokens, width, F32), (tokens, width, BF), (tokens, 3 * width, BF)]
        out_specs += [tile(block, w) for _, w, _ in outs[4:]]
    flops = 2 * tokens * width * (width + 2 * ff + (0 if last else 3 * width))
    return pl.pallas_call(
        functools.partial(post_kernel, d, last, parts, len(xs)),
        grid=(tokens // block,),
        in_specs=[tile(block, width)] + x_specs + specs + anywhere(weights),
        out_specs=out_specs,
        out_shape=[sds(*o) for o in outs],
        scratch_shapes=[pltpu.VMEM(params[n].shape[1:], BF) for n in weights]
        + [pltpu.SemaphoreType.DMA((2 * parts + 2,))],
        compiler_params=VMEM,
        cost_estimate=cost(flops, tokens * ff * 10, 2 * tokens * ff),
        name="post",
    )(*ops)


def norm_back(g_normed, xhat, rstd, gain):
    scaled = g_normed * gain
    mean1 = jnp.mean(scaled, -1, keepdims=True)
    mean2 = jnp.mean(scaled * xhat, -1, keepdims=True)
    return rstd * (scaled - mean1 - xhat * mean2)


def add_row(ref, row, start, value, fresh):
    cols = slice(start, start + value.shape[1])

    @pl.when(fresh)
    def _():
        ref[row : row + 1, cols] = value

    @pl.when(jnp.logical_not(fresh))
    def _():
        ref[row : row + 1, cols] += value


def colsum(x):
    return jnp.sum(x, 0, keepdims=True)


def ff_back_kernel(parts, n_x, *refs):
    gx_refs = refs[:n_x]
    slope_ref, resid_ref, wdown_ref, wup_ref, wout_ref, gain_ref = refs[n_x : n_x + 6]
    gy_ref, gu_ref, gres_ref, ga_ref, gmix_ref, vec_ref = refs[n_x + 6 :]
    fresh = pl.program_id(0) == 0
    width = resid_ref.shape[1]
    gx = joined(gx_refs)
    gy = gx.astype(BF)
    gy_ref[...] = gy
    hidden = wup_ref.shape[1] // parts
    g_n2 = None
    for j in range(parts):
        cols = slice(j * hidden, (j + 1) * hidden)
        g_act = dot_nt(gy, wdown_ref[cols, :])
        gu = (g_act * slope_ref[:, cols].astype(F32)).astype(BF)
        gu_ref[:, cols] = gu
        part = dot_nt(gu, wup_ref[:, cols])
        g_n2 = part if g_n2 is None else g_n2 + part
    xhat, rstd = normalize(resid_ref[...])
    g_resid = gx + norm_back(g_n2, xhat, rstd, gain_ref[...])
    gres_ref[...] = g_resid
    ga = g_resid.astype(BF)
    ga_ref[...] = ga
    gmix_ref[...] = dot_nt(ga, wout_ref[...]).astype(BF)
    add_row(vec_ref, 0, 0, colsum(g_n2 * xhat), fresh)
    add_row(vec_ref, 0, width, colsum(g_n2), fresh)


def ff_back(gxs, slope, resid, params, d, deps=()):
    tokens, width = resid.shape
    ff = slope.shape[1]
    block = 512
    outs = [(width, BF), (ff, BF), (width, F32), (width, BF), (width, BF)]
    assert ff == 4 * width
    x_specs = [tile(block, width)] if len(gxs) == 1 else halves(tokens, block, width)
    arrays = [params[n] for n in ("wdown", "wup", "wout", "gains")]
    return pl.pallas_call(
        ordered(functools.partial(ff_back_kernel, 4, len(gxs)), len(gxs) + 6, deps),
        grid=(tokens // block,),
        in_specs=x_specs
        + [tile(block, ff), tile(block, width)]
        + [layer(a, d, 1) for a in arrays]
        + anywhere(deps),
        out_specs=[tile(block, w) for w, _ in outs] + [pl.BlockSpec((8, 2 * width), lambda i: (0, 0))],
        out_shape=[sds(tokens, w, t) for w, t in outs] + [sds(8, 2 * width, F32)],
        compiler_params=VMEM,
        cost_estimate=cost(2 * tokens * width * (2 * ff + width), tokens * ff * 8),
        name="ff_back",
    )(*gxs, slope, resid, *arrays, *deps)


def qkv_back_kernel(grads_ref, wqkv_ref, x_ref, gres_ref, gain_ref, *refs):
    gx_ref, vec_ref = refs[-2:]
    fresh = pl.program_id(0) == 0
    width = x_ref.shape[1]
    grads = [grads_ref[n] for n in range(3)]
    g_norm = dot_nt(jnp.concatenate(grads, 1), wqkv_ref[...])
    xhat, rstd = normalize(x_ref[...].astype(F32))
    gx = gres_ref[...] + norm_back(g_norm, xhat, rstd, gain_ref[...])
    gx_ref[...] = gx.astype(gx_ref.dtype)
    add_row(vec_ref, 0, 0, colsum(g_norm * xhat), fresh)
    add_row(vec_ref, 0, width, colsum(g_norm), fresh)


def qkv_back(grads, x, g_resid, params, d, first, rows, dtype, deps=()):
    width = x.shape[1]
    block = 256
    at = first // block
    return pl.pallas_call(
        ordered(qkv_back_kernel, 5, deps),
        grid=(rows // block,),
        in_specs=[
            pl.BlockSpec((3, block, width), lambda i: (0, at + i, 0)),
            layer(params["wqkv"], d),
            tile(block, width),
            tile(block, width, at),
            layer(params["gains"], d, 0),
            *anywhere(deps),
        ],
        out_specs=[tile(block, width), pl.BlockSpec((8, 2 * width), lambda i: (0, 0))],
        out_shape=[sds(rows, width, dtype), sds(8, 2 * width, F32)],
        compiler_params=VMEM,
        cost_estimate=cost(6 * rows * width * width, rows * width * 20),
        name="qkv_back",
    )(grads, params["wqkv"], x, g_resid, params["gains"], *deps)


def plain_grad(lefts, right):
    return jnp.concatenate([dot_tn(left, right) for left in lefts], 0).astype(BF)


def chunk_of(owner):
    return (owner >> 2) * 2 + (owner & 1)


ROWS = 512


def ff_all_kernel(n_x, n_out, firsts, d, *refs):
    it = iter(refs)
    gx_refs = [next(it) for _ in range(n_x)]
    slope_ref, resid_ref, gain_ref, active_ref = next(it), next(it), next(it), next(it)
    sources = [next(it) for _ in range(5)]
    refs = list(it)
    gres_ref, gmix_ref, vec_ref = refs[-16 - n_out : -13 - n_out]
    bufs = refs[-13 - n_out : -13]
    wdown, wup, wout, n2, mixed, gy_all, gu_all, ga_all, down, up, out, arrive, leave = refs[-13:]
    step = pl.program_id(0)
    tokens, width = gy_all.shape
    parts = wup.shape[1] // width
    blocks = tokens // ROWS
    thin = width // 32
    core = lax.axis_index("dp") & 1

    def load(n):
        j = n // 2
        rows = pl.ds(j * width, width)
        if j < parts and n % 2 == 0:
            pair = sources[0].at[d, rows], wdown.at[rows]
        elif j < parts:
            pair = sources[1].at[d, :, rows], wup.at[:, rows]
        else:
            late = n - 2 * parts
            pair = (sources[2].at[d], sources[3], sources[4])[late], (wout, n2, mixed)[late]
        return pltpu.make_async_copy(*pair, arrive.at[n])

    @pl.when(step == 0)
    def _():
        for n in range(2 * parts + 3):
            load(n).start()

    def stores(kind, j):
        slot = j % 2
        if kind == "up":
            held, row, count, tall, place = up, firsts + 4 * thin, 8, 4 * thin, 8 * j
        else:
            held = down if kind == "down" else out
            row, count, tall, place = firsts + (j if kind == "down" else 8) * thin, 32, thin, 0
        sem = {"down": 0, "up": 4, "out": 8}[kind] + 2 * slot
        rows = pl.ds(row, tall)
        if n_out == 1:
            dst = bufs[0].at[pl.ds(place, count), rows]
            return [pltpu.make_async_copy(held.at[slot], dst, leave.at[sem])]
        part = count // 2
        found = []
        for n, buf in enumerate(bufs):
            src = held.at[slot, pl.ds((core if n == 0 else 1 - core) * part, part)]
            dst = buf.at[pl.ds(place // 2, part), rows]
            found.append(pltpu.make_async_copy(src, dst, leave.at[sem + n]))
        return found

    def put(held, slot, result):
        count, tall = held.shape[1], held.shape[2]
        for owner in range(count):
            at = owner if n_out == 1 else ((owner >> 1) & 1) * (count // 2) + chunk_of(owner)
            held[slot, at] = result[owner * tall : (owner + 1) * tall].astype(BF)

    def body(wait):
        rows = pl.ds(pl.multiple_of(step * ROWS, ROWS), ROWS)
        fresh = step == 0
        gx = joined_rows(gx_refs, step)
        gy = gx.astype(BF)
        gy_all[rows, :] = gy
        g_n2 = None
        for j in range(parts):
            cols = slice(j * width, (j + 1) * width)
            wait(2 * j)
            g_act = dot_nt(gy, wdown[cols, :])
            gu = (g_act * slope_ref[:, cols].astype(F32)).astype(BF)
            gu_all[rows, cols] = gu
            wait(2 * j + 1)
            part = dot_nt(gu, wup[:, cols])
            g_n2 = part if g_n2 is None else g_n2 + part
        xhat, rstd = normalize(resid_ref[...])
        g_resid = gx + norm_back(g_n2, xhat, rstd, gain_ref[...])
        gres_ref[...] = g_resid
        ga = g_resid.astype(BF)
        ga_all[rows, :] = ga
        wait(2 * parts)
        gmix_ref[...] = dot_nt(ga, wout[...]).astype(BF)
        add_row(vec_ref, 0, 0, colsum(g_n2 * xhat), fresh)
        add_row(vec_ref, 0, width, colsum(g_n2), fresh)
        add_row(vec_ref, 0, 2 * width, colsum(gy.astype(F32)), fresh)
        add_row(vec_ref, 0, 3 * width, colsum(ga.astype(F32)), fresh)

    pl.when(step == 0)(lambda: body(lambda n: load(n).wait()))
    pl.when(jnp.logical_and(step > 0, step < blocks))(lambda: body(lambda n: None))

    @pl.when(step == blocks)
    def _():
        load(2 * parts + 1).wait()
        load(2 * parts + 2).wait()

    for j in range(parts):

        @pl.when(step == blocks + j)
        def _():
            if j >= 2:
                for copy in stores("down", j - 2):
                    copy.wait()
            put(down, j % 2, dot_tn(gy_all[...], active_ref[...]))
            for copy in stores("down", j):
                copy.start()

        @pl.when(step == blocks + parts + j)
        def _():
            if j >= 2:
                for copy in stores("up", j - 2):
                    copy.wait()
            cols = slice(j * width, (j + 1) * width)
            left = gu_all[:, cols]
            put(up, j % 2, dot_tn(left, n2[...]))
            vec_ref[1:2, cols] = colsum(left.astype(F32))
            for copy in stores("up", j):
                copy.start()

    @pl.when(step == blocks + 2 * parts)
    def _():
        put(out, 0, dot_tn(ga_all[...], mixed[...]))
        for copy in stores("out", 0):
            copy.start()
        for kind, first, count in (("down", parts - 2, 2), ("up", parts - 2, 2), ("out", 0, 1)):
            for j in range(first, first + count):
                for copy in stores(kind, j):
                    copy.wait()


def joined_rows(refs, step):
    if len(refs) == 1:
        return refs[0][...].astype(F32)
    return jnp.where(step == 0, refs[0][...].astype(F32), refs[1][...].astype(F32))


def ff_all(gxs, slope, resid, active, n2, mixed, params, d, into, total, n_out):
    tokens, width = resid.shape
    ff = slope.shape[1]
    parts, blocks = ff // width, tokens // ROWS
    thin = width // 32
    early = lambda i: jnp.minimum(i, blocks - 1)
    row = lambda w: pl.BlockSpec((ROWS, w), lambda i: (early(i), 0))
    if len(gxs) == 1:
        x_specs = [row(width)]
    else:
        x_specs = [pl.BlockSpec((ROWS, width), lambda i: (0, 0), pipeline_mode=pl.Buffered(1))] * 2
    weights = [params[n] for n in ("wdown", "wup", "wout")]
    ops = [*gxs, slope, resid, params["gains"], active, *weights, n2, mixed]
    specs = x_specs + [
        row(ff),
        row(width),
        layer(params["gains"], d, 1),
        pl.BlockSpec((tokens, width), lambda i: (0, jnp.clip(i - blocks, 0, parts - 1))),
    ]
    extra = list(into or ())
    specs += anywhere(ops[len(specs) :]) + anywhere(extra)
    shape = jax.ShapeDtypeStruct((32 // n_out, total, width), BF)
    vec = pl.BlockSpec((8, ff), lambda i: (0, 0))
    vm = pltpu.VMEM
    scratch = [vm((ff, width), BF), vm((width, ff), BF), vm((width, width), BF)]
    scratch += [vm((tokens, width), BF)] * 3 + [vm((tokens, ff), BF), vm((tokens, width), BF)]
    scratch += [vm((2, 32, thin, width), BF), vm((2, 8, 4 * thin, width), BF), vm((1, 32, thin, width), BF)]
    scratch += [pltpu.SemaphoreType.DMA((2 * parts + 3,)), pltpu.SemaphoreType.DMA((12,))]
    flops = 2 * tokens * width * (4 * ff + 2 * width)
    return pl.pallas_call(
        functools.partial(ff_all_kernel, len(gxs), n_out, 0, d),
        grid=(blocks + 2 * parts + 1,),
        in_specs=specs,
        out_specs=[row(width), row(width), vec] + [pl.BlockSpec(memory_space=pl.ANY)] * n_out,
        out_shape=[sds(tokens, width, F32), sds(tokens, width, BF), sds(8, ff, F32)] + [shape] * n_out,
        input_output_aliases={len(ops) + n: 3 + n for n in range(len(extra))},
        scratch_shapes=scratch,
        compiler_params=pltpu.CompilerParams(
            vmem_limit_bytes=63 << 20, dimension_semantics=("arbitrary",)
        ),
        cost_estimate=cost(flops, 50 << 20),
        name="ff_all",
    )(*ops, *extra)


def vector_piece(square, long, owner):
    tall = long.shape[0] // 32
    thin = square.shape[0] // 32
    piece = long[owner * tall : (owner + 1) * tall]
    top = piece[:thin] + square[owner * thin : (owner + 1) * thin]
    piece = jnp.concatenate([top, piece[thin:]], 0)
    return jnp.concatenate([piece[16 * m : 16 * m + 16] for m in range(tall // 16)], 1)


def turned_vectors(found):
    width = found[0][0].shape[1] // 4
    rows, ups = [], []
    for proj_vec, ff_vec in found:
        p = [proj_vec[0:1, n * width : (n + 1) * width] for n in range(4)]
        f = [ff_vec[0:1, n * width : (n + 1) * width] for n in range(4)]
        rows += [p[0], f[0], p[1], f[1], p[2], p[3], f[3], f[2]]
        ups.append(ff_vec[1:2])
    square = jnp.concatenate(rows + [jnp.zeros((128 - len(rows), width), F32)], 0)
    before, after = len(rows), 128 - len(rows) - len(ups)
    zeros = lambda n: jnp.zeros((n, 4 * width), F32)
    long = jnp.concatenate([zeros(before)] + ups + [zeros(after)], 0)
    return square.T, long.T


def qkv_all_kernel(d, n_x, row0, *refs):
    it = iter(refs)
    g_hbm, n1_hbm, w_hbm, gres_hbm, gain_ref = [next(it) for _ in range(5)]
    x_hbm = [next(it) for _ in range(n_x)]
    others = [next(it) for _ in range(3 if n_x == 2 else 0)]
    n_g = 1 if n_x == 1 else 2
    outs = [next(it) for _ in range(n_g)]
    vec_ref, keep, send = next(it), next(it), next(it)
    g_all, n1, wqkv, gres, x_all, held, arrive, leave = [next(it) for _ in range(8)]
    gx_held = list(it)
    _, tokens, width = g_all.shape
    half = tokens // 2
    rows = 3 * width // 32
    core = lax.axis_index("dp") & 1
    pairs = [(g_hbm.at[0], g_all.at[0]), (n1_hbm, n1), (g_hbm.at[1], g_all.at[1])]
    pairs += [(g_hbm.at[2], g_all.at[2]), (w_hbm.at[d], wqkv), (gres_hbm, gres)]
    if n_x == 1:
        pairs.append((x_hbm[0], x_all))
    else:
        pairs += [(x_hbm[n], x_all.at[pl.ds(n * half, half)]) for n in range(2)]
    loads = [pltpu.make_async_copy(a, b, arrive.at[n]) for n, (a, b) in enumerate(pairs)]
    for copy in loads:
        copy.start()
    loads[0].wait()
    loads[1].wait()
    for n in range(3):
        if n:
            loads[n + 1].wait()
        left = g_all[n]
        result = dot_tn(left, n1[...])
        if n != 1:
            at = 2 * width if n == 0 else 3 * width
            vec_ref[0:1, at : at + width] = colsum(left.astype(F32))
        owner = n * width // rows
        while owner * rows < (n + 1) * width:
            low, high = max(owner * rows, n * width), min((owner + 1) * rows, (n + 1) * width)
            to = low - owner * rows
            held[(owner >> 1) & 1, chunk_of(owner), to : to + high - low, :] = result[
                low - n * width : high - n * width
            ].astype(BF)
            owner += 1
    tall = held.shape[2]
    stores = [
        pltpu.make_async_copy(
            held.at[core if n == 0 else 1 - core], buf.at[:, pl.ds(row0, tall)], leave.at[n]
        )
        for n, buf in enumerate((keep, send))
    ]
    if not others:
        for copy in stores:
            copy.start()
    for copy in loads[4:]:
        copy.wait()
    sums = []
    for n in (1, 0):
        part = slice(n * half, (n + 1) * half)
        g = jnp.concatenate([g_all[m, part, :] for m in range(3)], 1)
        g_norm = dot_nt(g, wqkv[...])
        xhat, rstd = normalize(x_all[part, :].astype(F32))
        gx = gres[part, :] + norm_back(g_norm, xhat, rstd, gain_ref[...])
        scratch = gx_held[n if n_g == 2 else 0]
        if n_g == 2:
            scratch[...] = gx.astype(scratch.dtype)
            copy = pltpu.make_async_copy(scratch, outs[n], leave.at[2 + n])
        else:
            scratch[part, :] = gx
            span = pl.ds(n * half, half)
            copy = pltpu.make_async_copy(scratch.at[span], outs[0].at[span], leave.at[2 + n])
        copy.start()
        stores.append(copy)
        sums.append((colsum(g_norm * xhat), colsum(g_norm)))
    vec_ref[0:1, :width] = sums[0][0] + sums[1][0]
    vec_ref[0:1, width : 2 * width] = sums[0][1] + sums[1][1]
    if others:
        square, long = turned_vectors([(vec_ref, others[0]), (others[1], others[2])])
        for owner in range(32):
            piece = vector_piece(square, long, owner).astype(BF)
            held[(owner >> 1) & 1, chunk_of(owner), rows:, :] = piece
        for copy in stores[:2]:
            copy.start()
    for copy in stores:
        copy.wait()


def qkv_all(grads, n1, xs, g_resid, params, d, total, row0, vecs=()):
    _, tokens, width = grads.shape
    half = tokens // 2
    rows = 3 * width // 32
    ops = [grads, n1, params["wqkv"], g_resid, params["gains"], *xs, *vecs]
    hbm = pl.BlockSpec(memory_space=pl.ANY)
    vec = pl.BlockSpec((8, 4 * width), lambda i: (0, 0))
    specs = [hbm] * 4 + [layer(params["gains"], d, 0)] + [hbm] * len(xs) + [vec] * len(vecs)
    vm = pltpu.VMEM
    if len(xs) == 1:
        g_outs, g_held = [sds(tokens, width, F32)], [vm((tokens, width), F32)]
    else:
        g_outs = [sds(half, width, F32), sds(half, width, BF)]
        g_held = [vm((half, width), F32), vm((half, width), BF)]
    buf = jax.ShapeDtypeStruct((16, total, width), BF)
    return pl.pallas_call(
        functools.partial(qkv_all_kernel, d, len(xs), row0),
        grid=(1,),
        in_specs=specs,
        out_specs=[hbm] * len(g_outs) + [vec, hbm, hbm],
        out_shape=g_outs + [sds(8, 4 * width, F32), buf, buf],
        scratch_shapes=[
            vm((3, tokens, width), BF),
            vm((tokens, width), BF),
            vm((width, 3 * width), BF),
            vm((tokens, width), F32),
            vm((tokens, width), xs[0].dtype),
            vm((2, 16, rows + (16 if vecs else 0), width), BF),
            pltpu.SemaphoreType.DMA((8,)),
            pltpu.SemaphoreType.DMA((4,)),
        ]
        + g_held,
        compiler_params=VMEM,
        cost_estimate=cost(1, 1),
        name="qkv_all",
    )(*ops)


def plus(*parts):
    total = parts[0].astype(F32)
    for part in parts[1:]:
        total = total + part.astype(F32)
    return total


def place_xy():
    return (lax.axis_index("dp") >> 1) & 1, lax.axis_index("blk")


def stage1_kernel(tall, keep, recv, kp, sp, kq, sq):
    x, y = place_xy()
    both = lambda a, b, rows: plus(keep[0, a, b, rows], recv[0, a, b, rows]).astype(BF)
    up, low = slice(0, tall), slice(tall, keep.shape[3])
    for n in range(2):
        kp[0, n] = both(x, n, up)
        sp[0, n] = both(1 - x, n, up)
        kq[0, n] = both(n, y, low)
        sq[0, n] = both(n, 1 - y, low)


def stage2_kernel(kp, rp, kq, rq, kp2, sp2, kq2, sq2):
    x, y = place_xy()
    kp2[0] = plus(kp[0, y], rp[0, y]).astype(BF)
    sp2[0] = plus(kp[0, 1 - y], rp[0, 1 - y]).astype(BF)
    kq2[0] = plus(kq[0, x], rq[0, x]).astype(BF)
    sq2[0] = plus(kq[0, 1 - x], rq[0, 1 - x]).astype(BF)


def stage3_kernel(kp, rp, kq, rq, own, *sends):
    tall = kp.shape[1]
    z = lax.axis_index("dp") >> 2
    for n, ref in enumerate((own,) + sends):
        at = z ^ n
        ref[:tall, :] = plus(kp[at], rp[at]).astype(ref.dtype)
        ref[tall:, :] = plus(kq[at], rq[at]).astype(ref.dtype)


def stage_call(kernel, name, ops, outs, deps):
    nbytes = sum(math.prod(a.shape) * 2 for a in ops) + sum(math.prod(s) * 2 for s in outs)
    spec = lambda shape: pl.BlockSpec((1,) + shape[1:], lambda i: (i,) + (0,) * (len(shape) - 1))
    return pl.pallas_call(
        ordered(kernel, len(ops), deps),
        grid=(ops[0].shape[0],),
        in_specs=[spec(a.shape) for a in ops] + anywhere(deps),
        out_specs=[spec(s) for s in outs],
        out_shape=[jax.ShapeDtypeStruct(s, BF) for s in outs],
        compiler_params=VMEM,
        cost_estimate=cost(nbytes, nbytes),
        name=name,
    )(*ops, *deps)


def xor_permute(x, dp, mask):
    return lax.ppermute(x, "dp", [(i, i ^ mask) for i in range(dp)])


class Group:
    def __init__(self, keep, send, tall, dp):
        self.tall, self.dp = tall, dp
        self.keep, self.recv = keep, xor_permute(send, dp, 1)

    def stage1(self, deps=()):
        _, total, width = self.keep.shape
        tall = self.tall
        cut = lambda a: a.reshape(4, 2, 2, total, width)
        ops = [cut(self.keep), cut(self.recv)]
        p, q = (4, 2, tall, width), (4, 2, total - tall, width)
        kernel = functools.partial(stage1_kernel, tall)
        self.kp, sp, self.kq, sq = stage_call(kernel, "stage1", ops, [p, p, q, q], deps)
        self.rp, self.rq = xor_permute(sp, self.dp, 2), swap_halves(sq)
        return [self.kp]

    def stage2(self, deps=()):
        p, q = [(4,) + a.shape[2:] for a in (self.kp, self.kq)]
        ops = [self.kp, self.rp, self.kq, self.rq]
        self.kp, sp, self.kq, sq = stage_call(stage2_kernel, "stage2", ops, [p, p, q, q], deps)
        self.rp, self.rq = swap_halves(sp), xor_permute(sq, self.dp, 2)
        return [self.kp]

    def stage3(self, deps=()):
        ops = [self.kp, self.rp, self.kq, self.rq]
        total, width = self.kp.shape[1] + self.kq.shape[1], self.kp.shape[2]
        nbytes = total * width * 24
        pieces = pl.pallas_call(
            ordered(stage3_kernel, 4, deps),
            grid=(1,),
            in_specs=[pl.BlockSpec(a.shape, lambda i: (0, 0, 0)) for a in ops] + anywhere(deps),
            out_specs=[pl.BlockSpec((total, width), lambda i: (0, 0))] * 4,
            out_shape=[sds(total, width, F32)] + [sds(total, width, BF)] * 3,
            compiler_params=VMEM,
            cost_estimate=cost(nbytes, nbytes),
            name="stage3",
        )(*ops, *deps)
        moved = [xor_permute(pieces[n], self.dp, n << 2) for n in range(1, 4)]
        self.pieces = [pieces[0]] + moved
        return [pieces[0]]


def final_kernel(layout, counts, *refs):
    groups = []
    for count in counts:
        groups.append(refs[:count])
        refs = refs[count:]
    outs = dict(zip(layout["outs"], refs))
    width = groups[0][0].shape[1]

    def rows(group, start, count):
        return plus(*(ref[start : start + count, :] for ref in groups[group]))

    for d in range(LAYERS):
        place = layout["rows"][d]
        for name in ("qkv", "out", "up"):
            outs[name][d] = rows(*place[name])
        down = rows(*place["down"])
        thin = outs["down"].shape[1]
        for j in range(down.shape[0] // thin):
            outs["down"][d, :, j * width : (j + 1) * width] = down[j * thin : (j + 1) * thin]
    vec = rows(*layout["vec"])
    lanes = [vec[:, 128 * m : 128 * m + 128] for m in range(width // 128)]
    lanes.append(jnp.zeros((128 - 16 * len(lanes), 128), F32))
    turned = jnp.concatenate(lanes, 0).T
    short = len(VECTORS) - 1
    for d in range(LAYERS):
        for at, (name, n) in enumerate(VECTORS):
            ref = outs[name]
            row = d * short + at if at < short else LAYERS * short + d
            value = turned[row : row + 1, : ref.shape[-1]]
            if n is None:
                ref[d : d + 1, :] = value
            else:
                ref[d, n : n + 1, :] = value


VECTORS = (
    ("gains", 0),
    ("gains", 1),
    ("shifts", 0),
    ("shifts", 1),
    ("bq", None),
    ("bv", None),
    ("bout", None),
    ("bdown", None),
    ("bup", None),
)


def finish(layout, groups, shapes):
    ops = [a for g in groups for a in g]
    names = list(shapes)
    layout = dict(layout, outs=names)
    total = sum(math.prod(a.shape) for a in ops) * 2
    return dict(
        zip(
            names,
            pl.pallas_call(
                functools.partial(final_kernel, layout, [len(g) for g in groups]),
                out_shape=[jax.ShapeDtypeStruct(shapes[n], F32) for n in names],
                compiler_params=pltpu.CompilerParams(vmem_limit_bytes=58 << 20),
                cost_estimate=cost(total, total),
                name="finish",
            )(*ops),
        )
    )


def swap_halves(x):
    return lax.ppermute(x, "blk", [(0, 1), (1, 0)])


class Halving:
    def __init__(self, mesh):
        self.dp = mesh.shape["dp"]
        self.blk = mesh.shape["blk"]
        self.bits = self.dp.bit_length() - 1
        assert self.blk == 2 and 1 << self.bits == self.dp

    def stages(self, blk_first):
        dp_bits = list(range(self.bits))
        rest = ["blk", 1] if blk_first else [1, "blk"]
        return [0] + rest + dp_bits[2:]

    def split(self, rows):
        owners = self.dp * self.blk
        return rows.reshape((2,) * (self.bits + 1) + (rows.shape[0] // owners, rows.shape[1]))

    def run(self, rows, blk_first, wide=False):
        arr = self.split(rows)
        names = list(reversed(range(self.bits))) + ["blk"]
        order = self.stages(blk_first)
        for n, stage in enumerate(order):
            dim = names.index(stage)
            names.pop(dim)
            if stage == "blk":
                mine = lax.axis_index("blk")
                send = lambda x: lax.ppermute(x, "blk", [(0, 1), (1, 0)])
            else:
                mine = (lax.axis_index("dp") >> stage) & 1
                perm = [(i, i ^ (1 << stage)) for i in range(self.dp)]
                send = lambda x: lax.ppermute(x, "dp", perm)
            keep = lax.dynamic_index_in_dim(arr, mine, dim, keepdims=False)
            other = lax.dynamic_index_in_dim(arr, 1 - mine, dim, keepdims=False)
            arr = keep.astype(F32) + send(other).astype(F32)
            if not wide and n + 1 < len(order):
                arr = arr.astype(BF)
        return arr


class PlainSums:
    def __init__(self, mesh):
        self.halving = Halving(mesh)
        self.held = {}

    def add(self, name, d, lefts, right, blk_first):
        self.held[name, d] = self.halving.run(plain_grad(lefts, right), blk_first)

    def results(self, vec):
        vec = self.halving.run(vec, False, wide=True)[0]
        out = {
            n: jnp.stack([self.held[n, d].T for d in range(LAYERS)])
            for n in ("qkv", "out", "up", "down")
        }
        thin = vec.shape[0] // (12 * LAYERS)
        at = 0
        found = {}
        for d in range(LAYERS):
            for name, n in VECTORS:
                size = 4 * thin if name == "bup" else thin
                found.setdefault((name, d), []).append(vec[at : at + size])
                at += size
        for name in dict(VECTORS):
            rows = [jnp.stack(found[name, d]) for d in range(LAYERS)]
            out[name] = jnp.stack(rows if len(rows[0]) == 2 else [r[0] for r in rows])
        return out


def shards(
    mesh,
    hidden_in,
    cell_lengths,
    cotangent,
    ln_gains,
    ln_biases,
    w_qkv,
    b_query,
    b_value,
    w_out,
    b_out,
    w_up,
    b_up,
    w_down,
    b_down,
):
    cells, half, width = hidden_in.shape
    tokens = cells * half
    dp, blk = mesh.shape["dp"], mesh.shape["blk"]
    owners = dp * blk
    assert cells == blk == 2
    side = lax.axis_index("blk")
    meta = cell_lengths
    grouped = dp == 16 and width == 768 and b_up.shape[1] == 4 * width

    def split_cell(both):
        own = lax.dynamic_index_in_dim(both, side, 0, False)
        other = lax.dynamic_index_in_dim(both, 1 - side, 0, False)
        return own, swap_halves(other)

    def return_cell(own, back):
        return jnp.where(side == 0, jnp.stack([own, back]), jnp.stack([back, own]))

    rows = lambda v: v[..., None, :]
    params = {
        "gains": rows(ln_gains),
        "shifts": rows(ln_biases),
        "wqkv": w_qkv,
        "bias": rows(jnp.concatenate([b_query, jnp.zeros_like(b_query), b_value], 1)),
        "wout": w_out,
        "bout": rows(b_out),
        "wup": w_up,
        "bup": rows(b_up),
        "wdown": w_down,
        "bdown": rows(b_down),
    }
    own, other = split_cell(hidden_in)
    entered = enter(own, params, 0, None, tokens, 0)
    n1, proj = enter(other, params, 0, entered, tokens, half)
    xs = (own, other)
    saved = []
    for d in range(LAYERS):
        mixed, low, lse = attn_fwd(proj, meta)
        last = d + 1 == LAYERS
        outs = post(mixed, xs, params, d, last)
        saved.append((xs, n1, proj, mixed, low, lse) + tuple(outs[:4]))
        if not last:
            x, n1, proj = outs[4:]
            xs = (x,)
    returned = swap_halves(outs[5])
    hidden_out = return_cell(outs[4], returned)

    gxs = split_cell(cotangent)
    backward = backward_grouped if grouped else backward_plain
    gx, out = backward(mesh, params, saved, gxs, meta, [returned])
    grad_in = return_cell(gx[0], gx[1].astype(F32))
    order = ("gains", "shifts", "qkv", "bq", "bv", "out", "bout", "up", "bup", "down", "bdown")
    return (hidden_out, grad_in) + tuple(out[n] for n in order)


def vector_rows(owners, width, ln1, ln2, sums):
    flat = []
    for d in range(LAYERS):
        for v in (
            ln1[d][:width],
            ln2[d][:width],
            ln1[d][width:],
            ln2[d][width:],
            sums["qkv", d][:width],
            sums["qkv", d][-width:],
            sums["out", d],
            sums["down", d],
            sums["up", d],
        ):
            flat.append(v.reshape(owners, -1))
    return jnp.concatenate(flat, 1)


def backward_plain(mesh, params, saved, gxs, meta, early):
    sums = PlainSums(mesh)
    ln1, ln2, cols = {}, {}, {}
    for d in reversed(range(LAYERS)):
        xs, n1, proj, mixed, low, lse, resid, n2, active, slope = saved[d]
        tokens, width = resid.shape
        gy, gu, g_resid, ga, g_mixed, vec2 = ff_back(gxs, slope, resid, params, d)
        sums.add("down", d, [gy], active, False)
        sums.add("up", d, [gu], n2, True)
        sums.add("out", d, [ga], mixed, False)
        grads = attn_bwd(proj, mixed, low, g_mixed, lse, meta, (0, width // 128))
        sums.add("qkv", d, [grads[n] for n in range(3)], n1, True)
        total = lambda a: jnp.sum(a.astype(F32), 0)
        cols.update({("down", d): total(gy), ("up", d): total(gu), ("out", d): total(ga)})
        cols["qkv", d] = jnp.concatenate([total(grads[n]) for n in range(3)])
        ln2[d] = vec2[0]
        if d > 0:
            gx, vec1 = qkv_back(grads, xs[0], g_resid, params, d, 0, tokens, F32)
            gxs = (gx,)
            ln1[d] = vec1[0]
        else:
            half = tokens // 2
            theirs, vec_a = qkv_back(grads, xs[1], g_resid, params, d, half, half, BF)
            mine, vec_b = qkv_back(grads, xs[0], g_resid, params, d, 0, half, F32)
            ln1[d] = vec_a[0] + vec_b[0]
    owners = mesh.shape["dp"] * mesh.shape["blk"]
    out = sums.results(vector_rows(owners, width, ln1, ln2, cols))
    return (mine, swap_halves(theirs)), out


def backward_grouped(mesh, params, saved, gxs, meta, early):
    dp = mesh.shape["dp"]
    width = saved[0][6].shape[1]
    t, pairs = width // 32, width // 128

    def ff_grads(gxs, d, into, total, n_out):
        mixed, resid, n2, active, slope = saved[d][3], *saved[d][6:]
        g_resid, g_mixed, vec, *bufs = ff_all(
            gxs, slope, resid, active, n2, mixed, params, d, into, total, n_out
        )
        return g_resid, g_mixed, vec, bufs

    xs, n1, proj, mixed, low, lse = saved[1][:6]
    g_resid, g_mixed, ff_vec1, bufs = ff_grads(gxs, 1, None, 9 * t, 1)
    layer1 = lax.psum_scatter(bufs[0], ("dp", "blk"), scatter_dimension=0, tiled=True)[0]
    grads = attn_bwd(proj, mixed, low, g_mixed, lse, meta, (0, pairs), None, bufs + early)
    gx, proj_vec1, *bufs = qkv_all(grads, n1, xs, g_resid, params, 1, 12 * t, 9 * t)
    xs, n1, proj, mixed, low, lse = saved[0][:6]
    g_resid, g_mixed, ff_vec0, bufs = ff_grads((gx,), 0, bufs, 12 * t, 2)
    ff0 = Group(*bufs, 6 * t, dp)
    grads = attn_bwd(proj, mixed, low, g_mixed, lse, meta, (0, 2), None, [ff0.keep])
    dep = ff0.stage1(deps=[grads])
    grads = attn_bwd(proj, mixed, low, g_mixed, lse, meta, (2, pairs), grads, dep)
    vecs = (ff_vec0, proj_vec1, ff_vec1)
    mine, theirs, _, *bufs = qkv_all(grads, n1, xs, g_resid, params, 0, 3 * t + 16, 0, vecs)
    dep = ff0.stage2(deps=[theirs])
    at0 = Group(bufs[0], after(bufs[1], dep), 48, dp)
    dep = at0.stage1(deps=dep)
    dep = ff0.stage3(deps=dep)
    dep = at0.stage2(deps=dep)
    dep = at0.stage3()
    back = swap_halves(after(theirs, dep))
    layout = {
        "rows": [
            {"down": (1, 0, 4 * t), "up": (1, 4 * t, 4 * t), "out": (1, 8 * t, t), "qkv": (2, 0, 3 * t)},
            {"down": (0, 0, 4 * t), "up": (0, 4 * t, 4 * t), "out": (0, 8 * t, t), "qkv": (1, 9 * t, 3 * t)},
        ],
        "vec": (2, 3 * t, 16),
    }
    shapes = {
        "qkv": (LAYERS, 3 * t, width),
        "out": (LAYERS, t, width),
        "up": (LAYERS, 4 * t, width),
        "down": (LAYERS, t, 4 * width),
        "gains": (LAYERS, 2, t),
        "shifts": (LAYERS, 2, t),
        "bq": (LAYERS, t),
        "bv": (LAYERS, t),
        "bout": (LAYERS, t),
        "bdown": (LAYERS, t),
        "bup": (LAYERS, 4 * t),
    }
    out = finish(layout, [[layer1], ff0.pieces, at0.pieces], shapes)
    for name in ("qkv", "out", "up", "down"):
        out[name] = jnp.swapaxes(out[name], 1, 2)
    return (mine, back), out


def solution(mesh):
    both = ("dp", "blk")
    row = P("dp", "blk", None)
    last3 = P(None, None, both)
    last2 = P(None, both)
    return jax.shard_map(
        functools.partial(shards, mesh),
        mesh=mesh,
        in_specs=(row, P("dp"), row) + (P(),) * 11,
        out_specs=(
            row,
            row,
            last3,
            last3,
            last3,
            last2,
            last2,
            last3,
            last2,
            last3,
            last2,
            last3,
            last2,
        ),
        check_vma=False,
    )
```

```python
import functools
import math

import jax
import jax.numpy as jnp
from jax import lax
from jax.experimental import pallas as pl
from jax.experimental.pallas import tpu as pltpu
from jax.sharding import PartitionSpec as P

HEAD_DIM = 64
LAYERS = 2
EPSILON = 1e-05
NEG = -1e30
BF = jnp.bfloat16
F32 = jnp.float32
QSCALE = math.log2(math.e) / math.sqrt(HEAD_DIM)


def dot_nn(a, b):
    return lax.dot_general(a, b, (((1,), (0,)), ((), ())), preferred_element_type=F32)


def dot_nt(a, b):
    return lax.dot_general(a, b, (((1,), (1,)), ((), ())), preferred_element_type=F32)


def dot_tn(a, b):
    return lax.dot_general(a, b, (((0,), (0,)), ((), ())), preferred_element_type=F32)


def mask_block(meta_ref, kaug, qone, tokens):
    side = lax.axis_index("blk")
    rows = lax.broadcasted_iota(jnp.int32, (tokens, 128), 0)
    lanes = lax.broadcasted_iota(jnp.int32, (tokens, 128), 1)
    half = tokens // 2
    position = jnp.where(rows < half, rows + side * half, rows - side * half)
    masked = jnp.logical_and(lanes == 0, position >= meta_ref[side])
    kaug[...] = jnp.where(masked, NEG, 0.0).astype(BF)
    qone[...] = jnp.where(lanes == 0, 1.0, 0.0).astype(BF)


def attn_fwd_kernel(
    chunk, ahead, meta_ref, q_ref, k_ref, v_ref, o_ref, low_ref, lse_ref, kaug, qone
):
    tokens = q_ref.shape[0]

    @pl.when(pl.program_id(0) == 0)
    def _():
        mask_block(meta_ref, kaug, qone, tokens)

    first = lax.broadcasted_iota(jnp.int32, (tokens, 128), 1) < HEAD_DIM
    q, k, v = q_ref[...], k_ref[...], v_ref[...]
    zero = jnp.zeros_like(k)
    sel = [first, jnp.logical_not(first)]
    keys = [jnp.concatenate([jnp.where(sel[h], k, zero), kaug[...]], 1) for h in range(2)]
    vals = [jnp.where(sel[h], v, zero).T for h in range(2)]
    qa = jnp.concatenate([q, qone[...]], 1)
    units = [(c, h) for c in range(tokens // chunk) for h in range(2)]
    ready = {}

    def scores(unit):
        c, h = unit
        ready[unit] = dot_nt(keys[h], qa[c * chunk : (c + 1) * chunk])

    for unit in units[:ahead]:
        scores(unit)
    kept = {}
    for n, unit in enumerate(units):
        if n + ahead < len(units):
            scores(units[n + ahead])
        c, h = unit
        cols = slice(c * chunk, (c + 1) * chunk)
        st = ready.pop(unit)
        top = jnp.max(st, axis=0, keepdims=True)
        p = jnp.exp2(st - top)
        p = p.astype(BF)
        total = jnp.sum(p.astype(F32), axis=0, keepdims=True)
        kept[h] = (dot_nn(vals[h], p), top, total)
        if h == 1:
            head = lax.broadcasted_iota(jnp.int32, (128, chunk), 0) < HEAD_DIM
            inv = jnp.where(head, 1.0 / kept[0][2], 1.0 / kept[1][2])
            out = ((kept[0][0] + kept[1][0]) * inv).T
            high = out.astype(BF)
            o_ref[cols, :] = high
            low_ref[cols, :] = (out - high.astype(F32)).astype(BF)
            for g in range(2):
                lse_ref[0, g : g + 1, cols] = kept[g][1] + jnp.log2(kept[g][2])


def attn_fwd(proj, meta):
    tokens, width = proj.shape[0], proj.shape[1] // 3
    pairs = width // 128
    spec = lambda off: pl.BlockSpec((tokens, 128), lambda i, m: (0, off + i))
    return pl.pallas_call(
        functools.partial(attn_fwd_kernel, tokens // 2, 2),
        grid_spec=pltpu.PrefetchScalarGridSpec(
            num_scalar_prefetch=1,
            grid=(pairs,),
            in_specs=[spec(0), spec(pairs), spec(2 * pairs)],
            out_specs=[spec(0), spec(0), pl.BlockSpec((1, 8, tokens), lambda i, m: (i, 0, 0))],
            scratch_shapes=[pltpu.VMEM((tokens, 128), BF), pltpu.VMEM((tokens, 128), BF)],
        ),
        out_shape=[
            jax.ShapeDtypeStruct((tokens, width), BF),
            jax.ShapeDtypeStruct((tokens, width), BF),
            jax.ShapeDtypeStruct((pairs, 8, tokens), F32),
        ],
        compiler_params=pltpu.CompilerParams(
            vmem_limit_bytes=56 << 20, dimension_semantics=("arbitrary",)
        ),
        cost_estimate=pl.CostEstimate(
            flops=4 * tokens * tokens * width * 3,
            bytes_accessed=tokens * width * 8,
            transcendentals=pairs * 2 * tokens * tokens,
        ),
        name="attn_fwd",
    )(meta, proj, proj, proj)


def attn_bwd_kernel(
    meta_ref, q_ref, k_ref, v_ref, o_ref, low_ref, do_ref, lse_ref, out_ref, kaug, qone
):
    tokens = q_ref.shape[0]

    @pl.when(pl.program_id(0) == 0)
    def _():
        mask_block(meta_ref, kaug, qone, tokens)

    first = lax.broadcasted_iota(jnp.int32, (tokens, 128), 1) < HEAD_DIM
    q, k, v, do = q_ref[...], k_ref[...], v_ref[...], do_ref[...]
    zero = jnp.zeros_like(k)
    sel = [first, jnp.logical_not(first)]
    qa = jnp.concatenate([q, qone[...]], 1)
    prod = ((o_ref[...].astype(F32) + low_ref[...].astype(F32)) * do.astype(F32)).T
    dq = dk = dv = None
    for h in range(2):
        kh = jnp.where(sel[h], k, zero)
        delta = jnp.sum(prod[h * HEAD_DIM : (h + 1) * HEAD_DIM], 0, keepdims=True)
        st = dot_nt(jnp.concatenate([kh, kaug[...]], 1), qa)
        dpt = dot_nt(jnp.where(sel[h], v, zero), do)
        p = jnp.exp2(st - lse_ref[0, h : h + 1, :])
        ds = (p * (dpt - delta)).astype(BF)
        dvh = dot_nn(p.astype(BF), jnp.where(sel[h], do, zero))
        dkh = dot_nn(ds, jnp.where(sel[h], q, zero))
        dqh = dot_nn(kh.T, ds)
        dq, dk, dv = (dqh, dkh, dvh) if h == 0 else (dq + dqh, dk + dkh, dv + dvh)
    out_ref[0] = (dq * (1.0 / math.sqrt(HEAD_DIM))).T.astype(BF)
    out_ref[1] = (dk * math.log(2.0)).astype(BF)
    out_ref[2] = dv.astype(BF)


def attn_bwd(proj, mixed, low, g_mixed, lse, meta, pairs, into=None, deps=()):
    tokens, width = mixed.shape
    count = width // 128
    start, stop = pairs
    spec = lambda off: pl.BlockSpec((tokens, 128), lambda i, m: (0, off + start + i))
    ops = [meta, proj, proj, proj, mixed, low, g_mixed, lse]
    specs = [spec(0), spec(count), spec(2 * count), spec(0), spec(0), spec(0)]
    specs += [pl.BlockSpec((1, 8, tokens), lambda i, m: (start + i, 0, 0))]
    extra = ([] if into is None else [into]) + list(deps)
    return pl.pallas_call(
        ordered(attn_bwd_kernel, len(ops), extra),
        grid_spec=pltpu.PrefetchScalarGridSpec(
            num_scalar_prefetch=1,
            grid=(stop - start,),
            in_specs=specs + anywhere(extra),
            out_specs=pl.BlockSpec((3, tokens, 128), lambda i, m: (0, 0, start + i)),
            scratch_shapes=[pltpu.VMEM((tokens, 128), BF), pltpu.VMEM((tokens, 128), BF)],
        ),
        out_shape=jax.ShapeDtypeStruct((3, tokens, width), BF),
        input_output_aliases={} if into is None else {len(ops): 0},
        compiler_params=pltpu.CompilerParams(
            vmem_limit_bytes=56 << 20, dimension_semantics=("arbitrary",)
        ),
        cost_estimate=cost(1, 1),
        name="attn_bwd",
    )(*ops, *extra)


VMEM = pltpu.CompilerParams(vmem_limit_bytes=58 << 20, dimension_semantics=("arbitrary",))
SMALL = pltpu.CompilerParams(vmem_limit_bytes=20 << 20)


def ordered(kernel, n_in, deps):
    if not deps:
        return kernel
    return lambda *refs: kernel(*refs[:n_in], *refs[n_in + len(deps) :])


def after(array, deps):
    return lax.optimization_barrier((array, *deps))[0]


def anywhere(arrays):
    return [pl.BlockSpec(memory_space=pl.ANY)] * len(arrays)


def layer(arr, d, n=0):
    lead = arr.ndim - 2
    index = (d, n)[:lead] + (0, 0)
    return pl.BlockSpec(
        (None,) * lead + arr.shape[lead:], lambda *_: index, pipeline_mode=pl.Buffered(1)
    )


def tile(rows, width, first=0):
    return pl.BlockSpec((rows, width), lambda i, *_: (first + i, 0))


def sds(rows, width, dtype):
    return jax.ShapeDtypeStruct((rows, width), dtype)


def cost(flops, nbytes, trans=0):
    return pl.CostEstimate(flops=int(flops), bytes_accessed=int(nbytes), transcendentals=int(trans))


def normalize(x):
    mean = jnp.mean(x, -1, keepdims=True)
    centered = x - mean
    variance = jnp.mean(centered * centered, -1, keepdims=True)
    rstd = lax.rsqrt(variance + EPSILON)
    return centered * rstd, rstd


def project(n1, wqkv_ref, bias_ref, proj_ref, width):
    for j, factor in enumerate((QSCALE, 1.0, 1.0)):
        cols = slice(j * width, (j + 1) * width)
        part = dot_nn(n1, wqkv_ref[:, cols]) + bias_ref[:, cols]
        proj_ref[:, cols] = (part * factor).astype(BF)


def attn_in(params, d):
    arrays = [params["gains"], params["shifts"], params["wqkv"], params["bias"]]
    return arrays, [layer(arrays[0], d, 0), layer(arrays[1], d, 0), layer(arrays[2], d), layer(arrays[3], d)]


def enter_kernel(x_ref, gain_ref, shift_ref, wqkv_ref, bias_ref, *refs):
    n1_ref, proj_ref = refs[-2:]
    width = x_ref.shape[1]
    xhat, _ = normalize(x_ref[...].astype(F32))
    n1 = (xhat * gain_ref[...] + shift_ref[...]).astype(BF)
    n1_ref[...] = n1
    project(n1, wqkv_ref, bias_ref, proj_ref, width)


def enter(x, params, d, into, tokens, first):
    rows, width = x.shape
    block = 256
    at = first // block
    arrays, specs = attn_in(params, d)
    ops = [x] + arrays
    specs = [tile(block, width)] + specs
    alias = {}
    if into is not None:
        ops += list(into)
        specs += [pl.BlockSpec(memory_space=pl.ANY)] * 2
        alias = {5: 0, 6: 1}
    return pl.pallas_call(
        enter_kernel,
        grid=(rows // block,),
        in_specs=specs,
        out_specs=[tile(block, width, at), tile(block, 3 * width, at)],
        out_shape=[sds(tokens, width, BF), sds(tokens, 3 * width, BF)],
        input_output_aliases=alias,
        compiler_params=SMALL,
        cost_estimate=cost(6 * rows * width * width, rows * width * 10 + 6 * width * width),
        name="enter",
    )(*ops)


def halves(tokens, block, width):
    turn = tokens // block // 2
    own = pl.BlockSpec((block, width), lambda i, *_: (jnp.minimum(i, turn - 1), 0))
    other = pl.BlockSpec((block, width), lambda i, *_: (jnp.maximum(i - turn, 0), 0))
    return [own, other]


def joined(refs):
    if len(refs) == 1:
        return refs[0][...].astype(F32)
    early = pl.program_id(0) < pl.num_programs(0) // 2
    return jnp.where(early, refs[0][...].astype(F32), refs[1][...].astype(F32))


def post_kernel(d, last, parts, n_x, *refs):
    it = iter(refs)
    mixed_ref = next(it)
    x_refs = [next(it) for _ in range(n_x)]
    bout_ref, gain_ref, shift_ref, bup_ref, bdown_ref = [next(it) for _ in range(5)]
    if not last:
        gain1_ref, shift1_ref, bias_ref = next(it), next(it), next(it)
    sources = [next(it) for _ in range(3 if last else 4)]
    resid_ref, n2_ref, active_ref, slope_ref = next(it), next(it), next(it), next(it)
    outs = [next(it) for _ in range(2 if last else 3)]
    wout, wup, wdown = next(it), next(it), next(it)
    wqkv = None if last else next(it)
    arrive = next(it)
    step = pl.program_id(0)
    width = mixed_ref.shape[1]
    hidden = wup.shape[1] // parts

    def load(n):
        part = pl.ds((n - 1) // 2 * hidden, hidden)
        if n == 0:
            pair = sources[0].at[d], wout
        elif n > 2 * parts:
            pair = sources[3].at[d + 1], wqkv
        elif n % 2:
            pair = sources[1].at[d, :, part], wup.at[:, part]
        else:
            pair = sources[2].at[d, part], wdown.at[part]
        return pltpu.make_async_copy(*pair, arrive.at[n])

    @pl.when(step == 0)
    def _():
        for n in range(2 * parts + (1 if last else 2)):
            load(n).start()

    def body(wait):
        wait(0)
        resid = joined(x_refs) + dot_nn(mixed_ref[...], wout[...]) + bout_ref[...]
        resid_ref[...] = resid
        xhat, _ = normalize(resid)
        n2 = (xhat * gain_ref[...] + shift_ref[...]).astype(BF)
        n2_ref[...] = n2
        total = resid + bdown_ref[...]
        for j in range(parts):
            cols = slice(j * hidden, (j + 1) * hidden)
            wait(2 * j + 1)
            upper = dot_nn(n2, wup[:, cols]) + bup_ref[:, cols]
            cdf = 0.5 + 0.5 * lax.erf(upper * math.sqrt(0.5))
            dens = jnp.exp2(upper * upper * (-0.5 * math.log2(math.e))) * (1.0 / math.sqrt(2.0 * math.pi))
            active = (upper * cdf).astype(BF)
            active_ref[:, cols] = active
            slope_ref[:, cols] = (cdf + upper * dens).astype(BF)
            wait(2 * j + 2)
            total = total + dot_nn(active, wdown[cols, :])
        if last:
            for n, ref in enumerate(outs):

                @pl.when(step // (pl.num_programs(0) // 2) == n)
                def _():
                    ref[...] = total.astype(BF)
        else:
            x_out, n1_ref, proj_ref = outs
            x_out[...] = total
            xhat, _ = normalize(total)
            n1 = (xhat * gain1_ref[...] + shift1_ref[...]).astype(BF)
            n1_ref[...] = n1
            wait(2 * parts + 1)
            project(n1, wqkv, bias_ref, proj_ref, width)

    pl.when(step == 0)(lambda: body(lambda n: load(n).wait()))
    pl.when(step > 0)(lambda: body(lambda n: None))


def post(mixed, xs, params, d, last):
    tokens, width = mixed.shape
    block = 256
    parts = 4
    ff = params["wup"].shape[2]
    small = [(params[n], d) for n in ("bout", "gains", "shifts", "bup", "bdown")]
    specs = [layer(a, e, 1) for a, e in small]
    weights = ["wout", "wup", "wdown"]
    if not last:
        more = [(params[n], d + 1) for n in ("gains", "shifts", "bias")]
        specs += [layer(a, e, 0) for a, e in more]
        small += more
        weights.append("wqkv")
    arrays = [a for a, _ in small] + [params[n] for n in weights]
    ops = [mixed] + list(xs) + arrays
    x_specs = [tile(block, width)] if len(xs) == 1 else halves(tokens, block, width)
    outs = [(tokens, width, F32), (tokens, width, BF), (tokens, ff, BF), (tokens, ff, BF)]
    out_specs = [tile(block, w) for _, w, _ in outs]
    if last:
        outs += [(tokens // 2, width, BF)] * 2
        out_specs += halves(tokens, block, width)
    else:
        outs += [(tokens, width, F32), (tokens, width, BF), (tokens, 3 * width, BF)]
        out_specs += [tile(block, w) for _, w, _ in outs[4:]]
    flops = 2 * tokens * width * (width + 2 * ff + (0 if last else 3 * width))
    return pl.pallas_call(
        functools.partial(post_kernel, d, last, parts, len(xs)),
        grid=(tokens // block,),
        in_specs=[tile(block, width)] + x_specs + specs + anywhere(weights),
        out_specs=out_specs,
        out_shape=[sds(*o) for o in outs],
        scratch_shapes=[pltpu.VMEM(params[n].shape[1:], BF) for n in weights]
        + [pltpu.SemaphoreType.DMA((2 * parts + 2,))],
        compiler_params=VMEM,
        cost_estimate=cost(flops, tokens * ff * 10, 2 * tokens * ff),
        name="post",
    )(*ops)


def norm_back(g_normed, xhat, rstd, gain):
    scaled = g_normed * gain
    mean1 = jnp.mean(scaled, -1, keepdims=True)
    mean2 = jnp.mean(scaled * xhat, -1, keepdims=True)
    return rstd * (scaled - mean1 - xhat * mean2)


def add_row(ref, row, start, value, fresh):
    cols = slice(start, start + value.shape[1])

    @pl.when(fresh)
    def _():
        ref[row : row + 1, cols] = value

    @pl.when(jnp.logical_not(fresh))
    def _():
        ref[row : row + 1, cols] += value


def colsum(x):
    return jnp.sum(x, 0, keepdims=True)


def ff_back_kernel(parts, n_x, *refs):
    gx_refs = refs[:n_x]
    slope_ref, resid_ref, wdown_ref, wup_ref, wout_ref, gain_ref = refs[n_x : n_x + 6]
    gy_ref, gu_ref, gres_ref, ga_ref, gmix_ref, vec_ref = refs[n_x + 6 :]
    fresh = pl.program_id(0) == 0
    width = resid_ref.shape[1]
    gx = joined(gx_refs)
    gy = gx.astype(BF)
    gy_ref[...] = gy
    hidden = wup_ref.shape[1] // parts
    g_n2 = None
    for j in range(parts):
        cols = slice(j * hidden, (j + 1) * hidden)
        g_act = dot_nt(gy, wdown_ref[cols, :])
        gu = (g_act * slope_ref[:, cols].astype(F32)).astype(BF)
        gu_ref[:, cols] = gu
        part = dot_nt(gu, wup_ref[:, cols])
        g_n2 = part if g_n2 is None else g_n2 + part
    xhat, rstd = normalize(resid_ref[...])
    g_resid = gx + norm_back(g_n2, xhat, rstd, gain_ref[...])
    gres_ref[...] = g_resid
    ga = g_resid.astype(BF)
    ga_ref[...] = ga
    gmix_ref[...] = dot_nt(ga, wout_ref[...]).astype(BF)
    add_row(vec_ref, 0, 0, colsum(g_n2 * xhat), fresh)
    add_row(vec_ref, 0, width, colsum(g_n2), fresh)


def ff_back(gxs, slope, resid, params, d, deps=()):
    tokens, width = resid.shape
    ff = slope.shape[1]
    block = 512
    outs = [(width, BF), (ff, BF), (width, F32), (width, BF), (width, BF)]
    assert ff == 4 * width
    x_specs = [tile(block, width)] if len(gxs) == 1 else halves(tokens, block, width)
    arrays = [params[n] for n in ("wdown", "wup", "wout", "gains")]
    return pl.pallas_call(
        ordered(functools.partial(ff_back_kernel, 4, len(gxs)), len(gxs) + 6, deps),
        grid=(tokens // block,),
        in_specs=x_specs
        + [tile(block, ff), tile(block, width)]
        + [layer(a, d, 1) for a in arrays]
        + anywhere(deps),
        out_specs=[tile(block, w) for w, _ in outs] + [pl.BlockSpec((8, 2 * width), lambda i: (0, 0))],
        out_shape=[sds(tokens, w, t) for w, t in outs] + [sds(8, 2 * width, F32)],
        compiler_params=VMEM,
        cost_estimate=cost(2 * tokens * width * (2 * ff + width), tokens * ff * 8),
        name="ff_back",
    )(*gxs, slope, resid, *arrays, *deps)


def qkv_back_kernel(grads_ref, wqkv_ref, x_ref, gres_ref, gain_ref, *refs):
    gx_ref, vec_ref = refs[-2:]
    fresh = pl.program_id(0) == 0
    width = x_ref.shape[1]
    grads = [grads_ref[n] for n in range(3)]
    g_norm = dot_nt(jnp.concatenate(grads, 1), wqkv_ref[...])
    xhat, rstd = normalize(x_ref[...].astype(F32))
    gx = gres_ref[...] + norm_back(g_norm, xhat, rstd, gain_ref[...])
    gx_ref[...] = gx.astype(gx_ref.dtype)
    add_row(vec_ref, 0, 0, colsum(g_norm * xhat), fresh)
    add_row(vec_ref, 0, width, colsum(g_norm), fresh)


def qkv_back(grads, x, g_resid, params, d, first, rows, dtype, deps=()):
    width = x.shape[1]
    block = 256
    at = first // block
    return pl.pallas_call(
        ordered(qkv_back_kernel, 5, deps),
        grid=(rows // block,),
        in_specs=[
            pl.BlockSpec((3, block, width), lambda i: (0, at + i, 0)),
            layer(params["wqkv"], d),
            tile(block, width),
            tile(block, width, at),
            layer(params["gains"], d, 0),
            *anywhere(deps),
        ],
        out_specs=[tile(block, width), pl.BlockSpec((8, 2 * width), lambda i: (0, 0))],
        out_shape=[sds(rows, width, dtype), sds(8, 2 * width, F32)],
        compiler_params=VMEM,
        cost_estimate=cost(6 * rows * width * width, rows * width * 20),
        name="qkv_back",
    )(grads, params["wqkv"], x, g_resid, params["gains"], *deps)


def plain_grad(lefts, right):
    return jnp.concatenate([dot_tn(left, right) for left in lefts], 0).astype(BF)


def chunk_of(owner):
    return (owner >> 2) * 2 + (owner & 1)


ROWS = 512


def ff_all_kernel(n_x, n_out, firsts, d, *refs):
    it = iter(refs)
    gx_refs = [next(it) for _ in range(n_x)]
    slope_ref, resid_ref, gain_ref, active_ref = next(it), next(it), next(it), next(it)
    sources = [next(it) for _ in range(5)]
    refs = list(it)
    gres_ref, gmix_ref, vec_ref = refs[-16 - n_out : -13 - n_out]
    bufs = refs[-13 - n_out : -13]
    wdown, wup, wout, n2, mixed, gy_all, gu_all, ga_all, down, up, out, arrive, leave = refs[-13:]
    step = pl.program_id(0)
    tokens, width = gy_all.shape
    parts = wup.shape[1] // width
    blocks = tokens // ROWS
    thin = width // 32
    core = lax.axis_index("dp") & 1

    def load(n):
        j = n // 2
        rows = pl.ds(j * width, width)
        if j < parts and n % 2 == 0:
            pair = sources[0].at[d, rows], wdown.at[rows]
        elif j < parts:
            pair = sources[1].at[d, :, rows], wup.at[:, rows]
        else:
            late = n - 2 * parts
            pair = (sources[2].at[d], sources[3], sources[4])[late], (wout, n2, mixed)[late]
        return pltpu.make_async_copy(*pair, arrive.at[n])

    @pl.when(step == 0)
    def _():
        for n in range(2 * parts + 3):
            load(n).start()

    def stores(kind, j):
        slot = j % 2
        if kind == "up":
            held, row, count, tall, place = up, firsts + 4 * thin, 8, 4 * thin, 8 * j
        else:
            held = down if kind == "down" else out
            row, count, tall, place = firsts + (j if kind == "down" else 8) * thin, 32, thin, 0
        sem = {"down": 0, "up": 4, "out": 8}[kind] + 2 * slot
        rows = pl.ds(row, tall)
        if n_out == 1:
            dst = bufs[0].at[pl.ds(place, count), rows]
            return [pltpu.make_async_copy(held.at[slot], dst, leave.at[sem])]
        part = count // 2
        found = []
        for n, buf in enumerate(bufs):
            src = held.at[slot, pl.ds((core if n == 0 else 1 - core) * part, part)]
            dst = buf.at[pl.ds(place // 2, part), rows]
            found.append(pltpu.make_async_copy(src, dst, leave.at[sem + n]))
        return found

    def put(held, slot, result):
        count, tall = held.shape[1], held.shape[2]
        for owner in range(count):
            at = owner if n_out == 1 else ((owner >> 1) & 1) * (count // 2) + chunk_of(owner)
            held[slot, at] = result[owner * tall : (owner + 1) * tall].astype(BF)

    def body(wait):
        rows = pl.ds(pl.multiple_of(step * ROWS, ROWS), ROWS)
        fresh = step == 0
        gx = joined_rows(gx_refs, step)
        gy = gx.astype(BF)
        gy_all[rows, :] = gy
        g_n2 = None
        for j in range(parts):
            cols = slice(j * width, (j + 1) * width)
            wait(2 * j)
            g_act = dot_nt(gy, wdown[cols, :])
            gu = (g_act * slope_ref[:, cols].astype(F32)).astype(BF)
            gu_all[rows, cols] = gu
            wait(2 * j + 1)
            part = dot_nt(gu, wup[:, cols])
            g_n2 = part if g_n2 is None else g_n2 + part
        xhat, rstd = normalize(resid_ref[...])
        g_resid = gx + norm_back(g_n2, xhat, rstd, gain_ref[...])
        gres_ref[...] = g_resid
        ga = g_resid.astype(BF)
        ga_all[rows, :] = ga
        wait(2 * parts)
        gmix_ref[...] = dot_nt(ga, wout[...]).astype(BF)
        add_row(vec_ref, 0, 0, colsum(g_n2 * xhat), fresh)
        add_row(vec_ref, 0, width, colsum(g_n2), fresh)
        add_row(vec_ref, 0, 2 * width, colsum(gy.astype(F32)), fresh)
        add_row(vec_ref, 0, 3 * width, colsum(ga.astype(F32)), fresh)

    pl.when(step == 0)(lambda: body(lambda n: load(n).wait()))
    pl.when(jnp.logical_and(step > 0, step < blocks))(lambda: body(lambda n: None))

    @pl.when(step == blocks)
    def _():
        load(2 * parts + 1).wait()
        load(2 * parts + 2).wait()

    for j in range(parts):

        @pl.when(step == blocks + j)
        def _():
            if j >= 2:
                for copy in stores("down", j - 2):
                    copy.wait()
            put(down, j % 2, dot_tn(gy_all[...], active_ref[...]))
            for copy in stores("down", j):
                copy.start()

        @pl.when(step == blocks + parts + j)
        def _():
            if j >= 2:
                for copy in stores("up", j - 2):
                    copy.wait()
            cols = slice(j * width, (j + 1) * width)
            left = gu_all[:, cols]
            put(up, j % 2, dot_tn(left, n2[...]))
            vec_ref[1:2, cols] = colsum(left.astype(F32))
            for copy in stores("up", j):
                copy.start()

    @pl.when(step == blocks + 2 * parts)
    def _():
        put(out, 0, dot_tn(ga_all[...], mixed[...]))
        for copy in stores("out", 0):
            copy.start()
        for kind, first, count in (("down", parts - 2, 2), ("up", parts - 2, 2), ("out", 0, 1)):
            for j in range(first, first + count):
                for copy in stores(kind, j):
                    copy.wait()


def joined_rows(refs, step):
    if len(refs) == 1:
        return refs[0][...].astype(F32)
    return jnp.where(step == 0, refs[0][...].astype(F32), refs[1][...].astype(F32))


def ff_all(gxs, slope, resid, active, n2, mixed, params, d, into, total, n_out):
    tokens, width = resid.shape
    ff = slope.shape[1]
    parts, blocks = ff // width, tokens // ROWS
    thin = width // 32
    early = lambda i: jnp.minimum(i, blocks - 1)
    row = lambda w: pl.BlockSpec((ROWS, w), lambda i: (early(i), 0))
    if len(gxs) == 1:
        x_specs = [row(width)]
    else:
        x_specs = [pl.BlockSpec((ROWS, width), lambda i: (0, 0), pipeline_mode=pl.Buffered(1))] * 2
    weights = [params[n] for n in ("wdown", "wup", "wout")]
    ops = [*gxs, slope, resid, params["gains"], active, *weights, n2, mixed]
    specs = x_specs + [
        row(ff),
        row(width),
        layer(params["gains"], d, 1),
        pl.BlockSpec((tokens, width), lambda i: (0, jnp.clip(i - blocks, 0, parts - 1))),
    ]
    extra = list(into or ())
    specs += anywhere(ops[len(specs) :]) + anywhere(extra)
    shape = jax.ShapeDtypeStruct((32 // n_out, total, width), BF)
    vec = pl.BlockSpec((8, ff), lambda i: (0, 0))
    vm = pltpu.VMEM
    scratch = [vm((ff, width), BF), vm((width, ff), BF), vm((width, width), BF)]
    scratch += [vm((tokens, width), BF)] * 3 + [vm((tokens, ff), BF), vm((tokens, width), BF)]
    scratch += [vm((2, 32, thin, width), BF), vm((2, 8, 4 * thin, width), BF), vm((1, 32, thin, width), BF)]
    scratch += [pltpu.SemaphoreType.DMA((2 * parts + 3,)), pltpu.SemaphoreType.DMA((12,))]
    flops = 2 * tokens * width * (4 * ff + 2 * width)
    return pl.pallas_call(
        functools.partial(ff_all_kernel, len(gxs), n_out, 0, d),
        grid=(blocks + 2 * parts + 1,),
        in_specs=specs,
        out_specs=[row(width), row(width), vec] + [pl.BlockSpec(memory_space=pl.ANY)] * n_out,
        out_shape=[sds(tokens, width, F32), sds(tokens, width, BF), sds(8, ff, F32)] + [shape] * n_out,
        input_output_aliases={len(ops) + n: 3 + n for n in range(len(extra))},
        scratch_shapes=scratch,
        compiler_params=pltpu.CompilerParams(
            vmem_limit_bytes=63 << 20, dimension_semantics=("arbitrary",)
        ),
        cost_estimate=cost(flops, 50 << 20),
        name="ff_all",
    )(*ops, *extra)


def vector_piece(square, long, owner):
    tall = long.shape[0] // 32
    thin = square.shape[0] // 32
    piece = long[owner * tall : (owner + 1) * tall]
    top = piece[:thin] + square[owner * thin : (owner + 1) * thin]
    piece = jnp.concatenate([top, piece[thin:]], 0)
    return jnp.concatenate([piece[16 * m : 16 * m + 16] for m in range(tall // 16)], 1)


def turned_vectors(found):
    width = found[0][0].shape[1] // 4
    rows, ups = [], []
    for proj_vec, ff_vec in found:
        p = [proj_vec[0:1, n * width : (n + 1) * width] for n in range(4)]
        f = [ff_vec[0:1, n * width : (n + 1) * width] for n in range(4)]
        rows += [p[0], f[0], p[1], f[1], p[2], p[3], f[3], f[2]]
        ups.append(ff_vec[1:2])
    square = jnp.concatenate(rows + [jnp.zeros((128 - len(rows), width), F32)], 0)
    before, after = len(rows), 128 - len(rows) - len(ups)
    zeros = lambda n: jnp.zeros((n, 4 * width), F32)
    long = jnp.concatenate([zeros(before)] + ups + [zeros(after)], 0)
    return square.T, long.T


def qkv_all_kernel(d, n_x, row0, *refs):
    it = iter(refs)
    g_hbm, n1_hbm, w_hbm, gres_hbm, gain_ref = [next(it) for _ in range(5)]
    x_hbm = [next(it) for _ in range(n_x)]
    others = [next(it) for _ in range(3 if n_x == 2 else 0)]
    n_g = 1 if n_x == 1 else 2
    outs = [next(it) for _ in range(n_g)]
    vec_ref, keep, send = next(it), next(it), next(it)
    g_all, n1, wqkv, gres, x_all, held, arrive, leave = [next(it) for _ in range(8)]
    gx_held = list(it)
    _, tokens, width = g_all.shape
    half = tokens // 2
    rows = 3 * width // 32
    core = lax.axis_index("dp") & 1
    pairs = [(g_hbm.at[0], g_all.at[0]), (n1_hbm, n1), (g_hbm.at[1], g_all.at[1])]
    pairs += [(g_hbm.at[2], g_all.at[2]), (w_hbm.at[d], wqkv), (gres_hbm, gres)]
    if n_x == 1:
        pairs.append((x_hbm[0], x_all))
    else:
        pairs += [(x_hbm[n], x_all.at[pl.ds(n * half, half)]) for n in range(2)]
    loads = [pltpu.make_async_copy(a, b, arrive.at[n]) for n, (a, b) in enumerate(pairs)]
    for copy in loads:
        copy.start()
    loads[0].wait()
    loads[1].wait()
    for n in range(3):
        if n:
            loads[n + 1].wait()
        left = g_all[n]
        result = dot_tn(left, n1[...])
        if n != 1:
            at = 2 * width if n == 0 else 3 * width
            vec_ref[0:1, at : at + width] = colsum(left.astype(F32))
        owner = n * width // rows
        while owner * rows < (n + 1) * width:
            low, high = max(owner * rows, n * width), min((owner + 1) * rows, (n + 1) * width)
            to = low - owner * rows
            held[(owner >> 1) & 1, chunk_of(owner), to : to + high - low, :] = result[
                low - n * width : high - n * width
            ].astype(BF)
            owner += 1
    tall = held.shape[2]
    stores = [
        pltpu.make_async_copy(
            held.at[core if n == 0 else 1 - core], buf.at[:, pl.ds(row0, tall)], leave.at[n]
        )
        for n, buf in enumerate((keep, send))
    ]
    if not others:
        for copy in stores:
            copy.start()
    for copy in loads[4:]:
        copy.wait()
    sums = []
    for n in (1, 0):
        part = slice(n * half, (n + 1) * half)
        g = jnp.concatenate([g_all[m, part, :] for m in range(3)], 1)
        g_norm = dot_nt(g, wqkv[...])
        xhat, rstd = normalize(x_all[part, :].astype(F32))
        gx = gres[part, :] + norm_back(g_norm, xhat, rstd, gain_ref[...])
        scratch = gx_held[n if n_g == 2 else 0]
        if n_g == 2:
            scratch[...] = gx.astype(scratch.dtype)
            copy = pltpu.make_async_copy(scratch, outs[n], leave.at[2 + n])
        else:
            scratch[part, :] = gx
            span = pl.ds(n * half, half)
            copy = pltpu.make_async_copy(scratch.at[span], outs[0].at[span], leave.at[2 + n])
        copy.start()
        stores.append(copy)
        sums.append((colsum(g_norm * xhat), colsum(g_norm)))
    vec_ref[0:1, :width] = sums[0][0] + sums[1][0]
    vec_ref[0:1, width : 2 * width] = sums[0][1] + sums[1][1]
    if others:
        square, long = turned_vectors([(vec_ref, others[0]), (others[1], others[2])])
        for owner in range(32):
            piece = vector_piece(square, long, owner).astype(BF)
            held[(owner >> 1) & 1, chunk_of(owner), rows:, :] = piece
        for copy in stores[:2]:
            copy.start()
    for copy in stores:
        copy.wait()


def qkv_all(grads, n1, xs, g_resid, params, d, total, row0, vecs=()):
    _, tokens, width = grads.shape
    half = tokens // 2
    rows = 3 * width // 32
    ops = [grads, n1, params["wqkv"], g_resid, params["gains"], *xs, *vecs]
    hbm = pl.BlockSpec(memory_space=pl.ANY)
    vec = pl.BlockSpec((8, 4 * width), lambda i: (0, 0))
    specs = [hbm] * 4 + [layer(params["gains"], d, 0)] + [hbm] * len(xs) + [vec] * len(vecs)
    vm = pltpu.VMEM
    if len(xs) == 1:
        g_outs, g_held = [sds(tokens, width, F32)], [vm((tokens, width), F32)]
    else:
        g_outs = [sds(half, width, F32), sds(half, width, BF)]
        g_held = [vm((half, width), F32), vm((half, width), BF)]
    buf = jax.ShapeDtypeStruct((16, total, width), BF)
    return pl.pallas_call(
        functools.partial(qkv_all_kernel, d, len(xs), row0),
        grid=(1,),
        in_specs=specs,
        out_specs=[hbm] * len(g_outs) + [vec, hbm, hbm],
        out_shape=g_outs + [sds(8, 4 * width, F32), buf, buf],
        scratch_shapes=[
            vm((3, tokens, width), BF),
            vm((tokens, width), BF),
            vm((width, 3 * width), BF),
            vm((tokens, width), F32),
            vm((tokens, width), xs[0].dtype),
            vm((2, 16, rows + (16 if vecs else 0), width), BF),
            pltpu.SemaphoreType.DMA((8,)),
            pltpu.SemaphoreType.DMA((4,)),
        ]
        + g_held,
        compiler_params=VMEM,
        cost_estimate=cost(1, 1),
        name="qkv_all",
    )(*ops)


def plus(*parts):
    total = parts[0].astype(F32)
    for part in parts[1:]:
        total = total + part.astype(F32)
    return total


def place_xy():
    return (lax.axis_index("dp") >> 1) & 1, lax.axis_index("blk")


def stage1_kernel(tall, keep, recv, kp, sp, kq, sq):
    x, y = place_xy()
    both = lambda a, b, rows: plus(keep[0, a, b, rows], recv[0, a, b, rows]).astype(BF)
    up, low = slice(0, tall), slice(tall, keep.shape[3])
    for n in range(2):
        kp[0, n] = both(x, n, up)
        sp[0, n] = both(1 - x, n, up)
        kq[0, n] = both(n, y, low)
        sq[0, n] = both(n, 1 - y, low)


def stage2_kernel(kp, rp, kq, rq, kp2, sp2, kq2, sq2):
    x, y = place_xy()
    kp2[0] = plus(kp[0, y], rp[0, y]).astype(BF)
    sp2[0] = plus(kp[0, 1 - y], rp[0, 1 - y]).astype(BF)
    kq2[0] = plus(kq[0, x], rq[0, x]).astype(BF)
    sq2[0] = plus(kq[0, 1 - x], rq[0, 1 - x]).astype(BF)


def stage3_kernel(kp, rp, kq, rq, own, *sends):
    tall = kp.shape[1]
    z = lax.axis_index("dp") >> 2
    for n, ref in enumerate((own,) + sends):
        at = z ^ n
        ref[:tall, :] = plus(kp[at], rp[at]).astype(ref.dtype)
        ref[tall:, :] = plus(kq[at], rq[at]).astype(ref.dtype)


def stage_call(kernel, name, ops, outs, deps):
    nbytes = sum(math.prod(a.shape) * 2 for a in ops) + sum(math.prod(s) * 2 for s in outs)
    spec = lambda shape: pl.BlockSpec((1,) + shape[1:], lambda i: (i,) + (0,) * (len(shape) - 1))
    return pl.pallas_call(
        ordered(kernel, len(ops), deps),
        grid=(ops[0].shape[0],),
        in_specs=[spec(a.shape) for a in ops] + anywhere(deps),
        out_specs=[spec(s) for s in outs],
        out_shape=[jax.ShapeDtypeStruct(s, BF) for s in outs],
        compiler_params=SMALL,
        cost_estimate=cost(nbytes, nbytes),
        name=name,
    )(*ops, *deps)


def xor_permute(x, dp, mask):
    return lax.ppermute(x, "dp", [(i, i ^ mask) for i in range(dp)])


class Group:
    def __init__(self, keep, send, tall, dp):
        self.tall, self.dp = tall, dp
        self.keep, self.recv = keep, xor_permute(send, dp, 1)

    def stage1(self, deps=()):
        _, total, width = self.keep.shape
        tall = self.tall
        cut = lambda a: a.reshape(4, 2, 2, total, width)
        ops = [cut(self.keep), cut(self.recv)]
        p, q = (4, 2, tall, width), (4, 2, total - tall, width)
        kernel = functools.partial(stage1_kernel, tall)
        self.kp, sp, self.kq, sq = stage_call(kernel, "stage1", ops, [p, p, q, q], deps)
        self.rp, self.rq = xor_permute(sp, self.dp, 2), swap_halves(sq)
        return [self.kp]

    def stage2(self, deps=()):
        p, q = [(4,) + a.shape[2:] for a in (self.kp, self.kq)]
        ops = [self.kp, self.rp, self.kq, self.rq]
        self.kp, sp, self.kq, sq = stage_call(stage2_kernel, "stage2", ops, [p, p, q, q], deps)
        self.rp, self.rq = swap_halves(sp), xor_permute(sq, self.dp, 2)
        return [self.kp]

    def stage3(self, deps=()):
        ops = [self.kp, self.rp, self.kq, self.rq]
        total, width = self.kp.shape[1] + self.kq.shape[1], self.kp.shape[2]
        nbytes = total * width * 24
        pieces = pl.pallas_call(
            ordered(stage3_kernel, 4, deps),
            grid=(1,),
            in_specs=[pl.BlockSpec(a.shape, lambda i: (0, 0, 0)) for a in ops] + anywhere(deps),
            out_specs=[pl.BlockSpec((total, width), lambda i: (0, 0))] * 4,
            out_shape=[sds(total, width, F32)] + [sds(total, width, BF)] * 3,
            compiler_params=SMALL,
            cost_estimate=cost(nbytes, nbytes),
            name="stage3",
        )(*ops, *deps)
        moved = [xor_permute(pieces[n], self.dp, n << 2) for n in range(1, 4)]
        self.pieces = [pieces[0]] + moved
        return [pieces[0]]


def final_kernel(layout, counts, *refs):
    groups = []
    for count in counts:
        groups.append(refs[:count])
        refs = refs[count:]
    outs = dict(zip(layout["outs"], refs))
    width = groups[0][0].shape[1]

    def rows(group, start, count):
        return plus(*(ref[start : start + count, :] for ref in groups[group]))

    for d in range(LAYERS):
        place = layout["rows"][d]
        for name in ("qkv", "out", "up"):
            outs[name][d] = rows(*place[name])
        down = rows(*place["down"])
        thin = outs["down"].shape[1]
        for j in range(down.shape[0] // thin):
            outs["down"][d, :, j * width : (j + 1) * width] = down[j * thin : (j + 1) * thin]
    vec = rows(*layout["vec"])
    lanes = [vec[:, 128 * m : 128 * m + 128] for m in range(width // 128)]
    lanes.append(jnp.zeros((128 - 16 * len(lanes), 128), F32))
    turned = jnp.concatenate(lanes, 0).T
    short = len(VECTORS) - 1
    for d in range(LAYERS):
        for at, (name, n) in enumerate(VECTORS):
            ref = outs[name]
            row = d * short + at if at < short else LAYERS * short + d
            value = turned[row : row + 1, : ref.shape[-1]]
            if n is None:
                ref[d : d + 1, :] = value
            else:
                ref[d, n : n + 1, :] = value


VECTORS = (
    ("gains", 0),
    ("gains", 1),
    ("shifts", 0),
    ("shifts", 1),
    ("bq", None),
    ("bv", None),
    ("bout", None),
    ("bdown", None),
    ("bup", None),
)


def finish(layout, groups, shapes):
    ops = [a for g in groups for a in g]
    names = list(shapes)
    layout = dict(layout, outs=names)
    total = sum(math.prod(a.shape) for a in ops) * 2
    return dict(
        zip(
            names,
            pl.pallas_call(
                functools.partial(final_kernel, layout, [len(g) for g in groups]),
                out_shape=[jax.ShapeDtypeStruct(shapes[n], F32) for n in names],
                compiler_params=SMALL,
                cost_estimate=cost(total, total),
                name="finish",
            )(*ops),
        )
    )


def swap_halves(x):
    return lax.ppermute(x, "blk", [(0, 1), (1, 0)])


class Halving:
    def __init__(self, mesh):
        self.dp = mesh.shape["dp"]
        self.blk = mesh.shape["blk"]
        self.bits = self.dp.bit_length() - 1
        assert self.blk == 2 and 1 << self.bits == self.dp

    def stages(self, blk_first):
        dp_bits = list(range(self.bits))
        rest = ["blk", 1] if blk_first else [1, "blk"]
        return [0] + rest + dp_bits[2:]

    def split(self, rows):
        owners = self.dp * self.blk
        return rows.reshape((2,) * (self.bits + 1) + (rows.shape[0] // owners, rows.shape[1]))

    def run(self, rows, blk_first, wide=False):
        arr = self.split(rows)
        names = list(reversed(range(self.bits))) + ["blk"]
        order = self.stages(blk_first)
        for n, stage in enumerate(order):
            dim = names.index(stage)
            names.pop(dim)
            if stage == "blk":
                mine = lax.axis_index("blk")
                send = lambda x: lax.ppermute(x, "blk", [(0, 1), (1, 0)])
            else:
                mine = (lax.axis_index("dp") >> stage) & 1
                perm = [(i, i ^ (1 << stage)) for i in range(self.dp)]
                send = lambda x: lax.ppermute(x, "dp", perm)
            keep = lax.dynamic_index_in_dim(arr, mine, dim, keepdims=False)
            other = lax.dynamic_index_in_dim(arr, 1 - mine, dim, keepdims=False)
            arr = keep.astype(F32) + send(other).astype(F32)
            if not wide and n + 1 < len(order):
                arr = arr.astype(BF)
        return arr


class PlainSums:
    def __init__(self, mesh):
        self.halving = Halving(mesh)
        self.held = {}

    def add(self, name, d, lefts, right, blk_first):
        self.held[name, d] = self.halving.run(plain_grad(lefts, right), blk_first)

    def results(self, vec):
        vec = self.halving.run(vec, False, wide=True)[0]
        out = {
            n: jnp.stack([self.held[n, d].T for d in range(LAYERS)])
            for n in ("qkv", "out", "up", "down")
        }
        thin = vec.shape[0] // (12 * LAYERS)
        at = 0
        found = {}
        for d in range(LAYERS):
            for name, n in VECTORS:
                size = 4 * thin if name == "bup" else thin
                found.setdefault((name, d), []).append(vec[at : at + size])
                at += size
        for name in dict(VECTORS):
            rows = [jnp.stack(found[name, d]) for d in range(LAYERS)]
            out[name] = jnp.stack(rows if len(rows[0]) == 2 else [r[0] for r in rows])
        return out


def shards(
    mesh,
    hidden_in,
    cell_lengths,
    cotangent,
    ln_gains,
    ln_biases,
    w_qkv,
    b_query,
    b_value,
    w_out,
    b_out,
    w_up,
    b_up,
    w_down,
    b_down,
):
    cells, half, width = hidden_in.shape
    tokens = cells * half
    dp, blk = mesh.shape["dp"], mesh.shape["blk"]
    owners = dp * blk
    assert cells == blk == 2
    side = lax.axis_index("blk")
    meta = cell_lengths
    grouped = dp == 16 and width == 768 and b_up.shape[1] == 4 * width

    def split_cell(both):
        own = lax.dynamic_index_in_dim(both, side, 0, False)
        other = lax.dynamic_index_in_dim(both, 1 - side, 0, False)
        return own, swap_halves(other)

    def return_cell(own, back):
        return jnp.where(side == 0, jnp.stack([own, back]), jnp.stack([back, own]))

    rows = lambda v: v[..., None, :]
    params = {
        "gains": rows(ln_gains),
        "shifts": rows(ln_biases),
        "wqkv": w_qkv,
        "bias": rows(jnp.concatenate([b_query, jnp.zeros_like(b_query), b_value], 1)),
        "wout": w_out,
        "bout": rows(b_out),
        "wup": w_up,
        "bup": rows(b_up),
        "wdown": w_down,
        "bdown": rows(b_down),
    }
    own, other = split_cell(hidden_in)
    entered = enter(own, params, 0, None, tokens, 0)
    n1, proj = enter(other, params, 0, entered, tokens, half)
    xs = (own, other)
    saved = []
    for d in range(LAYERS):
        mixed, low, lse = attn_fwd(proj, meta)
        last = d + 1 == LAYERS
        outs = post(mixed, xs, params, d, last)
        saved.append((xs, n1, proj, mixed, low, lse) + tuple(outs[:4]))
        if not last:
            x, n1, proj = outs[4:]
            xs = (x,)
    returned = swap_halves(outs[5])
    hidden_out = return_cell(outs[4], returned)

    gxs = split_cell(cotangent)
    backward = backward_grouped if grouped else backward_plain
    gx, out = backward(mesh, params, saved, gxs, meta, [returned])
    grad_in = return_cell(gx[0], gx[1].astype(F32))
    order = ("gains", "shifts", "qkv", "bq", "bv", "out", "bout", "up", "bup", "down", "bdown")
    return (hidden_out, grad_in) + tuple(out[n] for n in order)


def vector_rows(owners, width, ln1, ln2, sums):
    flat = []
    for d in range(LAYERS):
        for v in (
            ln1[d][:width],
            ln2[d][:width],
            ln1[d][width:],
            ln2[d][width:],
            sums["qkv", d][:width],
            sums["qkv", d][-width:],
            sums["out", d],
            sums["down", d],
            sums["up", d],
        ):
            flat.append(v.reshape(owners, -1))
    return jnp.concatenate(flat, 1)


def backward_plain(mesh, params, saved, gxs, meta, early):
    sums = PlainSums(mesh)
    ln1, ln2, cols = {}, {}, {}
    for d in reversed(range(LAYERS)):
        xs, n1, proj, mixed, low, lse, resid, n2, active, slope = saved[d]
        tokens, width = resid.shape
        gy, gu, g_resid, ga, g_mixed, vec2 = ff_back(gxs, slope, resid, params, d)
        sums.add("down", d, [gy], active, False)
        sums.add("up", d, [gu], n2, True)
        sums.add("out", d, [ga], mixed, False)
        grads = attn_bwd(proj, mixed, low, g_mixed, lse, meta, (0, width // 128))
        sums.add("qkv", d, [grads[n] for n in range(3)], n1, True)
        total = lambda a: jnp.sum(a.astype(F32), 0)
        cols.update({("down", d): total(gy), ("up", d): total(gu), ("out", d): total(ga)})
        cols["qkv", d] = jnp.concatenate([total(grads[n]) for n in range(3)])
        ln2[d] = vec2[0]
        if d > 0:
            gx, vec1 = qkv_back(grads, xs[0], g_resid, params, d, 0, tokens, F32)
            gxs = (gx,)
            ln1[d] = vec1[0]
        else:
            half = tokens // 2
            theirs, vec_a = qkv_back(grads, xs[1], g_resid, params, d, half, half, BF)
            mine, vec_b = qkv_back(grads, xs[0], g_resid, params, d, 0, half, F32)
            ln1[d] = vec_a[0] + vec_b[0]
    owners = mesh.shape["dp"] * mesh.shape["blk"]
    out = sums.results(vector_rows(owners, width, ln1, ln2, cols))
    return (mine, swap_halves(theirs)), out


def backward_grouped(mesh, params, saved, gxs, meta, early):
    dp = mesh.shape["dp"]
    width = saved[0][6].shape[1]
    t, pairs = width // 32, width // 128

    def ff_grads(gxs, d, into, total, n_out):
        mixed, resid, n2, active, slope = saved[d][3], *saved[d][6:]
        g_resid, g_mixed, vec, *bufs = ff_all(
            gxs, slope, resid, active, n2, mixed, params, d, into, total, n_out
        )
        return g_resid, g_mixed, vec, bufs

    xs, n1, proj, mixed, low, lse = saved[1][:6]
    g_resid, g_mixed, ff_vec1, bufs = ff_grads(gxs, 1, None, 9 * t, 1)
    layer1 = lax.psum_scatter(bufs[0], ("dp", "blk"), scatter_dimension=0, tiled=True)[0]
    grads = attn_bwd(proj, mixed, low, g_mixed, lse, meta, (0, pairs), None, bufs + early)
    gx, proj_vec1, *bufs = qkv_all(grads, n1, xs, g_resid, params, 1, 12 * t, 9 * t)
    xs, n1, proj, mixed, low, lse = saved[0][:6]
    g_resid, g_mixed, ff_vec0, bufs = ff_grads((gx,), 0, bufs, 12 * t, 2)
    ff0 = Group(*bufs, 6 * t, dp)
    grads = attn_bwd(proj, mixed, low, g_mixed, lse, meta, (0, 2), None, [ff0.keep])
    dep = ff0.stage1(deps=[grads])
    grads = attn_bwd(proj, mixed, low, g_mixed, lse, meta, (2, pairs), grads, dep)
    vecs = (ff_vec0, proj_vec1, ff_vec1)
    mine, theirs, _, *bufs = qkv_all(grads, n1, xs, g_resid, params, 0, 3 * t + 16, 0, vecs)
    dep = ff0.stage2(deps=[theirs])
    at0 = Group(bufs[0], after(bufs[1], dep), 48, dp)
    dep = at0.stage1(deps=dep)
    dep = ff0.stage3(deps=dep)
    back = swap_halves(after(theirs, dep))
    at0.stage2(deps=dep + ff0.pieces[1:3] + [back])
    at0.stage3(deps=ff0.pieces[3:])
    layout = {
        "rows": [
            {"down": (1, 0, 4 * t), "up": (1, 4 * t, 4 * t), "out": (1, 8 * t, t), "qkv": (2, 0, 3 * t)},
            {"down": (0, 0, 4 * t), "up": (0, 4 * t, 4 * t), "out": (0, 8 * t, t), "qkv": (1, 9 * t, 3 * t)},
        ],
        "vec": (2, 3 * t, 16),
    }
    shapes = {
        "qkv": (LAYERS, 3 * t, width),
        "out": (LAYERS, t, width),
        "up": (LAYERS, 4 * t, width),
        "down": (LAYERS, t, 4 * width),
        "gains": (LAYERS, 2, t),
        "shifts": (LAYERS, 2, t),
        "bq": (LAYERS, t),
        "bv": (LAYERS, t),
        "bout": (LAYERS, t),
        "bdown": (LAYERS, t),
        "bup": (LAYERS, 4 * t),
    }
    out = finish(layout, [[layer1], ff0.pieces, at0.pieces], shapes)
    for name in ("qkv", "out", "up", "down"):
        out[name] = jnp.swapaxes(out[name], 1, 2)
    return (mine, back), out


def solution(mesh):
    both = ("dp", "blk")
    row = P("dp", "blk", None)
    last3 = P(None, None, both)
    last2 = P(None, both)
    return jax.shard_map(
        functools.partial(shards, mesh),
        mesh=mesh,
        in_specs=(row, P("dp"), row) + (P(),) * 11,
        out_specs=(
            row,
            row,
            last3,
            last3,
            last3,
            last2,
            last2,
            last3,
            last2,
            last3,
            last2,
            last3,
            last2,
        ),
        check_vma=False,
    )
```

```python
import functools
import math

import jax
import jax.numpy as jnp
from jax import lax
from jax.experimental import pallas as pl
from jax.experimental.pallas import tpu as pltpu
from jax.sharding import PartitionSpec as P

HEAD_DIM = 64
LAYERS = 2
EPSILON = 1e-05
NEG = -1e30
BF = jnp.bfloat16
F32 = jnp.float32
QSCALE = math.log2(math.e) / math.sqrt(HEAD_DIM)


def dot_nn(a, b):
    return lax.dot_general(a, b, (((1,), (0,)), ((), ())), preferred_element_type=F32)


def dot_nt(a, b):
    return lax.dot_general(a, b, (((1,), (1,)), ((), ())), preferred_element_type=F32)


def dot_tn(a, b):
    return lax.dot_general(a, b, (((0,), (0,)), ((), ())), preferred_element_type=F32)


def mask_block(meta_ref, kaug, qone, tokens):
    side = lax.axis_index("blk")
    rows = lax.broadcasted_iota(jnp.int32, (tokens, 128), 0)
    lanes = lax.broadcasted_iota(jnp.int32, (tokens, 128), 1)
    half = tokens // 2
    position = jnp.where(rows < half, rows + side * half, rows - side * half)
    masked = jnp.logical_and(lanes == 0, position >= meta_ref[side])
    kaug[...] = jnp.where(masked, NEG, 0.0).astype(BF)
    qone[...] = jnp.where(lanes == 0, 1.0, 0.0).astype(BF)


def attn_fwd_kernel(
    chunk, ahead, meta_ref, q_ref, k_ref, v_ref, o_ref, low_ref, lse_ref, kaug, qone
):
    tokens = q_ref.shape[0]

    @pl.when(pl.program_id(0) == 0)
    def _():
        mask_block(meta_ref, kaug, qone, tokens)

    first = lax.broadcasted_iota(jnp.int32, (tokens, 128), 1) < HEAD_DIM
    q, k, v = q_ref[...], k_ref[...], v_ref[...]
    zero = jnp.zeros_like(k)
    sel = [first, jnp.logical_not(first)]
    keys = [jnp.concatenate([jnp.where(sel[h], k, zero), kaug[...]], 1) for h in range(2)]
    ones = jnp.ones((16, tokens), BF)
    vals = [jnp.concatenate([jnp.where(sel[h], v, zero).T, ones], 0) for h in range(2)]
    qa = jnp.concatenate([q, qone[...]], 1)
    units = [(c, h) for c in range(tokens // chunk) for h in range(2)]
    ready = {}

    def scores(unit):
        c, h = unit
        ready[unit] = dot_nt(keys[h], qa[c * chunk : (c + 1) * chunk])

    for unit in units[:ahead]:
        scores(unit)
    kept = {}
    for n, unit in enumerate(units):
        if n + ahead < len(units):
            scores(units[n + ahead])
        c, h = unit
        cols = slice(c * chunk, (c + 1) * chunk)
        st = ready.pop(unit)
        top = jnp.max(st, axis=0, keepdims=True)
        p = jnp.exp2(st - top)
        p = p.astype(BF)
        both = dot_nn(vals[h], p)
        kept[h] = (both[:128], top, both[128:129])
        if h == 1:
            head = lax.broadcasted_iota(jnp.int32, (128, chunk), 0) < HEAD_DIM
            inv = jnp.where(head, 1.0 / kept[0][2], 1.0 / kept[1][2])
            out = ((kept[0][0] + kept[1][0]) * inv).T
            high = out.astype(BF)
            o_ref[cols, :] = high
            low_ref[cols, :] = (out - high.astype(F32)).astype(BF)
            for g in range(2):
                lse_ref[0, g : g + 1, cols] = kept[g][1] + jnp.log2(kept[g][2])


def attn_fwd(proj, meta):
    tokens, width = proj.shape[0], proj.shape[1] // 3
    pairs = width // 128
    spec = lambda off: pl.BlockSpec((tokens, 128), lambda i, m: (0, off + i))
    return pl.pallas_call(
        functools.partial(attn_fwd_kernel, tokens // 2, 3),
        grid_spec=pltpu.PrefetchScalarGridSpec(
            num_scalar_prefetch=1,
            grid=(pairs,),
            in_specs=[spec(0), spec(pairs), spec(2 * pairs)],
            out_specs=[spec(0), spec(0), pl.BlockSpec((1, 8, tokens), lambda i, m: (i, 0, 0))],
            scratch_shapes=[pltpu.VMEM((tokens, 128), BF), pltpu.VMEM((tokens, 128), BF)],
        ),
        out_shape=[
            jax.ShapeDtypeStruct((tokens, width), BF),
            jax.ShapeDtypeStruct((tokens, width), BF),
            jax.ShapeDtypeStruct((pairs, 8, tokens), F32),
        ],
        compiler_params=pltpu.CompilerParams(
            vmem_limit_bytes=56 << 20, dimension_semantics=("arbitrary",)
        ),
        cost_estimate=pl.CostEstimate(
            flops=4 * tokens * tokens * width * 3,
            bytes_accessed=tokens * width * 8,
            transcendentals=pairs * 2 * tokens * tokens,
        ),
        name="attn_fwd",
    )(meta, proj, proj, proj)


def attn_bwd_kernel(
    meta_ref, q_ref, k_ref, v_ref, o_ref, low_ref, do_ref, lse_ref, out_ref, kaug, qone
):
    tokens = q_ref.shape[0]

    @pl.when(pl.program_id(0) == 0)
    def _():
        mask_block(meta_ref, kaug, qone, tokens)

    first = lax.broadcasted_iota(jnp.int32, (tokens, 128), 1) < HEAD_DIM
    q, k, v, do = q_ref[...], k_ref[...], v_ref[...], do_ref[...]
    zero = jnp.zeros_like(k)
    sel = [first, jnp.logical_not(first)]
    qa = jnp.concatenate([q, qone[...]], 1)
    prod = ((o_ref[...].astype(F32) + low_ref[...].astype(F32)) * do.astype(F32)).T
    dq = dk = dv = None
    for h in range(2):
        kh = jnp.where(sel[h], k, zero)
        delta = jnp.sum(prod[h * HEAD_DIM : (h + 1) * HEAD_DIM], 0, keepdims=True)
        st = dot_nt(jnp.concatenate([kh, kaug[...]], 1), qa)
        dpt = dot_nt(jnp.where(sel[h], v, zero), do)
        p = jnp.exp2(st - lse_ref[0, h : h + 1, :])
        ds = (p * (dpt - delta)).astype(BF)
        dvh = dot_nn(p.astype(BF), jnp.where(sel[h], do, zero))
        dkh = dot_nn(ds, jnp.where(sel[h], q, zero))
        dqh = dot_nn(kh.T, ds)
        dq, dk, dv = (dqh, dkh, dvh) if h == 0 else (dq + dqh, dk + dkh, dv + dvh)
    out_ref[0] = (dq * (1.0 / math.sqrt(HEAD_DIM))).T.astype(BF)
    out_ref[1] = (dk * math.log(2.0)).astype(BF)
    out_ref[2] = dv.astype(BF)


def attn_bwd(proj, mixed, low, g_mixed, lse, meta, pairs, into=None, deps=()):
    tokens, width = mixed.shape
    count = width // 128
    start, stop = pairs
    spec = lambda off: pl.BlockSpec((tokens, 128), lambda i, m: (0, off + start + i))
    ops = [meta, proj, proj, proj, mixed, low, g_mixed, lse]
    specs = [spec(0), spec(count), spec(2 * count), spec(0), spec(0), spec(0)]
    specs += [pl.BlockSpec((1, 8, tokens), lambda i, m: (start + i, 0, 0))]
    extra = ([] if into is None else [into]) + list(deps)
    return pl.pallas_call(
        ordered(attn_bwd_kernel, len(ops), extra),
        grid_spec=pltpu.PrefetchScalarGridSpec(
            num_scalar_prefetch=1,
            grid=(stop - start,),
            in_specs=specs + anywhere(extra),
            out_specs=pl.BlockSpec((3, tokens, 128), lambda i, m: (0, 0, start + i)),
            scratch_shapes=[pltpu.VMEM((tokens, 128), BF), pltpu.VMEM((tokens, 128), BF)],
        ),
        out_shape=jax.ShapeDtypeStruct((3, tokens, width), BF),
        input_output_aliases={} if into is None else {len(ops): 0},
        compiler_params=pltpu.CompilerParams(
            vmem_limit_bytes=56 << 20, dimension_semantics=("arbitrary",)
        ),
        cost_estimate=cost(1, 1),
        name="attn_bwd",
    )(*ops, *extra)


VMEM = pltpu.CompilerParams(vmem_limit_bytes=58 << 20, dimension_semantics=("arbitrary",))
SMALL = pltpu.CompilerParams(vmem_limit_bytes=20 << 20)


def ordered(kernel, n_in, deps):
    if not deps:
        return kernel
    return lambda *refs: kernel(*refs[:n_in], *refs[n_in + len(deps) :])


def after(array, deps):
    return lax.optimization_barrier((array, *deps))[0]


def anywhere(arrays):
    return [pl.BlockSpec(memory_space=pl.ANY)] * len(arrays)


def layer(arr, d, n=0):
    lead = arr.ndim - 2
    index = (d, n)[:lead] + (0, 0)
    return pl.BlockSpec(
        (None,) * lead + arr.shape[lead:], lambda *_: index, pipeline_mode=pl.Buffered(1)
    )


def tile(rows, width, first=0):
    return pl.BlockSpec((rows, width), lambda i, *_: (first + i, 0))


def sds(rows, width, dtype):
    return jax.ShapeDtypeStruct((rows, width), dtype)


def cost(flops, nbytes, trans=0):
    return pl.CostEstimate(flops=int(flops), bytes_accessed=int(nbytes), transcendentals=int(trans))


def normalize(x):
    mean = jnp.mean(x, -1, keepdims=True)
    centered = x - mean
    variance = jnp.mean(centered * centered, -1, keepdims=True)
    rstd = lax.rsqrt(variance + EPSILON)
    return centered * rstd, rstd


def project(n1, wqkv_ref, bias_ref, proj_ref, width):
    for j, factor in enumerate((QSCALE, 1.0, 1.0)):
        cols = slice(j * width, (j + 1) * width)
        part = dot_nn(n1, wqkv_ref[:, cols]) + bias_ref[:, cols]
        proj_ref[:, cols] = (part * factor).astype(BF)


def attn_in(params, d):
    arrays = [params["gains"], params["shifts"], params["wqkv"], params["bias"]]
    return arrays, [layer(arrays[0], d, 0), layer(arrays[1], d, 0), layer(arrays[2], d), layer(arrays[3], d)]


def enter_kernel(x_ref, gain_ref, shift_ref, wqkv_ref, bias_ref, *refs):
    n1_ref, proj_ref = refs[-2:]
    width = x_ref.shape[1]
    xhat, _ = normalize(x_ref[...].astype(F32))
    n1 = (xhat * gain_ref[...] + shift_ref[...]).astype(BF)
    n1_ref[...] = n1
    project(n1, wqkv_ref, bias_ref, proj_ref, width)


def enter(x, params, d, into, tokens, first):
    rows, width = x.shape
    block = 256
    at = first // block
    arrays, specs = attn_in(params, d)
    ops = [x] + arrays
    specs = [tile(block, width)] + specs
    alias = {}
    if into is not None:
        ops += list(into)
        specs += [pl.BlockSpec(memory_space=pl.ANY)] * 2
        alias = {5: 0, 6: 1}
    return pl.pallas_call(
        enter_kernel,
        grid=(rows // block,),
        in_specs=specs,
        out_specs=[tile(block, width, at), tile(block, 3 * width, at)],
        out_shape=[sds(tokens, width, BF), sds(tokens, 3 * width, BF)],
        input_output_aliases=alias,
        compiler_params=SMALL,
        cost_estimate=cost(6 * rows * width * width, rows * width * 10 + 6 * width * width),
        name="enter",
    )(*ops)


def halves(tokens, block, width):
    turn = tokens // block // 2
    own = pl.BlockSpec((block, width), lambda i, *_: (jnp.minimum(i, turn - 1), 0))
    other = pl.BlockSpec((block, width), lambda i, *_: (jnp.maximum(i - turn, 0), 0))
    return [own, other]


def joined(refs):
    if len(refs) == 1:
        return refs[0][...].astype(F32)
    early = pl.program_id(0) < pl.num_programs(0) // 2
    return jnp.where(early, refs[0][...].astype(F32), refs[1][...].astype(F32))


def post_kernel(d, last, parts, n_x, *refs):
    it = iter(refs)
    mixed_ref = next(it)
    x_refs = [next(it) for _ in range(n_x)]
    bout_ref, gain_ref, shift_ref, bup_ref, bdown_ref = [next(it) for _ in range(5)]
    if not last:
        gain1_ref, shift1_ref, bias_ref = next(it), next(it), next(it)
    sources = [next(it) for _ in range(3 if last else 4)]
    resid_ref, n2_ref, active_ref, slope_ref = next(it), next(it), next(it), next(it)
    outs = [next(it) for _ in range(2 if last else 3)]
    wout, wup, wdown = next(it), next(it), next(it)
    wqkv = None if last else next(it)
    arrive = next(it)
    step = pl.program_id(0)
    width = mixed_ref.shape[1]
    hidden = wup.shape[1] // parts

    def load(n):
        part = pl.ds((n - 1) // 2 * hidden, hidden)
        if n == 0:
            pair = sources[0].at[d], wout
        elif n > 2 * parts:
            pair = sources[3].at[d + 1], wqkv
        elif n % 2:
            pair = sources[1].at[d, :, part], wup.at[:, part]
        else:
            pair = sources[2].at[d, part], wdown.at[part]
        return pltpu.make_async_copy(*pair, arrive.at[n])

    @pl.when(step == 0)
    def _():
        for n in range(2 * parts + (1 if last else 2)):
            load(n).start()

    def body(wait):
        wait(0)
        resid = joined(x_refs) + dot_nn(mixed_ref[...], wout[...]) + bout_ref[...]
        resid_ref[...] = resid
        xhat, _ = normalize(resid)
        n2 = (xhat * gain_ref[...] + shift_ref[...]).astype(BF)
        n2_ref[...] = n2
        total = resid + bdown_ref[...]
        for j in range(parts):
            cols = slice(j * hidden, (j + 1) * hidden)
            wait(2 * j + 1)
            upper = dot_nn(n2, wup[:, cols]) + bup_ref[:, cols]
            cdf = 0.5 + 0.5 * lax.erf(upper * math.sqrt(0.5))
            dens = jnp.exp2(upper * upper * (-0.5 * math.log2(math.e))) * (1.0 / math.sqrt(2.0 * math.pi))
            active = (upper * cdf).astype(BF)
            active_ref[:, cols] = active
            slope_ref[:, cols] = (cdf + upper * dens).astype(BF)
            wait(2 * j + 2)
            total = total + dot_nn(active, wdown[cols, :])
        if last:
            for n, ref in enumerate(outs):

                @pl.when(step // (pl.num_programs(0) // 2) == n)
                def _():
                    ref[...] = total.astype(BF)
        else:
            x_out, n1_ref, proj_ref = outs
            x_out[...] = total
            xhat, _ = normalize(total)
            n1 = (xhat * gain1_ref[...] + shift1_ref[...]).astype(BF)
            n1_ref[...] = n1
            wait(2 * parts + 1)
            project(n1, wqkv, bias_ref, proj_ref, width)

    pl.when(step == 0)(lambda: body(lambda n: load(n).wait()))
    pl.when(step > 0)(lambda: body(lambda n: None))


def post(mixed, xs, params, d, last):
    tokens, width = mixed.shape
    block = 256
    parts = 4
    ff = params["wup"].shape[2]
    small = [(params[n], d) for n in ("bout", "gains", "shifts", "bup", "bdown")]
    specs = [layer(a, e, 1) for a, e in small]
    weights = ["wout", "wup", "wdown"]
    if not last:
        more = [(params[n], d + 1) for n in ("gains", "shifts", "bias")]
        specs += [layer(a, e, 0) for a, e in more]
        small += more
        weights.append("wqkv")
    arrays = [a for a, _ in small] + [params[n] for n in weights]
    ops = [mixed] + list(xs) + arrays
    x_specs = [tile(block, width)] if len(xs) == 1 else halves(tokens, block, width)
    outs = [(tokens, width, F32), (tokens, width, BF), (tokens, ff, BF), (tokens, ff, BF)]
    out_specs = [tile(block, w) for _, w, _ in outs]
    if last:
        outs += [(tokens // 2, width, BF)] * 2
        out_specs += halves(tokens, block, width)
    else:
        outs += [(tokens, width, F32), (tokens, width, BF), (tokens, 3 * width, BF)]
        out_specs += [tile(block, w) for _, w, _ in outs[4:]]
    flops = 2 * tokens * width * (width + 2 * ff + (0 if last else 3 * width))
    return pl.pallas_call(
        functools.partial(post_kernel, d, last, parts, len(xs)),
        grid=(tokens // block,),
        in_specs=[tile(block, width)] + x_specs + specs + anywhere(weights),
        out_specs=out_specs,
        out_shape=[sds(*o) for o in outs],
        scratch_shapes=[pltpu.VMEM(params[n].shape[1:], BF) for n in weights]
        + [pltpu.SemaphoreType.DMA((2 * parts + 2,))],
        compiler_params=VMEM,
        cost_estimate=cost(flops, tokens * ff * 10, 2 * tokens * ff),
        name="post",
    )(*ops)


def norm_back(g_normed, xhat, rstd, gain):
    scaled = g_normed * gain
    mean1 = jnp.mean(scaled, -1, keepdims=True)
    mean2 = jnp.mean(scaled * xhat, -1, keepdims=True)
    return rstd * (scaled - mean1 - xhat * mean2)


def add_row(ref, row, start, value, fresh):
    cols = slice(start, start + value.shape[1])

    @pl.when(fresh)
    def _():
        ref[row : row + 1, cols] = value

    @pl.when(jnp.logical_not(fresh))
    def _():
        ref[row : row + 1, cols] += value


def colsum(x):
    return jnp.sum(x, 0, keepdims=True)


def ff_back_kernel(parts, n_x, *refs):
    gx_refs = refs[:n_x]
    slope_ref, resid_ref, wdown_ref, wup_ref, wout_ref, gain_ref = refs[n_x : n_x + 6]
    gy_ref, gu_ref, gres_ref, ga_ref, gmix_ref, vec_ref = refs[n_x + 6 :]
    fresh = pl.program_id(0) == 0
    width = resid_ref.shape[1]
    gx = joined(gx_refs)
    gy = gx.astype(BF)
    gy_ref[...] = gy
    hidden = wup_ref.shape[1] // parts
    g_n2 = None
    for j in range(parts):
        cols = slice(j * hidden, (j + 1) * hidden)
        g_act = dot_nt(gy, wdown_ref[cols, :])
        gu = (g_act * slope_ref[:, cols].astype(F32)).astype(BF)
        gu_ref[:, cols] = gu
        part = dot_nt(gu, wup_ref[:, cols])
        g_n2 = part if g_n2 is None else g_n2 + part
    xhat, rstd = normalize(resid_ref[...])
    g_resid = gx + norm_back(g_n2, xhat, rstd, gain_ref[...])
    gres_ref[...] = g_resid
    ga = g_resid.astype(BF)
    ga_ref[...] = ga
    gmix_ref[...] = dot_nt(ga, wout_ref[...]).astype(BF)
    add_row(vec_ref, 0, 0, colsum(g_n2 * xhat), fresh)
    add_row(vec_ref, 0, width, colsum(g_n2), fresh)


def ff_back(gxs, slope, resid, params, d, deps=()):
    tokens, width = resid.shape
    ff = slope.shape[1]
    block = 512
    outs = [(width, BF), (ff, BF), (width, F32), (width, BF), (width, BF)]
    assert ff == 4 * width
    x_specs = [tile(block, width)] if len(gxs) == 1 else halves(tokens, block, width)
    arrays = [params[n] for n in ("wdown", "wup", "wout", "gains")]
    return pl.pallas_call(
        ordered(functools.partial(ff_back_kernel, 4, len(gxs)), len(gxs) + 6, deps),
        grid=(tokens // block,),
        in_specs=x_specs
        + [tile(block, ff), tile(block, width)]
        + [layer(a, d, 1) for a in arrays]
        + anywhere(deps),
        out_specs=[tile(block, w) for w, _ in outs] + [pl.BlockSpec((8, 2 * width), lambda i: (0, 0))],
        out_shape=[sds(tokens, w, t) for w, t in outs] + [sds(8, 2 * width, F32)],
        compiler_params=VMEM,
        cost_estimate=cost(2 * tokens * width * (2 * ff + width), tokens * ff * 8),
        name="ff_back",
    )(*gxs, slope, resid, *arrays, *deps)


def qkv_back_kernel(grads_ref, wqkv_ref, x_ref, gres_ref, gain_ref, *refs):
    gx_ref, vec_ref = refs[-2:]
    fresh = pl.program_id(0) == 0
    width = x_ref.shape[1]
    grads = [grads_ref[n] for n in range(3)]
    g_norm = dot_nt(jnp.concatenate(grads, 1), wqkv_ref[...])
    xhat, rstd = normalize(x_ref[...].astype(F32))
    gx = gres_ref[...] + norm_back(g_norm, xhat, rstd, gain_ref[...])
    gx_ref[...] = gx.astype(gx_ref.dtype)
    add_row(vec_ref, 0, 0, colsum(g_norm * xhat), fresh)
    add_row(vec_ref, 0, width, colsum(g_norm), fresh)


def qkv_back(grads, x, g_resid, params, d, first, rows, dtype, deps=()):
    width = x.shape[1]
    block = 256
    at = first // block
    return pl.pallas_call(
        ordered(qkv_back_kernel, 5, deps),
        grid=(rows // block,),
        in_specs=[
            pl.BlockSpec((3, block, width), lambda i: (0, at + i, 0)),
            layer(params["wqkv"], d),
            tile(block, width),
            tile(block, width, at),
            layer(params["gains"], d, 0),
            *anywhere(deps),
        ],
        out_specs=[tile(block, width), pl.BlockSpec((8, 2 * width), lambda i: (0, 0))],
        out_shape=[sds(rows, width, dtype), sds(8, 2 * width, F32)],
        compiler_params=VMEM,
        cost_estimate=cost(6 * rows * width * width, rows * width * 20),
        name="qkv_back",
    )(grads, params["wqkv"], x, g_resid, params["gains"], *deps)


def plain_grad(lefts, right):
    return jnp.concatenate([dot_tn(left, right) for left in lefts], 0).astype(BF)


def chunk_of(owner):
    return (owner >> 2) * 2 + (owner & 1)


ROWS = 512


def ff_all_kernel(n_x, n_out, firsts, d, *refs):
    it = iter(refs)
    gx_refs = [next(it) for _ in range(n_x)]
    slope_ref, resid_ref, gain_ref, active_ref = next(it), next(it), next(it), next(it)
    sources = [next(it) for _ in range(5)]
    refs = list(it)
    gres_ref, gmix_ref, vec_ref = refs[-16 - n_out : -13 - n_out]
    bufs = refs[-13 - n_out : -13]
    wdown, wup, wout, n2, mixed, gy_all, gu_all, ga_all, down, up, out, arrive, leave = refs[-13:]
    step = pl.program_id(0)
    tokens, width = gy_all.shape
    parts = wup.shape[1] // width
    blocks = tokens // ROWS
    thin = width // 32
    core = lax.axis_index("dp") & 1

    def load(n):
        j = n // 2
        rows = pl.ds(j * width, width)
        if j < parts and n % 2 == 0:
            pair = sources[0].at[d, rows], wdown.at[rows]
        elif j < parts:
            pair = sources[1].at[d, :, rows], wup.at[:, rows]
        else:
            late = n - 2 * parts
            pair = (sources[2].at[d], sources[3], sources[4])[late], (wout, n2, mixed)[late]
        return pltpu.make_async_copy(*pair, arrive.at[n])

    @pl.when(step == 0)
    def _():
        for n in range(2 * parts + 3):
            load(n).start()

    def stores(kind, j):
        slot = j % 2
        if kind == "up":
            held, row, count, tall, place = up, firsts + 4 * thin, 8, 4 * thin, 8 * j
        else:
            held = down if kind == "down" else out
            row, count, tall, place = firsts + (j if kind == "down" else 8) * thin, 32, thin, 0
        sem = {"down": 0, "up": 4, "out": 8}[kind] + 2 * slot
        rows = pl.ds(row, tall)
        if n_out == 1:
            dst = bufs[0].at[pl.ds(place, count), rows]
            return [pltpu.make_async_copy(held.at[slot], dst, leave.at[sem])]
        part = count // 2
        found = []
        for n, buf in enumerate(bufs):
            src = held.at[slot, pl.ds((core if n == 0 else 1 - core) * part, part)]
            dst = buf.at[pl.ds(place // 2, part), rows]
            found.append(pltpu.make_async_copy(src, dst, leave.at[sem + n]))
        return found

    def put(held, slot, result):
        count, tall = held.shape[1], held.shape[2]
        for owner in range(count):
            at = owner if n_out == 1 else ((owner >> 1) & 1) * (count // 2) + chunk_of(owner)
            held[slot, at] = result[owner * tall : (owner + 1) * tall].astype(BF)

    def body(wait):
        rows = pl.ds(pl.multiple_of(step * ROWS, ROWS), ROWS)
        fresh = step == 0
        gx = joined_rows(gx_refs, step)
        gy = gx.astype(BF)
        gy_all[rows, :] = gy
        g_n2 = None
        for j in range(parts):
            cols = slice(j * width, (j + 1) * width)
            wait(2 * j)
            g_act = dot_nt(gy, wdown[cols, :])
            gu = (g_act * slope_ref[:, cols].astype(F32)).astype(BF)
            gu_all[rows, cols] = gu
            wait(2 * j + 1)
            part = dot_nt(gu, wup[:, cols])
            g_n2 = part if g_n2 is None else g_n2 + part
        xhat, rstd = normalize(resid_ref[...])
        g_resid = gx + norm_back(g_n2, xhat, rstd, gain_ref[...])
        gres_ref[...] = g_resid
        ga = g_resid.astype(BF)
        ga_all[rows, :] = ga
        wait(2 * parts)
        gmix_ref[...] = dot_nt(ga, wout[...]).astype(BF)
        add_row(vec_ref, 0, 0, colsum(g_n2 * xhat), fresh)
        add_row(vec_ref, 0, width, colsum(g_n2), fresh)
        add_row(vec_ref, 0, 2 * width, colsum(gy.astype(F32)), fresh)
        add_row(vec_ref, 0, 3 * width, colsum(ga.astype(F32)), fresh)

    pl.when(step == 0)(lambda: body(lambda n: load(n).wait()))
    pl.when(jnp.logical_and(step > 0, step < blocks))(lambda: body(lambda n: None))

    @pl.when(step == blocks)
    def _():
        load(2 * parts + 1).wait()
        load(2 * parts + 2).wait()

    for j in range(parts):

        @pl.when(step == blocks + j)
        def _():
            if j >= 2:
                for copy in stores("down", j - 2):
                    copy.wait()
            put(down, j % 2, dot_tn(gy_all[...], active_ref[...]))
            for copy in stores("down", j):
                copy.start()

        @pl.when(step == blocks + parts + j)
        def _():
            if j >= 2:
                for copy in stores("up", j - 2):
                    copy.wait()
            cols = slice(j * width, (j + 1) * width)
            left = gu_all[:, cols]
            put(up, j % 2, dot_tn(left, n2[...]))
            vec_ref[1:2, cols] = colsum(left.astype(F32))
            for copy in stores("up", j):
                copy.start()

    @pl.when(step == blocks + 2 * parts)
    def _():
        put(out, 0, dot_tn(ga_all[...], mixed[...]))
        for copy in stores("out", 0):
            copy.start()
        for kind, first, count in (("down", parts - 2, 2), ("up", parts - 2, 2), ("out", 0, 1)):
            for j in range(first, first + count):
                for copy in stores(kind, j):
                    copy.wait()


def joined_rows(refs, step):
    if len(refs) == 1:
        return refs[0][...].astype(F32)
    return jnp.where(step == 0, refs[0][...].astype(F32), refs[1][...].astype(F32))


def ff_all(gxs, slope, resid, active, n2, mixed, params, d, into, total, n_out):
    tokens, width = resid.shape
    ff = slope.shape[1]
    parts, blocks = ff // width, tokens // ROWS
    thin = width // 32
    early = lambda i: jnp.minimum(i, blocks - 1)
    row = lambda w: pl.BlockSpec((ROWS, w), lambda i: (early(i), 0))
    if len(gxs) == 1:
        x_specs = [row(width)]
    else:
        x_specs = [pl.BlockSpec((ROWS, width), lambda i: (0, 0), pipeline_mode=pl.Buffered(1))] * 2
    weights = [params[n] for n in ("wdown", "wup", "wout")]
    ops = [*gxs, slope, resid, params["gains"], active, *weights, n2, mixed]
    specs = x_specs + [
        row(ff),
        row(width),
        layer(params["gains"], d, 1),
        pl.BlockSpec((tokens, width), lambda i: (0, jnp.clip(i - blocks, 0, parts - 1))),
    ]
    extra = list(into or ())
    specs += anywhere(ops[len(specs) :]) + anywhere(extra)
    shape = jax.ShapeDtypeStruct((32 // n_out, total, width), BF)
    vec = pl.BlockSpec((8, ff), lambda i: (0, 0))
    vm = pltpu.VMEM
    scratch = [vm((ff, width), BF), vm((width, ff), BF), vm((width, width), BF)]
    scratch += [vm((tokens, width), BF)] * 3 + [vm((tokens, ff), BF), vm((tokens, width), BF)]
    scratch += [vm((2, 32, thin, width), BF), vm((2, 8, 4 * thin, width), BF), vm((1, 32, thin, width), BF)]
    scratch += [pltpu.SemaphoreType.DMA((2 * parts + 3,)), pltpu.SemaphoreType.DMA((12,))]
    flops = 2 * tokens * width * (4 * ff + 2 * width)
    return pl.pallas_call(
        functools.partial(ff_all_kernel, len(gxs), n_out, 0, d),
        grid=(blocks + 2 * parts + 1,),
        in_specs=specs,
        out_specs=[row(width), row(width), vec] + [pl.BlockSpec(memory_space=pl.ANY)] * n_out,
        out_shape=[sds(tokens, width, F32), sds(tokens, width, BF), sds(8, ff, F32)] + [shape] * n_out,
        input_output_aliases={len(ops) + n: 3 + n for n in range(len(extra))},
        scratch_shapes=scratch,
        compiler_params=pltpu.CompilerParams(
            vmem_limit_bytes=63 << 20, dimension_semantics=("arbitrary",)
        ),
        cost_estimate=cost(flops, 50 << 20),
        name="ff_all",
    )(*ops, *extra)


def vector_piece(square, long, owner):
    tall = long.shape[0] // 32
    thin = square.shape[0] // 32
    piece = long[owner * tall : (owner + 1) * tall]
    top = piece[:thin] + square[owner * thin : (owner + 1) * thin]
    piece = jnp.concatenate([top, piece[thin:]], 0)
    return jnp.concatenate([piece[16 * m : 16 * m + 16] for m in range(tall // 16)], 1)


def turned_vectors(found):
    width = found[0][0].shape[1] // 4
    rows, ups = [], []
    for proj_vec, ff_vec in found:
        p = [proj_vec[0:1, n * width : (n + 1) * width] for n in range(4)]
        f = [ff_vec[0:1, n * width : (n + 1) * width] for n in range(4)]
        rows += [p[0], f[0], p[1], f[1], p[2], p[3], f[3], f[2]]
        ups.append(ff_vec[1:2])
    square = jnp.concatenate(rows + [jnp.zeros((128 - len(rows), width), F32)], 0)
    before, after = len(rows), 128 - len(rows) - len(ups)
    zeros = lambda n: jnp.zeros((n, 4 * width), F32)
    long = jnp.concatenate([zeros(before)] + ups + [zeros(after)], 0)
    return square.T, long.T


def qkv_all_kernel(d, n_x, row0, *refs):
    it = iter(refs)
    g_hbm, n1_hbm, w_hbm, gres_hbm, gain_ref = [next(it) for _ in range(5)]
    x_hbm = [next(it) for _ in range(n_x)]
    others = [next(it) for _ in range(3 if n_x == 2 else 0)]
    n_g = 1 if n_x == 1 else 2
    outs = [next(it) for _ in range(n_g)]
    vec_ref, keep, send = next(it), next(it), next(it)
    g_all, n1, wqkv, gres, x_all, held, arrive, leave = [next(it) for _ in range(8)]
    gx_held = list(it)
    _, tokens, width = g_all.shape
    half = tokens // 2
    rows = 3 * width // 32
    core = lax.axis_index("dp") & 1
    pairs = [(g_hbm.at[0], g_all.at[0]), (n1_hbm, n1), (g_hbm.at[1], g_all.at[1])]
    pairs += [(g_hbm.at[2], g_all.at[2]), (w_hbm.at[d], wqkv), (gres_hbm, gres)]
    if n_x == 1:
        pairs.append((x_hbm[0], x_all))
    else:
        pairs += [(x_hbm[n], x_all.at[pl.ds(n * half, half)]) for n in range(2)]
    loads = [pltpu.make_async_copy(a, b, arrive.at[n]) for n, (a, b) in enumerate(pairs)]
    for copy in loads:
        copy.start()
    loads[0].wait()
    loads[1].wait()
    for n in range(3):
        if n:
            loads[n + 1].wait()
        left = g_all[n]
        result = dot_tn(left, n1[...])
        if n != 1:
            at = 2 * width if n == 0 else 3 * width
            vec_ref[0:1, at : at + width] = colsum(left.astype(F32))
        owner = n * width // rows
        while owner * rows < (n + 1) * width:
            low, high = max(owner * rows, n * width), min((owner + 1) * rows, (n + 1) * width)
            to = low - owner * rows
            held[(owner >> 1) & 1, chunk_of(owner), to : to + high - low, :] = result[
                low - n * width : high - n * width
            ].astype(BF)
            owner += 1
    tall = held.shape[2]
    stores = [
        pltpu.make_async_copy(
            held.at[core if n == 0 else 1 - core], buf.at[:, pl.ds(row0, tall)], leave.at[n]
        )
        for n, buf in enumerate((keep, send))
    ]
    if not others:
        for copy in stores:
            copy.start()
    for copy in loads[4:]:
        copy.wait()
    sums = []
    for n in (1, 0):
        part = slice(n * half, (n + 1) * half)
        g = jnp.concatenate([g_all[m, part, :] for m in range(3)], 1)
        g_norm = dot_nt(g, wqkv[...])
        xhat, rstd = normalize(x_all[part, :].astype(F32))
        gx = gres[part, :] + norm_back(g_norm, xhat, rstd, gain_ref[...])
        scratch = gx_held[n if n_g == 2 else 0]
        if n_g == 2:
            scratch[...] = gx.astype(scratch.dtype)
            copy = pltpu.make_async_copy(scratch, outs[n], leave.at[2 + n])
        else:
            scratch[part, :] = gx
            span = pl.ds(n * half, half)
            copy = pltpu.make_async_copy(scratch.at[span], outs[0].at[span], leave.at[2 + n])
        copy.start()
        stores.append(copy)
        sums.append((colsum(g_norm * xhat), colsum(g_norm)))
    vec_ref[0:1, :width] = sums[0][0] + sums[1][0]
    vec_ref[0:1, width : 2 * width] = sums[0][1] + sums[1][1]
    if others:
        square, long = turned_vectors([(vec_ref, others[0]), (others[1], others[2])])
        for owner in range(32):
            piece = vector_piece(square, long, owner).astype(BF)
            held[(owner >> 1) & 1, chunk_of(owner), rows:, :] = piece
        for copy in stores[:2]:
            copy.start()
    for copy in stores:
        copy.wait()


def qkv_all(grads, n1, xs, g_resid, params, d, total, row0, vecs=()):
    _, tokens, width = grads.shape
    half = tokens // 2
    rows = 3 * width // 32
    ops = [grads, n1, params["wqkv"], g_resid, params["gains"], *xs, *vecs]
    hbm = pl.BlockSpec(memory_space=pl.ANY)
    vec = pl.BlockSpec((8, 4 * width), lambda i: (0, 0))
    specs = [hbm] * 4 + [layer(params["gains"], d, 0)] + [hbm] * len(xs) + [vec] * len(vecs)
    vm = pltpu.VMEM
    if len(xs) == 1:
        g_outs, g_held = [sds(tokens, width, F32)], [vm((tokens, width), F32)]
    else:
        g_outs = [sds(half, width, F32), sds(half, width, BF)]
        g_held = [vm((half, width), F32), vm((half, width), BF)]
    buf = jax.ShapeDtypeStruct((16, total, width), BF)
    return pl.pallas_call(
        functools.partial(qkv_all_kernel, d, len(xs), row0),
        grid=(1,),
        in_specs=specs,
        out_specs=[hbm] * len(g_outs) + [vec, hbm, hbm],
        out_shape=g_outs + [sds(8, 4 * width, F32), buf, buf],
        scratch_shapes=[
            vm((3, tokens, width), BF),
            vm((tokens, width), BF),
            vm((width, 3 * width), BF),
            vm((tokens, width), F32),
            vm((tokens, width), xs[0].dtype),
            vm((2, 16, rows + (16 if vecs else 0), width), BF),
            pltpu.SemaphoreType.DMA((8,)),
            pltpu.SemaphoreType.DMA((4,)),
        ]
        + g_held,
        compiler_params=VMEM,
        cost_estimate=cost(1, 1),
        name="qkv_all",
    )(*ops)


def plus(*parts):
    total = parts[0].astype(F32)
    for part in parts[1:]:
        total = total + part.astype(F32)
    return total


def place_xy():
    return (lax.axis_index("dp") >> 1) & 1, lax.axis_index("blk")


def stage1_kernel(tall, keep, recv, kp, sp, kq, sq):
    x, y = place_xy()
    both = lambda a, b, rows: plus(keep[0, a, b, rows], recv[0, a, b, rows]).astype(BF)
    up, low = slice(0, tall), slice(tall, keep.shape[3])
    for n in range(2):
        kp[0, n] = both(x, n, up)
        sp[0, n] = both(1 - x, n, up)
        kq[0, n] = both(n, y, low)
        sq[0, n] = both(n, 1 - y, low)


def stage2_kernel(kp, rp, kq, rq, kp2, sp2, kq2, sq2):
    x, y = place_xy()
    kp2[0] = plus(kp[0, y], rp[0, y]).astype(BF)
    sp2[0] = plus(kp[0, 1 - y], rp[0, 1 - y]).astype(BF)
    kq2[0] = plus(kq[0, x], rq[0, x]).astype(BF)
    sq2[0] = plus(kq[0, 1 - x], rq[0, 1 - x]).astype(BF)


def stage3_kernel(kp, rp, kq, rq, own, *sends):
    tall = kp.shape[1]
    z = lax.axis_index("dp") >> 2
    for n, ref in enumerate((own,) + sends):
        at = z ^ n
        ref[:tall, :] = plus(kp[at], rp[at]).astype(ref.dtype)
        ref[tall:, :] = plus(kq[at], rq[at]).astype(ref.dtype)


def stage_call(kernel, name, ops, outs, deps):
    nbytes = sum(math.prod(a.shape) * 2 for a in ops) + sum(math.prod(s) * 2 for s in outs)
    spec = lambda shape: pl.BlockSpec((1,) + shape[1:], lambda i: (i,) + (0,) * (len(shape) - 1))
    return pl.pallas_call(
        ordered(kernel, len(ops), deps),
        grid=(ops[0].shape[0],),
        in_specs=[spec(a.shape) for a in ops] + anywhere(deps),
        out_specs=[spec(s) for s in outs],
        out_shape=[jax.ShapeDtypeStruct(s, BF) for s in outs],
        compiler_params=SMALL,
        cost_estimate=cost(nbytes, nbytes),
        name=name,
    )(*ops, *deps)


def xor_permute(x, dp, mask):
    return lax.ppermute(x, "dp", [(i, i ^ mask) for i in range(dp)])


class Group:
    def __init__(self, keep, send, tall, dp):
        self.tall, self.dp = tall, dp
        self.keep, self.recv = keep, xor_permute(send, dp, 1)

    def stage1(self, deps=()):
        _, total, width = self.keep.shape
        tall = self.tall
        cut = lambda a: a.reshape(4, 2, 2, total, width)
        ops = [cut(self.keep), cut(self.recv)]
        p, q = (4, 2, tall, width), (4, 2, total - tall, width)
        kernel = functools.partial(stage1_kernel, tall)
        self.kp, sp, self.kq, sq = stage_call(kernel, "stage1", ops, [p, p, q, q], deps)
        self.rp, self.rq = xor_permute(sp, self.dp, 2), swap_halves(sq)
        return [self.kp]

    def stage2(self, deps=()):
        p, q = [(4,) + a.shape[2:] for a in (self.kp, self.kq)]
        ops = [self.kp, self.rp, self.kq, self.rq]
        self.kp, sp, self.kq, sq = stage_call(stage2_kernel, "stage2", ops, [p, p, q, q], deps)
        self.rp, self.rq = swap_halves(sp), xor_permute(sq, self.dp, 2)
        return [self.kp]

    def stage3(self, deps=()):
        ops = [self.kp, self.rp, self.kq, self.rq]
        total, width = self.kp.shape[1] + self.kq.shape[1], self.kp.shape[2]
        nbytes = total * width * 24
        pieces = pl.pallas_call(
            ordered(stage3_kernel, 4, deps),
            grid=(1,),
            in_specs=[pl.BlockSpec(a.shape, lambda i: (0, 0, 0)) for a in ops] + anywhere(deps),
            out_specs=[pl.BlockSpec((total, width), lambda i: (0, 0))] * 4,
            out_shape=[sds(total, width, F32)] + [sds(total, width, BF)] * 3,
            compiler_params=SMALL,
            cost_estimate=cost(nbytes, nbytes),
            name="stage3",
        )(*ops, *deps)
        moved = [xor_permute(pieces[n], self.dp, n << 2) for n in range(1, 4)]
        self.pieces = [pieces[0]] + moved
        return [pieces[0]]


def final_kernel(layout, counts, *refs):
    groups = []
    for count in counts:
        groups.append(refs[:count])
        refs = refs[count:]
    outs = dict(zip(layout["outs"], refs))
    width = groups[0][0].shape[1]

    def rows(group, start, count):
        return plus(*(ref[start : start + count, :] for ref in groups[group]))

    for d in range(LAYERS):
        place = layout["rows"][d]
        for name in ("qkv", "out", "up"):
            outs[name][d] = rows(*place[name])
        down = rows(*place["down"])
        thin = outs["down"].shape[1]
        for j in range(down.shape[0] // thin):
            outs["down"][d, :, j * width : (j + 1) * width] = down[j * thin : (j + 1) * thin]
    vec = rows(*layout["vec"])
    lanes = [vec[:, 128 * m : 128 * m + 128] for m in range(width // 128)]
    lanes.append(jnp.zeros((128 - 16 * len(lanes), 128), F32))
    turned = jnp.concatenate(lanes, 0).T
    short = len(VECTORS) - 1
    for d in range(LAYERS):
        for at, (name, n) in enumerate(VECTORS):
            ref = outs[name]
            row = d * short + at if at < short else LAYERS * short + d
            value = turned[row : row + 1, : ref.shape[-1]]
            if n is None:
                ref[d : d + 1, :] = value
            else:
                ref[d, n : n + 1, :] = value


VECTORS = (
    ("gains", 0),
    ("gains", 1),
    ("shifts", 0),
    ("shifts", 1),
    ("bq", None),
    ("bv", None),
    ("bout", None),
    ("bdown", None),
    ("bup", None),
)


def finish(layout, groups, shapes):
    ops = [a for g in groups for a in g]
    names = list(shapes)
    layout = dict(layout, outs=names)
    total = sum(math.prod(a.shape) for a in ops) * 2
    return dict(
        zip(
            names,
            pl.pallas_call(
                functools.partial(final_kernel, layout, [len(g) for g in groups]),
                out_shape=[jax.ShapeDtypeStruct(shapes[n], F32) for n in names],
                compiler_params=SMALL,
                cost_estimate=cost(total, total),
                name="finish",
            )(*ops),
        )
    )


def swap_halves(x):
    return lax.ppermute(x, "blk", [(0, 1), (1, 0)])


class Halving:
    def __init__(self, mesh):
        self.dp = mesh.shape["dp"]
        self.blk = mesh.shape["blk"]
        self.bits = self.dp.bit_length() - 1
        assert self.blk == 2 and 1 << self.bits == self.dp

    def stages(self, blk_first):
        dp_bits = list(range(self.bits))
        rest = ["blk", 1] if blk_first else [1, "blk"]
        return [0] + rest + dp_bits[2:]

    def split(self, rows):
        owners = self.dp * self.blk
        return rows.reshape((2,) * (self.bits + 1) + (rows.shape[0] // owners, rows.shape[1]))

    def run(self, rows, blk_first, wide=False):
        arr = self.split(rows)
        names = list(reversed(range(self.bits))) + ["blk"]
        order = self.stages(blk_first)
        for n, stage in enumerate(order):
            dim = names.index(stage)
            names.pop(dim)
            if stage == "blk":
                mine = lax.axis_index("blk")
                send = lambda x: lax.ppermute(x, "blk", [(0, 1), (1, 0)])
            else:
                mine = (lax.axis_index("dp") >> stage) & 1
                perm = [(i, i ^ (1 << stage)) for i in range(self.dp)]
                send = lambda x: lax.ppermute(x, "dp", perm)
            keep = lax.dynamic_index_in_dim(arr, mine, dim, keepdims=False)
            other = lax.dynamic_index_in_dim(arr, 1 - mine, dim, keepdims=False)
            arr = keep.astype(F32) + send(other).astype(F32)
            if not wide and n + 1 < len(order):
                arr = arr.astype(BF)
        return arr


class PlainSums:
    def __init__(self, mesh):
        self.halving = Halving(mesh)
        self.held = {}

    def add(self, name, d, lefts, right, blk_first):
        self.held[name, d] = self.halving.run(plain_grad(lefts, right), blk_first)

    def results(self, vec):
        vec = self.halving.run(vec, False, wide=True)[0]
        out = {
            n: jnp.stack([self.held[n, d].T for d in range(LAYERS)])
            for n in ("qkv", "out", "up", "down")
        }
        thin = vec.shape[0] // (12 * LAYERS)
        at = 0
        found = {}
        for d in range(LAYERS):
            for name, n in VECTORS:
                size = 4 * thin if name == "bup" else thin
                found.setdefault((name, d), []).append(vec[at : at + size])
                at += size
        for name in dict(VECTORS):
            rows = [jnp.stack(found[name, d]) for d in range(LAYERS)]
            out[name] = jnp.stack(rows if len(rows[0]) == 2 else [r[0] for r in rows])
        return out


def shards(
    mesh,
    hidden_in,
    cell_lengths,
    cotangent,
    ln_gains,
    ln_biases,
    w_qkv,
    b_query,
    b_value,
    w_out,
    b_out,
    w_up,
    b_up,
    w_down,
    b_down,
):
    cells, half, width = hidden_in.shape
    tokens = cells * half
    dp, blk = mesh.shape["dp"], mesh.shape["blk"]
    owners = dp * blk
    assert cells == blk == 2
    side = lax.axis_index("blk")
    meta = cell_lengths
    grouped = dp == 16 and width == 768 and b_up.shape[1] == 4 * width

    def split_cell(both):
        own = lax.dynamic_index_in_dim(both, side, 0, False)
        other = lax.dynamic_index_in_dim(both, 1 - side, 0, False)
        return own, swap_halves(other)

    def return_cell(own, back):
        return jnp.where(side == 0, jnp.stack([own, back]), jnp.stack([back, own]))

    rows = lambda v: v[..., None, :]
    params = {
        "gains": rows(ln_gains),
        "shifts": rows(ln_biases),
        "wqkv": w_qkv,
        "bias": rows(jnp.concatenate([b_query, jnp.zeros_like(b_query), b_value], 1)),
        "wout": w_out,
        "bout": rows(b_out),
        "wup": w_up,
        "bup": rows(b_up),
        "wdown": w_down,
        "bdown": rows(b_down),
    }
    own, other = split_cell(hidden_in)
    entered = enter(own, params, 0, None, tokens, 0)
    n1, proj = enter(other, params, 0, entered, tokens, half)
    xs = (own, other)
    saved = []
    for d in range(LAYERS):
        mixed, low, lse = attn_fwd(proj, meta)
        last = d + 1 == LAYERS
        outs = post(mixed, xs, params, d, last)
        saved.append((xs, n1, proj, mixed, low, lse) + tuple(outs[:4]))
        if not last:
            x, n1, proj = outs[4:]
            xs = (x,)
    returned = swap_halves(outs[5])
    hidden_out = return_cell(outs[4], returned)

    gxs = split_cell(cotangent)
    backward = backward_grouped if grouped else backward_plain
    gx, out = backward(mesh, params, saved, gxs, meta, [returned])
    grad_in = return_cell(gx[0], gx[1].astype(F32))
    order = ("gains", "shifts", "qkv", "bq", "bv", "out", "bout", "up", "bup", "down", "bdown")
    return (hidden_out, grad_in) + tuple(out[n] for n in order)


def vector_rows(owners, width, ln1, ln2, sums):
    flat = []
    for d in range(LAYERS):
        for v in (
            ln1[d][:width],
            ln2[d][:width],
            ln1[d][width:],
            ln2[d][width:],
            sums["qkv", d][:width],
            sums["qkv", d][-width:],
            sums["out", d],
            sums["down", d],
            sums["up", d],
        ):
            flat.append(v.reshape(owners, -1))
    return jnp.concatenate(flat, 1)


def backward_plain(mesh, params, saved, gxs, meta, early):
    sums = PlainSums(mesh)
    ln1, ln2, cols = {}, {}, {}
    for d in reversed(range(LAYERS)):
        xs, n1, proj, mixed, low, lse, resid, n2, active, slope = saved[d]
        tokens, width = resid.shape
        gy, gu, g_resid, ga, g_mixed, vec2 = ff_back(gxs, slope, resid, params, d)
        sums.add("down", d, [gy], active, False)
        sums.add("up", d, [gu], n2, True)
        sums.add("out", d, [ga], mixed, False)
        grads = attn_bwd(proj, mixed, low, g_mixed, lse, meta, (0, width // 128))
        sums.add("qkv", d, [grads[n] for n in range(3)], n1, True)
        total = lambda a: jnp.sum(a.astype(F32), 0)
        cols.update({("down", d): total(gy), ("up", d): total(gu), ("out", d): total(ga)})
        cols["qkv", d] = jnp.concatenate([total(grads[n]) for n in range(3)])
        ln2[d] = vec2[0]
        if d > 0:
            gx, vec1 = qkv_back(grads, xs[0], g_resid, params, d, 0, tokens, F32)
            gxs = (gx,)
            ln1[d] = vec1[0]
        else:
            half = tokens // 2
            theirs, vec_a = qkv_back(grads, xs[1], g_resid, params, d, half, half, BF)
            mine, vec_b = qkv_back(grads, xs[0], g_resid, params, d, 0, half, F32)
            ln1[d] = vec_a[0] + vec_b[0]
    owners = mesh.shape["dp"] * mesh.shape["blk"]
    out = sums.results(vector_rows(owners, width, ln1, ln2, cols))
    return (mine, swap_halves(theirs)), out


def backward_grouped(mesh, params, saved, gxs, meta, early):
    dp = mesh.shape["dp"]
    width = saved[0][6].shape[1]
    t, pairs = width // 32, width // 128

    def ff_grads(gxs, d, into, total, n_out):
        mixed, resid, n2, active, slope = saved[d][3], *saved[d][6:]
        g_resid, g_mixed, vec, *bufs = ff_all(
            gxs, slope, resid, active, n2, mixed, params, d, into, total, n_out
        )
        return g_resid, g_mixed, vec, bufs

    xs, n1, proj, mixed, low, lse = saved[1][:6]
    g_resid, g_mixed, ff_vec1, bufs = ff_grads(gxs, 1, None, 9 * t, 1)
    layer1 = lax.psum_scatter(bufs[0], ("dp", "blk"), scatter_dimension=0, tiled=True)[0]
    grads = attn_bwd(proj, mixed, low, g_mixed, lse, meta, (0, pairs), None, bufs + early)
    gx, proj_vec1, *bufs = qkv_all(grads, n1, xs, g_resid, params, 1, 12 * t, 9 * t)
    xs, n1, proj, mixed, low, lse = saved[0][:6]
    g_resid, g_mixed, ff_vec0, bufs = ff_grads((gx,), 0, bufs, 12 * t, 2)
    ff0 = Group(*bufs, 6 * t, dp)
    grads = attn_bwd(proj, mixed, low, g_mixed, lse, meta, (0, 2), None, [ff0.keep])
    dep = ff0.stage1(deps=[grads])
    grads = attn_bwd(proj, mixed, low, g_mixed, lse, meta, (2, pairs), grads, dep)
    vecs = (ff_vec0, proj_vec1, ff_vec1)
    mine, theirs, _, *bufs = qkv_all(grads, n1, xs, g_resid, params, 0, 3 * t + 16, 0, vecs)
    dep = ff0.stage2(deps=[theirs])
    at0 = Group(bufs[0], after(bufs[1], dep), 48, dp)
    dep = at0.stage1(deps=dep)
    dep = ff0.stage3(deps=dep)
    back = swap_halves(after(theirs, dep))
    at0.stage2(deps=dep + ff0.pieces[1:3] + [back])
    at0.stage3(deps=ff0.pieces[3:])
    layout = {
        "rows": [
            {"down": (1, 0, 4 * t), "up": (1, 4 * t, 4 * t), "out": (1, 8 * t, t), "qkv": (2, 0, 3 * t)},
            {"down": (0, 0, 4 * t), "up": (0, 4 * t, 4 * t), "out": (0, 8 * t, t), "qkv": (1, 9 * t, 3 * t)},
        ],
        "vec": (2, 3 * t, 16),
    }
    shapes = {
        "qkv": (LAYERS, 3 * t, width),
        "out": (LAYERS, t, width),
        "up": (LAYERS, 4 * t, width),
        "down": (LAYERS, t, 4 * width),
        "gains": (LAYERS, 2, t),
        "shifts": (LAYERS, 2, t),
        "bq": (LAYERS, t),
        "bv": (LAYERS, t),
        "bout": (LAYERS, t),
        "bdown": (LAYERS, t),
        "bup": (LAYERS, 4 * t),
    }
    out = finish(layout, [[layer1], ff0.pieces, at0.pieces], shapes)
    for name in ("qkv", "out", "up", "down"):
        out[name] = jnp.swapaxes(out[name], 1, 2)
    return (mine, back), out


def solution(mesh):
    both = ("dp", "blk")
    row = P("dp", "blk", None)
    last3 = P(None, None, both)
    last2 = P(None, both)
    return jax.shard_map(
        functools.partial(shards, mesh),
        mesh=mesh,
        in_specs=(row, P("dp"), row) + (P(),) * 11,
        out_specs=(
            row,
            row,
            last3,
            last3,
            last3,
            last2,
            last2,
            last3,
            last2,
            last3,
            last2,
            last3,
            last2,
        ),
        check_vma=False,
    )
```
